32 devices in a mesh: dp: 16 (over z, x, core), seq: 2 (over y).
Axes of the slice: x: 2, y: 2, z: 4, core: 2. Of those that a mesh axis runs over, the one named last changes fastest.
Arguments:
- tokens: bfloat16 [64, 512, 768], P('dp', 'seq'), may hold values from -6 to 6
- weight_in: bfloat16 [768, 3072], P(('dp', 'seq')), may hold values from -0.21875 to 0.21875
- bias_in: bfloat16 [3072], P(('dp', 'seq')), may hold values from -3 to 3
- weight_out: bfloat16 [3072, 768], P(('dp', 'seq')), may hold values from -0.15625 to 0.15625
- bias_out: bfloat16 [768], P(('dp', 'seq')), may hold values from -2 to 2
- gain_mix: bfloat16 [768], P(('dp', 'seq')), may hold values from 0.099609375 to 1.8984375
- shift_mix: bfloat16 [768], P(('dp', 'seq')), may hold values from -2 to 2
- gain_ffn: bfloat16 [768], P(('dp', 'seq')), may hold values from 0.099609375 to 1.8984375
- shift_ffn: bfloat16 [768], P(('dp', 'seq')), may hold values from -2 to 2
- cotangent: bfloat16 [64, 512, 768], P('dp', 'seq'), may hold values from -6 to 6
Outputs:
- output: bfloat16 [64, 512, 768], P('dp', 'seq')
- grad_tokens: float32 [64, 512, 768], P('dp', 'seq')
- grad_weight_in: float32 [768, 3072], P(('dp', 'seq'))
- grad_bias_in: float32 [3072], P(('dp', 'seq'))
- grad_weight_out: float32 [3072, 768], P(('dp', 'seq'))
- grad_bias_out: float32 [768], P(('dp', 'seq'))
- grad_gain_mix: float32 [768], P(('dp', 'seq'))
- grad_shift_mix: float32 [768], P(('dp', 'seq'))
- grad_gain_ffn: float32 [768], P(('dp', 'seq'))
- grad_shift_ffn: float32 [768], P(('dp', 'seq'))
The draws below stay inside these ranges and needn't reach their ends.
All inputs are finite; a program needn't handle non-finite values.
Results may differ from the reference program's by a relative error of at most 0.0074.
Values may be sent and summed in bfloat16 or wider, within the bound.
No kernel may reach another device: no remote copies, remote signals or barrier semaphores. Data moves between devices by JAX's collectives and lax.ppermute only.
A program may use at most 192 MiB of HBM per device.

```python
import math
import jax
import jax.numpy as jnp
from jax import lax

D = 768
FF = 3072
S = 512
ROWS = 64


def steps_of(key, dims, split, low, high):
    factor_of, own = 1.0, jax.random.fold_in(key, 6)
    for position, parts in split:
        steps = jnp.exp(jax.random.uniform(jax.random.fold_in(own, position), (parts,), jnp.float32, low / len(split), high / len(split)))
        factor_of = factor_of * jnp.repeat(steps, dims[position] // parts).reshape([-1 if axis == position else 1 for axis in range(len(dims))])
    return factor_of


def bell_draw(stream_key, extent, scale, most, shards=(), held_as=jnp.bfloat16):
    values = scale * jax.random.normal(stream_key, extent, jnp.float32)
    if shards:
        values = values * steps_of(stream_key, extent, shards, -0.22, 0.18)
    return jnp.clip(values, -most, most).astype(held_as)


def setup_inputs(seed: int = 0) -> dict:
    key_list = jax.random.split(jax.random.key(seed), 11)
    tokens = bell_draw(key_list[0], (ROWS, S, D), 1.0, 6.0, ((0, 16), (1, 2)))
    weight_in = bell_draw(key_list[1], (D, FF), D ** -0.5, 0.21875, ((0, 32),))
    bias_in = bell_draw(key_list[2], (FF,), 0.5, 3.0, ((0, 32),))
    weight_out = bell_draw(key_list[3], (FF, D), (FF // 2) ** -0.5, 0.15625, ((0, 32),))
    bias_out = bell_draw(key_list[4], (D,), 0.3, 2.0, ((0, 32),))
    gain_mix = jnp.clip(1.0 + 0.18 * jax.random.normal(key_list[5], (D,), jnp.float32), 0.099609375, 1.8984375).astype(jnp.bfloat16)
    shift_mix = bell_draw(key_list[6], (D,), 0.3, 2.0, ((0, 32),))
    gain_ffn = jnp.clip(1.0 + 0.18 * jax.random.normal(key_list[7], (D,), jnp.float32), 0.099609375, 1.8984375).astype(jnp.bfloat16)
    shift_ffn = bell_draw(key_list[8], (D,), 0.3, 2.0, ((0, 32),))
    cotangent = bell_draw(key_list[9], (ROWS, S, D), 1.0, 6.0, ((0, 16), (1, 2)))
    return dict(tokens=tokens, weight_in=weight_in, bias_in=bias_in, weight_out=weight_out, bias_out=bias_out, gain_mix=gain_mix, shift_mix=shift_mix, gain_ffn=gain_ffn, shift_ffn=shift_ffn, cotangent=cotangent)


EPS = 1e-12

@jax.custom_vjp
def low(v):
    return lax.optimization_barrier(v.astype(jnp.bfloat16)).astype(jnp.float32)

@jax.custom_vjp
def low_back(v):
    return v

def low_keep(v):
    return (low(v), None)

def low_pass(kept, grad):
    return (grad,)

def back_keep(v):
    return (v, None)

def back_low(kept, grad):
    return (low(grad),)
low.defvjp(low_keep, low_pass)
low_back.defvjp(back_keep, back_low)

def dft_tables(length):
    index = jnp.arange(length, dtype=jnp.int32)
    product = index[:, None] * index[None, :] % length
    angle = product.astype(jnp.float32) * (2.0 * math.pi / length)
    scale = length ** (-0.5)
    return (jnp.cos(angle) * scale, jnp.sin(angle) * scale)

def layer_norm(values, gain, shift):
    center = values - lax.optimization_barrier(jnp.mean(values, axis=-1, keepdims=True))
    spread = lax.optimization_barrier(jnp.mean(center * center, axis=-1, keepdims=True))
    return center * lax.rsqrt(spread + EPS) * gain + shift

def forward(tokens, weight_in, bias_in, weight_out, bias_out, gain_mix, shift_mix, gain_ffn, shift_ffn, seq_table, hid_table):
    highest = lax.Precision.HIGHEST
    stacked = jnp.einsum('kn,rnd->rkd', seq_table, tokens, precision=highest)
    spectra = low(low_back(jnp.concatenate([stacked[:, :S], stacked[:, S:]], axis=-1)))
    mixed = low_back(jnp.einsum('rkj,jd->rkd', spectra, hid_table, precision=highest))
    normed = layer_norm(tokens + mixed, gain_mix, shift_mix)
    hidden_pre = low_back(jnp.einsum('rkd,df->rkf', low(normed), weight_in, precision=highest) + bias_in)
    activated = low(jax.nn.gelu(hidden_pre, approximate=False))
    branch = low_back(jnp.einsum('rkf,fd->rkd', activated, weight_out, precision=highest) + bias_out)
    return layer_norm(normed + branch, gain_ffn, shift_ffn)

def reference(tokens, weight_in, bias_in, weight_out, bias_out, gain_mix, shift_mix, gain_ffn, shift_ffn, cotangent):
    params = tuple((p.astype(jnp.float32) for p in (weight_in, bias_in, weight_out, bias_out, gain_mix, shift_mix, gain_ffn, shift_ffn)))
    cos_seq, sin_seq = dft_tables(S)
    seq_table = low(jnp.concatenate([cos_seq, sin_seq], axis=0))
    cos_hid, sin_hid = dft_tables(D)
    hid_table = low(jnp.concatenate([cos_hid, -sin_hid], axis=0))
    group = 8 if ROWS % 8 == 0 else 1
    token_groups = tokens.astype(jnp.float32).reshape(ROWS // group, group, S, D)
    cot_groups = cotangent.astype(jnp.float32).reshape(ROWS // group, group, S, D)

    def one_group(totals, pair):
        block, cot_block = pair

        def apply_layer(block_in, *weights):
            return forward(block_in, *weights, seq_table, hid_table)
        result, pullback = jax.vjp(apply_layer, block, *params)
        grads = pullback(cot_block)
        totals = tuple((total + grad for total, grad in zip(totals, grads[1:])))
        return (totals, (result.astype(jnp.bfloat16), grads[0]))
    start_totals = tuple((jnp.zeros_like(p) for p in params))
    totals, (results, grad_input) = lax.scan(one_group, start_totals, (token_groups, cot_groups))
    output = results.reshape(ROWS, S, D)
    grad_tokens = grad_input.reshape(ROWS, S, D)
    return (output, grad_tokens, totals[0], totals[1], totals[2], totals[3], totals[4], totals[5], totals[6], totals[7])
```

```python
import math

import jax
import jax.numpy as jnp
import numpy as np
from jax import lax
from jax.sharding import PartitionSpec as P

EPS = 1e-12
AXES = ("dp", "seq")
BF16 = jnp.bfloat16
F32 = jnp.float32


def dft_tables(length):
    index = np.arange(length, dtype=np.int64)
    angle = (index[:, None] * index[None, :] % length).astype(np.float64) * (2.0 * math.pi / length)
    scale = length ** (-0.5)
    return np.cos(angle) * scale, np.sin(angle) * scale


class Grid:
    def __init__(self, mesh):
        self.dp = mesh.shape["dp"]
        self.seq = mesh.shape["seq"]
        chips = self.dp // 2
        radices, bits = [], 1
        while chips > 1:
            radix = min(2**bits, chips)
            radices.append(radix)
            chips //= radix
            bits += 1
        self.low = radices[0]
        self.high = math.prod(radices[1:])

    def ids(self):
        for z in range(self.high):
            for x in range(self.low):
                for c in range(2):
                    for y in range(self.seq):
                        yield z, x, c, y

    def index(self, z, x, c, y):
        return ((z * self.low + x) * 2 + c) * self.seq + y

    def perm(self, move):
        return [(self.index(*at), self.index(*move(*at))) for at in self.ids()]

    def place(self):
        dp = lax.axis_index("dp")
        return dp // (2 * self.low), dp // 2 % self.low, dp % 2, lax.axis_index("seq")


def send(value, perm):
    return lax.ppermute(value, AXES, perm)


def pick(value, index, axis):
    return lax.dynamic_index_in_dim(value, index, axis, keepdims=False)


def gather(grid, shard):
    z, x, c, y = grid.place()
    ring = grid.perm(lambda z, x, c, y: ((z + 1) % grid.high, x, c, y))
    first = grid.perm(lambda z, x, c, y: (z, 1 - x, c, y) if c == 0 else (z, x, c, 1 - y))
    second = grid.perm(lambda z, x, c, y: (z, x, c, 1 - y) if c == 0 else (z, 1 - x, c, y))
    cores = grid.perm(lambda z, x, c, y: (z, x, 1 - c, y))
    zero = jnp.int32(0)
    column = jnp.zeros((grid.high,) + shard.shape, shard.dtype)
    piece = shard
    column = lax.dynamic_update_slice_in_dim(column, piece[None], z, 0)
    for step in range(1, grid.high):
        piece = send(piece, ring)
        column = lax.dynamic_update_slice_in_dim(column, piece[None], (z - step) % grid.high, 0)
    other = send(column, first)
    pair = jnp.stack([column, other])
    far = send(pair, second)
    plane = jnp.zeros((grid.high, grid.low, grid.seq) + shard.shape, shard.dtype)

    def put(plane, part, px, py):
        start = (zero, px, py) + (zero,) * shard.ndim
        return lax.dynamic_update_slice(plane, part[:, None, None], start)

    plane = put(plane, column, x, y)
    plane = put(plane, other, jnp.where(c == 0, 1 - x, x), jnp.where(c == 0, y, 1 - y))
    plane = put(plane, far[0], jnp.where(c == 0, x, 1 - x), jnp.where(c == 0, 1 - y, y))
    plane = put(plane, far[1], 1 - x, 1 - y)
    twin = send(plane, cores)
    return jnp.where(
        c == 0, jnp.stack([plane, twin], axis=2), jnp.stack([twin, plane], axis=2)
    )


def scatter(grid, total):
    z, x, c, y = grid.place()
    ring = grid.perm(lambda z, x, c, y: ((z + 1) % grid.high, x, c, y))
    first = grid.perm(lambda z, x, c, y: (z, 1 - x, c, y) if c == 0 else (z, x, c, 1 - y))
    second = grid.perm(lambda z, x, c, y: (z, x, c, 1 - y) if c == 0 else (z, 1 - x, c, y))
    cores = grid.perm(lambda z, x, c, y: (z, x, 1 - c, y))
    low = lambda value: value.astype(BF16)
    plane = pick(total, c, 2) + send(low(pick(total, 1 - c, 2)), cores).astype(F32)
    away = jnp.where(c == 0, pick(plane, 1 - y, 2), pick(plane, 1 - x, 1))
    mine = jnp.where(c == 0, pick(plane, y, 2), pick(plane, x, 1))
    pair = mine + send(low(away), second).astype(F32)
    bit = jnp.where(c == 0, x, y)
    column = pick(pair, bit, 1) + send(low(pick(pair, 1 - bit, 1)), first).astype(F32)
    part = pick(column, (z - 1) % grid.high, 0)
    for step in range(1, grid.high):
        part = pick(column, (z - 1 - step) % grid.high, 0) + send(low(part), ring).astype(F32)
    return part


def layer_norm(values, gain, shift):
    center = values - jnp.mean(values, axis=-1, keepdims=True)
    spread = jnp.mean(center * center, axis=-1, keepdims=True)
    return center * lax.rsqrt(spread + EPS) * gain + shift


def gelu_exact(values):
    return jax.nn.gelu(values, approximate=False)


def per_device(grid, tokens, weight_in, bias_in, weight_out, bias_out, gain_mix, shift_mix, gain_ffn, shift_ffn, cotangent):
    rows, block, width = tokens.shape
    hidden = weight_in.shape[1]
    length = block * grid.seq
    half = rows // 2
    y = lax.axis_index("seq")
    swap = grid.perm(lambda z, x, c, y: (z, x, c, 1 - y))

    def to_rows(value):
        mine = lax.dynamic_slice_in_dim(value, y * half, half, 0)
        other = send(lax.dynamic_slice_in_dim(value, (1 - y) * half, half, 0), swap)
        return jnp.where(
            y == 0, jnp.concatenate([mine, other], 1), jnp.concatenate([other, mine], 1)
        )

    def to_blocks(value):
        mine = lax.dynamic_slice_in_dim(value, y * block, block, 1)
        other = send(lax.dynamic_slice_in_dim(value, (1 - y) * block, block, 1).astype(BF16), swap)
        other = other.astype(value.dtype)
        return jnp.where(
            y == 0, jnp.concatenate([mine, other], 0), jnp.concatenate([other, mine], 0)
        )

    smalls = (bias_in, bias_out, gain_mix, shift_mix, gain_ffn, shift_ffn)
    edges = np.cumsum([0] + [v.shape[0] for v in smalls])
    piece = to_rows(tokens)
    small_pack = jnp.pad(jnp.concatenate(smalls), (0, hidden - int(edges[-1])))
    packed = jnp.concatenate([weight_in, jnp.broadcast_to(small_pack, (8, hidden))], axis=0)
    part_in = weight_in.shape[0]
    packed_all = gather(grid, packed)
    full_w_in = packed_all[..., :part_in, :].reshape(-1, hidden)
    small_all = packed_all[..., part_in, :]
    vectors = [
        small_all[..., int(edges[i]) : int(edges[i + 1])].reshape(-1).astype(F32)
        for i in range(6)
    ]
    full_b_in, full_b_out, mix_gain, mix_shift, ffn_gain, ffn_shift = vectors
    full_w_out = gather(grid, weight_out).reshape(hidden, width)
    cot = to_rows(cotangent)

    cos_seq, sin_seq = dft_tables(length)
    seq_table = jnp.asarray(np.concatenate([cos_seq, sin_seq], 0).astype(np.float32)).astype(BF16)
    cos_hid, sin_hid = dft_tables(width)
    hid_table = jnp.asarray(np.concatenate([cos_hid, -sin_hid], 0).astype(np.float32)).astype(BF16)

    stacked = jnp.einsum("kn,rnd->rkd", seq_table, piece, preferred_element_type=F32)
    spectra = jnp.concatenate([stacked[:, :length], stacked[:, length:]], axis=-1).astype(BF16)
    mixed = jnp.einsum("rkj,jd->rkd", spectra, hid_table, preferred_element_type=F32)
    resid_one = piece.astype(F32) + mixed
    normed, norm_pull = jax.vjp(layer_norm, resid_one, mix_gain, mix_shift)
    normed_low = normed.astype(BF16)
    hidden_pre = (
        jnp.einsum("rkd,df->rkf", normed_low, full_w_in, preferred_element_type=F32) + full_b_in
    )
    activated, gelu_pull = jax.vjp(gelu_exact, hidden_pre)
    act_low = activated.astype(BF16)
    branch = (
        jnp.einsum("rkf,fd->rkd", act_low, full_w_out, preferred_element_type=F32) + full_b_out
    )
    result, final_pull = jax.vjp(layer_norm, normed + branch, ffn_gain, ffn_shift)
    output = to_blocks(result.astype(BF16))
    d_resid_two, d_gain_ffn, d_shift_ffn = final_pull(cot.astype(F32))
    d_branch = d_resid_two.astype(BF16)
    grad_w_out = jnp.einsum("rkf,rkd->fd", act_low, d_branch, preferred_element_type=F32)
    grad_b_out = jnp.sum(d_branch.astype(F32), axis=(0, 1))
    lead = (grid.high, grid.low, 2, grid.seq)
    my_w_out = scatter(grid, grad_w_out.reshape(lead + weight_out.shape))
    d_act = jnp.einsum("rkd,fd->rkf", d_branch, full_w_out, preferred_element_type=F32)
    (d_pre,) = gelu_pull(d_act)
    d_pre_low = d_pre.astype(BF16)
    d_normed = d_resid_two + jnp.einsum(
        "rkf,df->rkd", d_pre_low, full_w_in, preferred_element_type=F32
    )
    d_resid_one, d_gain_mix, d_shift_mix = norm_pull(d_normed)
    d_mix_low = d_resid_one.astype(BF16)
    d_spectra = jnp.einsum("rkd,jd->rkj", d_mix_low, hid_table, preferred_element_type=F32).astype(
        BF16
    )
    d_stacked = jnp.concatenate([d_spectra[..., :width], d_spectra[..., width:]], axis=1)
    d_tokens_mix = jnp.einsum("kn,rkd->rnd", seq_table, d_stacked, preferred_element_type=F32)
    grad_tokens = to_blocks(d_resid_one + d_tokens_mix)
    grad_w_in = jnp.einsum("rkd,rkf->df", normed_low, d_pre_low, preferred_element_type=F32)
    grad_b_in = jnp.sum(d_pre_low.astype(F32), axis=(0, 1))
    small_grads = (grad_b_in, grad_b_out, d_gain_mix, d_shift_mix, d_gain_ffn, d_shift_ffn)
    devices = grid.dp * grid.seq
    strip = jnp.concatenate([g.reshape(devices, -1) for g in small_grads], axis=1)
    strip = jnp.pad(strip, ((0, 0), (0, hidden - strip.shape[1])))[:, None, :]
    strip = jnp.pad(strip, ((0, 0), (0, 7), (0, 0)))
    joined = jnp.concatenate([grad_w_in.reshape(devices, part_in, hidden), strip], axis=1)
    my_joined = scatter(grid, joined.reshape(lead + joined.shape[1:]))
    my_small = [my_joined[part_in, int(edges[i]) : int(edges[i + 1])] for i in range(6)]
    return (
        output,
        grad_tokens,
        my_joined[:part_in],
        my_small[0],
        my_w_out,
        my_small[1],
        my_small[2],
        my_small[3],
        my_small[4],
        my_small[5],
    )


def solution(mesh):
    grid = Grid(mesh)
    cut, cut2 = P(AXES), P(AXES, None)
    block = P("dp", "seq", None)
    in_specs = (block, cut2, cut, cut2, cut, cut, cut, cut, cut, block)
    out_specs = (block, block, cut2, cut, cut2, cut, cut, cut, cut, cut)

    def program(*arrays):
        return per_device(grid, *arrays)

    return jax.shard_map(
        program, mesh=mesh, in_specs=in_specs, out_specs=out_specs, check_vma=False
    )
```

```python
import functools
import math

import jax
import jax.numpy as jnp
import numpy as np
from jax import lax
from jax.experimental import pallas as pl
from jax.experimental.pallas import tpu as pltpu
from jax.sharding import PartitionSpec as P

EPS = 1e-12
AXES = ("dp", "seq")
BF16 = jnp.bfloat16
F32 = jnp.float32
MIB = 1 << 20
LANES = 128
ERF_T = 0.3275911
ERF_P = (0.254829592, -0.284496736, 1.421413741, -1.453152027, 1.061405429)


def dft_tables(length):
    index = np.arange(length, dtype=np.int64)
    angle = (index[:, None] * index[None, :] % length).astype(np.float64) * (2.0 * math.pi / length)
    scale = length ** (-0.5)
    return np.cos(angle) * scale, np.sin(angle) * scale


def table(values):
    return jnp.asarray(values.astype(np.float32)).astype(BF16)


class Grid:
    def __init__(self, mesh):
        self.dp = mesh.shape["dp"]
        self.seq = mesh.shape["seq"]
        chips = self.dp // 2
        self.low = min(2, chips)
        self.high = chips // self.low
        self.ring = self.perm(lambda z, x, c, y: ((z + 1) % self.high, x, c, y))
        self.across = self.perm(lambda z, x, c, y: (z, (x + 1) % self.low, c, y))
        self.cores = self.perm(lambda z, x, c, y: (z, x, 1 - c, y))
        self.blocks = self.perm(lambda z, x, c, y: (z, x, c, (y + 1) % self.seq))
        self.across_0 = self.perm(
            lambda z, x, c, y: (z, (x + 1 - c) % self.low, c, (y + c) % self.seq)
        )
        self.across_1 = self.perm(
            lambda z, x, c, y: (z, (x + c) % self.low, c, (y + 1 - c) % self.seq)
        )
        self.chained = self.high == 4 and self.low == 2 and self.seq == 2

    def index(self, z, x, c, y):
        return ((z * self.low + x) * 2 + c) * self.seq + y

    def perm(self, move):
        return [
            (self.index(z, x, c, y), self.index(*move(z, x, c, y)))
            for z in range(self.high)
            for x in range(self.low)
            for c in range(2)
            for y in range(self.seq)
        ]

    def place(self):
        dp = lax.axis_index("dp")
        return dp // (2 * self.low), dp // 2 % self.low, dp % 2, lax.axis_index("seq")


def send(value, perm):
    return lax.ppermute(value, AXES, perm)


def pick(value, index):
    zero = jnp.uint32(0)
    starts = (index,) + (zero,) * (value.ndim - 1)
    return lax.dynamic_slice(value, starts, (1,) + value.shape[1:])[0]


def dot(a, b):
    return jnp.dot(a, b, preferred_element_type=F32)


def dot_nt(a, b):
    return lax.dot_general(a, b, (((1,), (1,)), ((), ())), preferred_element_type=F32)


def dot_tn(a, b):
    return lax.dot_general(a, b, (((0,), (0,)), ((), ())), preferred_element_type=F32)


def params(mib):
    return pltpu.CompilerParams(vmem_limit_bytes=mib * MIB)


def cost(flops, bytes_accessed, transcendentals=0):
    return pl.CostEstimate(
        flops=int(flops), bytes_accessed=int(bytes_accessed), transcendentals=int(transcendentals)
    )


def row_sum(values):
    return jnp.sum(values, axis=0, keepdims=True)


def after(value, *others):
    return lax.optimization_barrier((value,) + others)[0]


def together(*values):
    return lax.optimization_barrier(values)


def device_number(place, distance, group, other_core):
    z, x, c, y = place
    zz = lax.rem(z - distance + 4, 4)
    cc = 1 - c if other_core else c
    flip_x, flip_y = ((0, 0), (1 - cc, cc), (cc, 1 - cc), (1, 1))[group]
    xx = x + flip_x - 2 * x * flip_x
    yy = y + flip_y - 2 * y * flip_y
    return ((zz * 2 + xx) * 2 + cc) * 2 + yy


def column_slab(part, index):
    return index % 4, part + index // 4


def pair_slab(part, index):
    return part // 2, part % 2 * 2 + index


def copy_slabs(place, refs, slab_of, start_copy):
    for part, ref in enumerate(refs):
        own = len(refs) // 2
        for i in range(ref.shape[0]):
            distance, group = slab_of(part % own, i)
            start_copy(ref.at[i], device_number(place, distance, group, part >= own))


def vmem_call(kernel, name, out_shape, mib, work, scratch_shapes=(), places=0, anywhere=0):
    def call(*operands):
        here = len(operands) - places - anywhere
        return pl.pallas_call(
            kernel,
            name=name,
            in_specs=[pl.BlockSpec(memory_space=pltpu.SMEM)] * places
            + [pl.BlockSpec(memory_space=pltpu.VMEM)] * here
            + [pl.BlockSpec(memory_space=pl.ANY)] * anywhere,
            out_specs=[pl.BlockSpec(memory_space=pltpu.VMEM)] * len(out_shape),
            out_shape=[jax.ShapeDtypeStruct(*each) for each in out_shape],
            scratch_shapes=list(scratch_shapes),
            compiler_params=params(mib),
            cost_estimate=work,
        )(*operands)

    return call


def tile_rows(index, size):
    return pl.ds(pl.multiple_of(index * size, size), size)


def assemble(place, groups, split):
    _, rows, columns = groups[0].shape
    slabs = sum(group.shape[0] for group in groups)
    return vmem_call(
        functools.partial(assemble_kernel, count=len(groups), split=split),
        "assemble_w_in",
        [((slabs * rows, split), BF16), ((slabs, rows, LANES), BF16)],
        2,
        cost(0, 4 * slabs * rows * columns),
        [pltpu.SemaphoreType.DMA((2 * slabs,))],
        places=1,
        anywhere=len(groups),
    )(place, *groups)


def spread_matrix(size, start, total):
    lane = lax.broadcasted_iota(jnp.int32, (LANES, total), 0)
    column = lax.broadcasted_iota(jnp.int32, (LANES, total), 1)
    return lane == start + lax.rem(column, size)


def owner_mask(owners, total):
    owner = lax.broadcasted_iota(jnp.int32, (owners, total), 0)
    column = lax.broadcasted_iota(jnp.int32, (owners, total), 1)
    return lax.div(column, total // owners) == owner


def first_weight_kernel(place_ref, xhat_ref, *refs, count, split):
    groups = refs[:count]
    full_ref, bias_ref, vec_ref, low_ref, low_t_ref, extra_ref, sem = refs[count:]
    rows = groups[0].shape[1]
    place = tuple(place_ref[i] for i in range(4))
    sides, mains = [], []

    def add(slab, at):
        side = slab.at[:, pl.ds(split, LANES)]
        sides.append(pltpu.make_async_copy(side, extra_ref.at[at], sem.at[2 * len(sides)]))
        target = full_ref.at[tile_rows(at, rows), :]
        main = slab.at[:, pl.ds(0, split)]
        mains.append(pltpu.make_async_copy(main, target, sem.at[2 * len(mains) + 1]))

    copy_slabs(place, groups, column_slab, add)
    for copy in sides + mains:
        copy.start()
    for copy in sides:
        copy.wait()
    owners, width = extra_ref.shape[0], vec_ref.shape[1]
    line = extra_ref[:, 0, :]
    wide = dot(line, spread_matrix(split // owners, 0, split).astype(BF16))
    bias_ref[...] = row_sum(jnp.where(owner_mask(owners, split), wide, 0.0))
    line = extra_ref[:, 1, :]
    mask = owner_mask(owners, width)
    size = width // owners
    vec_ref[...] = jnp.zeros_like(vec_ref)
    for i in range(5):
        wide = dot(line, spread_matrix(size, i * size, width).astype(BF16))
        vec_ref[i : i + 1, :] = row_sum(jnp.where(mask, wide, 0.0))
    low = (xhat_ref[...] * vec_ref[1:2, :] + vec_ref[2:3, :]).astype(BF16)
    low_ref[...] = low
    low_t_ref[...] = low.T
    for copy in mains:
        copy.wait()


def first_weight(place, xhat, groups, split):
    _, rows, columns = groups[0].shape
    slabs = sum(group.shape[0] for group in groups)
    count, width = xhat.shape
    return vmem_call(
        functools.partial(first_weight_kernel, count=len(groups), split=split),
        "first_weight",
        [
            ((slabs * rows, split), BF16),
            ((1, split), F32),
            ((8, width), F32),
            ((count, width), BF16),
            ((width, count), BF16),
        ],
        10,
        cost(2 * count * width, 4 * slabs * rows * columns),
        [pltpu.VMEM((slabs, rows, LANES), BF16), pltpu.SemaphoreType.DMA((2 * slabs,))],
        places=1,
        anywhere=len(groups),
    )(place, xhat, *groups)


def mix_kernel(place_ref, mine_ref, other_ref, seq_ref, hid_ref, xhat_ref, rstd_ref, row_ref):
    half, block, width = other_ref.shape
    length = 2 * block
    y = place_ref[3]

    def step(r, carry):
        row_ref[tile_rows(y, block), :] = mine_ref[half * y + r]
        row_ref[tile_rows(1 - y, block), :] = other_ref[r]
        tokens = row_ref[...]
        for part in range(2):
            at = part * block
            cos_part = dot(seq_ref[at : at + block, :], tokens).astype(BF16)
            sin_part = dot(seq_ref[length + at : length + at + block, :], tokens).astype(BF16)
            mixed = dot(cos_part, hid_ref[:width, :]) + dot(sin_part, hid_ref[width:, :])
            resid = tokens[at : at + block, :].astype(F32) + mixed
            center = resid - jnp.mean(resid, axis=-1, keepdims=True)
            rstd = lax.rsqrt(jnp.mean(center * center, axis=-1, keepdims=True) + EPS)
            rows = tile_rows(2 * r + part, block)
            xhat_ref[rows, :] = center * rstd
            rstd_ref[rows, :] = rstd
        return carry

    lax.fori_loop(0, half, step, 0)


def mix(place, tokens, other, seq_table, hid_table):
    half, block, width = other.shape
    length = 2 * block
    count = half * length
    return vmem_call(
        mix_kernel,
        "mix_norm",
        [((count, width), F32), ((count, 1), F32)],
        14,
        cost(4 * count * width * (length + width), 10 * count * width),
        [pltpu.VMEM((length, width), BF16)],
        places=1,
    )(place, tokens, other, seq_table, hid_table)


def gelu_both(values):
    size = jnp.abs(values)
    t = 1.0 / (1.0 + (ERF_T / math.sqrt(2.0)) * size)
    bell = jnp.exp(-0.5 * (values * values))
    poly = 0.5 * ERF_P[4]
    for term in ERF_P[3::-1]:
        poly = 0.5 * term + t * poly
    tail = t * poly * bell
    phi = jnp.where(values > 0, 1.0 - tail, tail)
    return values * phi, phi + values * (bell * (1.0 / math.sqrt(2.0 * math.pi)))


def ffn_low_kernel(xhat_ref, vec_ref, low_ref, low_t_ref):
    low = (xhat_ref[...] * vec_ref[1:2, :] + vec_ref[2:3, :]).astype(BF16)
    low_ref[...] = low
    low_t_ref[...] = low.T


def ffn_low(xhat, vectors):
    count, width = xhat.shape
    return vmem_call(
        ffn_low_kernel,
        "normed_low",
        [((count, width), BF16), ((width, count), BF16)],
        8,
        cost(2 * count * width, 8 * count * width),
    )(xhat, vectors)


def ffn_in_kernel(low_ref, w_ref, bias_ref, act_ref, slope_ref, *, at, tile, columns):
    hidden = act_ref.shape[1]
    for part in range(0, hidden, columns):
        cut, full = slice(part, part + columns), slice(at + part, at + part + columns)

        def step(i, carry):
            rows = tile_rows(i, tile)
            hidden_pre = dot(low_ref[rows, :], w_ref[:, full]) + bias_ref[:, full]
            act, slope = gelu_both(hidden_pre)
            act_ref[rows, cut] = act.astype(BF16)
            slope_ref[rows, cut] = slope.astype(BF16)
            return carry

        lax.fori_loop(0, low_ref.shape[0] // tile, step, 0)


def ffn_in(low, w_in, bias, part, parts, columns=768, tile=512):
    count, width = low.shape
    hidden = w_in.shape[1] // parts
    return vmem_call(
        functools.partial(ffn_in_kernel, at=part * hidden, tile=tile, columns=columns),
        "ffn_in_gelu",
        [((count, hidden), BF16)] * 2,
        14,
        cost(2 * count * width * hidden, 4 * count * hidden, 2 * count * hidden),
    )(low, w_in, bias)


def ffn_out_kernel(place_ref, act_0_ref, act_1_ref, xhat_ref, mine_ref, other_ref, vec_ref, *refs, count):
    groups = refs[:count]
    send_ref, keep_ref, resid_ref, low_ref, sums_ref, w_ref, sem = refs[count:]
    half, block, _ = other_ref.shape
    y = place_ref[3]
    place = tuple(place_ref[i] for i in range(4))
    copies = []
    if count == 1:
        copies.append(pltpu.make_async_copy(groups[0], w_ref, sem.at[0]))
    else:
        rows = groups[0].shape[1]

        def add(slab, at):
            target = w_ref.at[tile_rows(at, rows), :]
            copies.append(pltpu.make_async_copy(slab, target, sem.at[len(copies)]))

        copy_slabs(place, groups, pair_slab, add)
    for copy in copies:
        copy.start()
    sums_ref[...] = jnp.zeros_like(sums_ref)
    bias, gain_mix, shift_mix = vec_ref[0:1, :], vec_ref[1:2, :], vec_ref[2:3, :]
    gain, shift = vec_ref[3:4, :], vec_ref[4:5, :]
    cut = act_0_ref.shape[1]
    for copy in copies:
        copy.wait()

    def side(away):
        def step(r, carry):
            spot = 1 - y if away else y
            rows = tile_rows(2 * r + spot, block)
            branch = dot(act_0_ref[rows, :], w_ref[:cut, :]) + dot(act_1_ref[rows, :], w_ref[cut:, :])
            value = xhat_ref[rows, :] * gain_mix + shift_mix + (branch + bias)
            center = value - jnp.mean(value, axis=-1, keepdims=True)
            rstd = lax.rsqrt(jnp.mean(center * center, axis=-1, keepdims=True) + EPS)
            xhat = center * rstd
            result = (xhat * gain + shift).astype(BF16)
            if away:
                send_ref[r] = result
                cot = other_ref[r].astype(F32)
            else:
                keep_ref[r] = result
                cot = mine_ref[half * y + r].astype(F32)
            d_xhat = cot * gain
            d_resid = rstd * (
                d_xhat
                - jnp.mean(d_xhat, axis=-1, keepdims=True)
                - xhat * jnp.mean(d_xhat * xhat, axis=-1, keepdims=True)
            )
            d_low = d_resid.astype(BF16)
            resid_ref[rows, :] = d_resid
            low_ref[rows, :] = d_low
            sums_ref[0:1, :] += row_sum(d_low.astype(F32))
            sums_ref[1:2, :] += row_sum(cot * xhat)
            sums_ref[2:3, :] += row_sum(cot)
            return carry

        lax.fori_loop(0, half, step, 0)

    side(True)
    side(False)


def ffn_out(place, acts, xhat, cotangent, cot_other, vectors, blocks):
    count = acts[0].shape[0]
    hidden = 2 * acts[0].shape[1]
    half, block, width = cot_other.shape
    slabs = sum(b.shape[0] for b in blocks) if len(blocks) > 1 else 1
    return vmem_call(
        functools.partial(ffn_out_kernel, count=len(blocks)),
        "ffn_out_norm",
        [
            ((half, block, width), BF16),
            ((half, block, width), BF16),
            ((count, width), F32),
            ((count, width), BF16),
            ((8, width), F32),
            ((hidden, width), BF16),
        ],
        12,
        cost(2 * count * hidden * width, 4 * hidden * width + 2 * count * hidden),
        [pltpu.SemaphoreType.DMA((slabs,))],
        places=1,
        anywhere=len(blocks),
    )(place, *acts, xhat, cotangent, cot_other, vectors, *blocks)


def slot(place_ref, xx, yy, core):
    same_x = jnp.where(place_ref[1] == xx, 1, 0)
    same_y = jnp.where(place_ref[3] == yy, 1, 0)
    return jnp.where(core == 0, same_y, same_x), jnp.where(core == 0, same_x, same_y)


def grad_out_kernel(place_ref, act_ref, low_ref, send_ref, keep_ref):
    c = place_ref[2]
    rows = send_ref.shape[3]
    for z in range(send_ref.shape[1]):
        for xx in range(2):
            at = (8 * z + 4 * xx) * rows
            total = dot_tn(act_ref[:, at : at + 4 * rows], low_ref[...])
            for yy in range(2):
                first = total[yy * rows : (yy + 1) * rows]
                second = total[(2 + yy) * rows : (3 + yy) * rows]
                away, stay = slot(place_ref, xx, yy, 1 - c), slot(place_ref, xx, yy, c)
                send_ref[away[0], z, away[1]] = jnp.where(c == 0, second, first).astype(BF16)
                keep_ref[stay[0], z, stay[1]] = jnp.where(c == 0, first, second)


def grad_out(place, act, d_low, rows):
    count = act.shape[0]
    width = d_low.shape[1]
    shape = (2, 2, 2, rows, width)
    return vmem_call(
        grad_out_kernel,
        "grad_w_out",
        [(shape, BF16), (shape, F32)],
        12,
        cost(32 * count * rows * width, 32 * count * rows),
        places=1,
    )(place, act, d_low)


def ffn_back_kernel(low_ref, resid_ref, slope_ref, w_out_ref, w_in_ref, *refs, at, tile, columns, last):
    if last:
        xhat_ref, rstd_ref, vec_ref, pre_ref, bias_ref, one_ref, mix_ref, sums_ref = refs
        sums_ref[...] = jnp.zeros_like(sums_ref)
    else:
        pre_ref, bias_ref, total_ref = refs
    hidden = pre_ref.shape[1]
    bias_ref[...] = jnp.zeros_like(bias_ref)

    def step(i, carry):
        rows = tile_rows(i, tile)
        d_low = low_ref[rows, :]
        d_normed = resid_ref[rows, :]
        for part in range(0, hidden, columns):
            cut, full = slice(part, part + columns), slice(at + part, at + part + columns)
            slope = slope_ref[rows, cut].astype(F32)
            d_pre = (dot_nt(d_low, w_out_ref[full, :]) * slope).astype(BF16)
            pre_ref[rows, cut] = d_pre
            bias_ref[0:1, cut] += row_sum(d_pre.astype(F32))
            d_normed += dot_nt(d_pre, w_in_ref[:, full])
        if not last:
            total_ref[rows, :] = d_normed
            return carry
        xhat = xhat_ref[rows, :]
        sums_ref[0:1, :] += row_sum(d_normed * xhat)
        sums_ref[1:2, :] += row_sum(d_normed)
        d_xhat = d_normed * vec_ref[1:2, :]
        d_one = rstd_ref[rows, :] * (
            d_xhat
            - jnp.mean(d_xhat, axis=-1, keepdims=True)
            - xhat * jnp.mean(d_xhat * xhat, axis=-1, keepdims=True)
        )
        one_ref[rows, :] = d_one
        mix_ref[rows, :] = d_one.astype(BF16)
        return carry

    lax.fori_loop(0, low_ref.shape[0] // tile, step, 0)


def ffn_back(d_low, d_resid, slope, w_out, w_in, part, norm=(), tile=256, columns=768):
    count, width = d_low.shape
    hidden = slope.shape[1]
    out_shape = [((count, hidden), BF16), ((8, hidden), F32), ((count, width), F32)]
    if norm:
        out_shape += [((count, width), BF16), ((8, width), F32)]
    return vmem_call(
        functools.partial(
            ffn_back_kernel, at=part * hidden, tile=tile, columns=columns, last=bool(norm)
        ),
        "ffn_back",
        out_shape,
        12,
        cost(4 * count * hidden * width, 6 * count * hidden + 4 * hidden * width),
    )(d_low, d_resid, slope, w_out, w_in, *norm)


def grad_in_kernel(place_ref, low_ref, pre_ref, *refs):
    c = place_ref[2]
    split = pre_ref.shape[1]
    if len(refs) == 2:
        send_ref, keep_ref = refs
    else:
        bias_0_ref, bias_1_ref, two_ref, one_ref, send_ref, keep_ref = refs
        owners, width = 32, low_ref.shape[0]
        size = width // owners

        def gathered(values, first, part):
            total = values.shape[1]
            mine = jnp.where(owner_mask(total // part, total), values, 0.0)
            matrix = spread_matrix(part, first, total).astype(F32)
            return lax.dot_general(
                mine, matrix, (((1,), (1,)), ((), ())), precision=lax.Precision.HIGHEST,
                preferred_element_type=F32,
            )

        line_0 = jnp.concatenate(
            [gathered(ref[0:1, :], 0, 4 * size) for ref in (bias_0_ref, bias_1_ref)], axis=0
        )
        line_1 = jnp.zeros((owners, LANES), F32)
        for i, (ref, row) in enumerate(
            ((two_ref, 0), (one_ref, 0), (one_ref, 1), (two_ref, 1), (two_ref, 2))
        ):
            line_1 += gathered(ref[row : row + 1, :], i * size, size)
        send_ref[:, :, :, :, split:] = jnp.zeros(send_ref.shape[:4] + (LANES,), BF16)
        keep_ref[:, :, :, :, split:] = jnp.zeros(keep_ref.shape[:4] + (LANES,), F32)
    rows = send_ref.shape[3]
    for z in range(4):
        total = dot(low_ref[8 * z * rows : 8 * (z + 1) * rows, :], pre_ref[...])
        for xx in range(2):
            for yy in range(2):
                at = (4 * xx + yy) * rows
                first, second = total[at : at + rows], total[at + 2 * rows : at + 3 * rows]
                away, stay = slot(place_ref, xx, yy, 1 - c), slot(place_ref, xx, yy, c)
                send_ref[away[0], z, away[1], :, :split] = jnp.where(c == 0, second, first).astype(BF16)
                keep_ref[stay[0], z, stay[1], :, :split] = jnp.where(c == 0, first, second)
                if len(refs) > 2:
                    at = 8 * z + 4 * xx + yy
                    for row, line in enumerate((line_0, line_1)):
                        first, second = line[at : at + 1], line[at + 2 : at + 3]
                        side = jnp.where(c == 0, second, first)
                        send_ref[away[0], z, away[1], row : row + 1, split:] = side.astype(BF16)
                        side = jnp.where(c == 0, first, second)
                        keep_ref[stay[0], z, stay[1], row : row + 1, split:] = side


def grad_in(place, low_t, d_pre, sums=()):
    width, count = low_t.shape
    hidden = d_pre.shape[1]
    rows = width // 32
    shape = (2, 4, 2, rows, hidden + (LANES if sums else 0))
    return vmem_call(
        grad_in_kernel,
        "grad_w_in",
        [(shape, BF16), (shape, F32)],
        14,
        cost(2 * count * width * hidden, 2 * count * hidden),
        places=1,
    )(place, low_t, d_pre, *sums)


def mix_back_kernel(place_ref, low_ref, one_ref, hid_ref, seq_ref, send_ref, keep_ref, spec_ref):
    width = low_ref.shape[1]
    length = seq_ref.shape[0]
    block = length // 2
    y = place_ref[3]

    def step(r, carry):
        for part in range(2):
            cut = slice(part * width, (part + 1) * width)
            spec = dot(low_ref[tile_rows(r, length), :], hid_ref[:, cut])
            spec_ref[part * length : (part + 1) * length, :] = spec.astype(BF16)
        for spot, away in ((1 - y, True), (y, False)):
            total = dot(seq_ref[tile_rows(spot, block), :], spec_ref[...])
            total += one_ref[tile_rows(2 * r + spot, block), :]
            if away:
                send_ref[r] = total.astype(BF16)
            else:
                keep_ref[r] = total
        return carry

    lax.fori_loop(0, low_ref.shape[0] // length, step, 0)


def mix_back(place, d_low, d_one, hid_table, seq_table):
    count, width = d_low.shape
    length = seq_table.shape[0]
    half, block = count // length, length // 2
    return vmem_call(
        mix_back_kernel,
        "mix_back",
        [((half, block, width), BF16), ((half, block, width), F32)],
        14,
        cost(4 * count * width * (length + width), 10 * count * width),
        [pltpu.VMEM((2 * length, width), BF16)],
        places=1,
    )(place, d_low, d_one, hid_table, seq_table)


def add_up(keep, other):
    return keep + other.astype(F32)


def per_device(grid, tokens, weight_in, bias_in, weight_out, bias_out, gain_mix, shift_mix, gain_ffn, shift_ffn, cotangent):
    rows, block, width = tokens.shape
    part_in, hidden = weight_in.shape
    part_out = weight_out.shape[0]
    half = rows // 2
    length = 2 * block
    devices = grid.dp * grid.seq
    z, x, c, y = grid.place()
    place = jnp.stack([z, x, c, y]).astype(jnp.int32)
    zero = jnp.uint32(0)
    across = ((1 - y) * half).astype(jnp.uint32)
    behind = [((z + 3 - step) % 4).astype(jnp.uint32) for step in range(4)]
    place, across, behind, weight_in = together(place, across, behind, weight_in)
    chained = grid.chained and part_in % 8 == 0

    def other_rows(value):
        return lax.dynamic_slice(value, (across, zero, zero), (half,) + value.shape[1:])

    def join_rows(keep, other):
        other = other.astype(keep.dtype)
        return jnp.where(
            y == 0, jnp.concatenate([keep, other], 0), jnp.concatenate([other, keep], 0)
        )

    def core(value):
        return send(value, grid.cores)

    smalls = (bias_in, bias_out, gain_mix, shift_mix, gain_ffn, shift_ffn)
    sizes = [v.shape[0] for v in smalls]
    spots = [(0, 0)] + [(1, i * sizes[1]) for i in range(5)]
    lines = [0, 0]
    for value, (line, at) in zip(smalls, spots):
        lines[line] += jnp.pad(value, (at, LANES - at - value.shape[0]))
    strip = jnp.pad(jnp.stack(lines), ((0, part_in - 2), (0, 0)))
    tok_other = send(other_rows(tokens), grid.blocks)

    cos_seq, sin_seq = dft_tables(length)
    cos_hid, sin_hid = dft_tables(width)
    mix_tables = (
        table(np.concatenate([cos_seq, sin_seq], 0)),
        table(np.concatenate([cos_hid, -sin_hid], 0)),
    )
    if chained:
        packed = jnp.concatenate([weight_in, strip], axis=1)
        packed, shard_out = together(packed, weight_out)
        piece_1, near_out = together(send(packed, grid.ring), send(shard_out, grid.across_0))
        pair = jnp.stack([shard_out, near_out])
        piece_2, far_pair = together(send(piece_1, grid.ring), send(pair, grid.across_1))
        piece_3, tok_other = together(send(piece_2, grid.ring), tok_other)
        column, pair, far_pair, tok_other = together(
            jnp.stack([packed, piece_1, piece_2, piece_3]), pair, far_pair, tok_other
        )
        pairs = [pair, far_pair]
        near, ring_pair, (xhat, rstd) = together(
            send(column, grid.across_0),
            send(pair, grid.ring),
            mix(place, tokens, tok_other, *mix_tables),
        )
        both = jnp.concatenate([column, near], axis=0)
        both, ring_pair, far_pair = together(both, ring_pair, far_pair)
        pairs.append(ring_pair)
        groups = [column, near, send(both, grid.across_1)]
        twins = [core(column), core(near)]
        groups[2], twins, ring_far, ring_pair = together(
            groups[2], twins, send(far_pair, grid.ring), send(ring_pair, grid.ring)
        )
        pairs += [ring_far, ring_pair]
        ring_far, ring_pair = send(ring_far, grid.ring), send(ring_pair, grid.ring)
        cot_other = send(after(other_rows(cotangent), groups[2]), grid.blocks)
        w_in, bias, vectors, low, low_t = first_weight(
            place, xhat, groups + twins + [core(groups[2])], hidden
        )
    else:
        cot_other = send(other_rows(cotangent), grid.blocks)
        xhat, rstd = mix(place, tokens, tok_other, *mix_tables)
        w_in = lax.all_gather(weight_in, AXES, axis=0, tiled=True)
        blocks = [lax.all_gather(weight_out, AXES, axis=0, tiled=True)]
        extra = lax.all_gather(strip, AXES, axis=0)[:, :2]
        bias, *vectors = [
            extra[:, line, at : at + size].reshape(1, -1).astype(F32)
            for size, (line, at) in zip(sizes, spots)
        ]
        vectors = jnp.concatenate(vectors + [jnp.zeros((3, width), F32)], axis=0)
        low, low_t = ffn_low(xhat, vectors)
    acts, slopes = [], []
    for i in range(2):
        act, slope = ffn_in(low, w_in, bias, i, 2)
        if chained and i == 0:
            act, slope, low, ring_far, ring_pair = together(act, slope, low, ring_far, ring_pair)
            pairs += [ring_far, ring_pair, send(ring_far, grid.ring)]
        if chained and i == 1:
            act, pairs[7], cot_other = together(act, pairs[7], cot_other)
            pairs = [pairs[k] for k in (0, 1, 2, 3, 4, 5, 6, 7)]
            blocks = pairs + [core(p) for p in pairs]
        acts.append(act)
        slopes.append(slope)

    out_send, out_keep, d_resid, d_low, sums_two, w_out = ffn_out(
        place, acts, xhat, cotangent, cot_other, vectors, blocks
    )

    norm = (xhat, rstd, vectors)
    back_tables = (
        table(np.concatenate([cos_hid, -sin_hid], 1)),
        table(np.concatenate([cos_seq, sin_seq], 1)),
    )

    def pack_small(bias_sum, norm_sum):
        grads = (bias_sum, sums_two[0], norm_sum[0], norm_sum[1], sums_two[1], sums_two[2])
        lines = [0, 0]
        for value, (line, at) in zip(grads, spots):
            value = value.reshape(devices, -1)
            lines[line] += jnp.pad(value, ((0, 0), (at, LANES - at - value.shape[1])))
        return jnp.pad(jnp.stack(lines, axis=1), ((0, 0), (0, part_in - 2), (0, 0)))

    def ring_step(column, part, step):
        own = pick(column, behind[step])
        return own if part is None else add_up(own, part)

    def low_send(value, perm):
        return send(value.astype(BF16), perm)

    if chained:
        away_a, keep_a = grad_out(place, acts[0], d_low, part_out)
        away_a, keep_a, start = together(away_a, keep_a, d_low)
        twin_a, (away_b, keep_b) = together(core(away_a), grad_out(place, acts[1], start, part_out))
        out_other = send(out_send, grid.blocks)
        twin_b, first_a, out_other, (pre_0, bias_0, d_normed) = together(
            core(away_b),
            low_send(add_up(keep_a[0], twin_a[0]), grid.across_1),
            out_other,
            ffn_back(start, d_resid, slopes[0], w_out, w_in, 0),
        )
        output = join_rows(out_keep, out_other)
        first_b, (away_0, keep_0), back = together(
            low_send(add_up(keep_b[0], twin_b[0]), grid.across_1),
            grad_in(place, low_t, pre_0),
            ffn_back(start, d_normed, slopes[1], w_out, w_in, 1, norm),
        )
        pre_1, bias_1, d_one, d_mix, norm_sum = back
        pair_a = add_up(add_up(keep_a[1], twin_a[1]), first_a)
        pair_b = add_up(add_up(keep_b[1], twin_b[1]), first_b)
        passed = jnp.concatenate([pair_a[:, 0].astype(BF16), pair_b[:, 0].astype(BF16)], axis=0)
        second, twin_0, (away_1, keep_1), d_mix = together(
            send(passed, grid.across_0),
            core(away_0),
            grad_in(place, low_t, pre_1, (bias_0, bias_1, sums_two, norm_sum)),
            d_mix,
        )
        column = add_up(jnp.concatenate([pair_a[:, 1], pair_b[:, 1]], axis=0), second)
        part = ring_step(column, None, 0)
        part, first_0, twin_1, (gt_send, gt_keep) = together(
            low_send(part, grid.ring),
            low_send(add_up(keep_0[0], twin_0[0]), grid.across_1),
            core(away_1),
            mix_back(place, d_mix, d_one, *back_tables),
        )
        part = ring_step(column, part, 1)
        pair_0 = add_up(add_up(keep_0[1], twin_0[1]), first_0)
        part, first_1, second_0 = together(
            low_send(part, grid.ring),
            low_send(add_up(keep_1[0], twin_1[0]), grid.across_1),
            low_send(pair_0[:, 0], grid.across_0),
        )
        part = ring_step(column, part, 2)
        pair_1 = add_up(add_up(keep_1[1], twin_1[1]), first_1)
        column_0 = add_up(pair_0[:, 1], second_0)
        part_0 = ring_step(column_0, None, 0)
        gt_other = [send(gt_send[:1], grid.blocks), None]
        part, second_1, part_0 = together(
            low_send(part, grid.ring),
            low_send(pair_1[:, 0], grid.across_0),
            low_send(part_0, grid.ring),
        )
        my_w_out = ring_step(column, part, 3)
        column_1 = add_up(pair_1[:, 1], second_1)
        part_0 = ring_step(column_0, part_0, 1)
        part_1 = ring_step(column_1, None, 0)
        part_0, part_1, gt_other[0] = together(
            low_send(part_0, grid.ring), low_send(part_1, grid.ring), gt_other[0]
        )
        part_0 = ring_step(column_0, part_0, 2)
        part_1 = ring_step(column_1, part_1, 1)
        gt_other[1] = send(after(gt_send[1:], gt_other[0]), grid.blocks)
        part_0, part_1 = together(low_send(part_0, grid.ring), low_send(part_1, grid.ring))
        mine_0 = ring_step(column_0, part_0, 3)
        part_1 = ring_step(column_1, part_1, 2)
        mine_1 = ring_step(column_1, low_send(part_1, grid.ring), 3)
        grad_tokens = join_rows(gt_keep, jnp.concatenate(gt_other, axis=0))
        my_w_in = jnp.concatenate([mine_0, mine_1[:, : hidden // 2]], axis=1)
        my_strip = mine_1[:2, hidden // 2 :]
    else:
        output = join_rows(out_keep, send(out_send, grid.blocks))
        grad_w_out = jnp.concatenate([dot_tn(act, d_low) for act in acts], axis=0)
        my_w_out = lax.psum_scatter(grad_w_out, AXES, scatter_dimension=0, tiled=True)
        pre_0, bias_0, d_normed = ffn_back(d_low, d_resid, slopes[0], w_out, w_in, 0)
        pre_1, bias_1, d_one, d_mix, norm_sum = ffn_back(
            d_low, d_normed, slopes[1], w_out, w_in, 1, norm
        )
        gt_send, gt_keep = mix_back(place, d_mix, d_one, *back_tables)
        grad_tokens = join_rows(gt_keep, send(gt_send, grid.blocks))
        grad_w_in = jnp.concatenate([dot(low_t, pre_0), dot(low_t, pre_1)], axis=1)
        my_w_in = lax.psum_scatter(grad_w_in, AXES, scatter_dimension=0, tiled=True)
        strips = pack_small(jnp.concatenate([bias_0[0], bias_1[0]]), norm_sum)
        my_strip = lax.psum_scatter(strips, AXES, scatter_dimension=0, tiled=True)[0, :2]
    my_small = [my_strip[line, at : at + size] for size, (line, at) in zip(sizes, spots)]
    return (
        output,
        grad_tokens,
        my_w_in,
        my_small[0],
        my_w_out,
        my_small[1],
        my_small[2],
        my_small[3],
        my_small[4],
        my_small[5],
    )


def solution(mesh):
    grid = Grid(mesh)
    cut, cut2 = P(AXES), P(AXES, None)
    block = P("dp", "seq", None)
    in_specs = (block, cut2, cut, cut2, cut, cut, cut, cut, cut, block)
    out_specs = (block, block, cut2, cut, cut2, cut, cut, cut, cut, cut)

    def program(*arrays):
        return per_device(grid, *arrays)

    return jax.shard_map(
        program, mesh=mesh, in_specs=in_specs, out_specs=out_specs, check_vma=False
    )
```

```python
import functools
import math

import jax
import jax.numpy as jnp
import numpy as np
from jax import lax
from jax.experimental import pallas as pl
from jax.experimental.pallas import tpu as pltpu
from jax.sharding import PartitionSpec as P

EPS = 1e-12
AXES = ("dp", "seq")
BF16 = jnp.bfloat16
F32 = jnp.float32
MIB = 1 << 20
LANES = 128
ERF_T = 0.3275911
ERF_P = (0.254829592, -0.284496736, 1.421413741, -1.453152027, 1.061405429)


def dft_tables(length):
    index = np.arange(length, dtype=np.int64)
    angle = (index[:, None] * index[None, :] % length).astype(np.float64) * (2.0 * math.pi / length)
    scale = length ** (-0.5)
    return np.cos(angle) * scale, np.sin(angle) * scale


def table(values):
    return jnp.asarray(values.astype(np.float32)).astype(BF16)


class Grid:
    def __init__(self, mesh):
        self.dp = mesh.shape["dp"]
        self.seq = mesh.shape["seq"]
        chips = self.dp // 2
        self.low = min(2, chips)
        self.high = chips // self.low
        self.shifts = [
            self.perm(lambda z, x, c, y: ((z + step) % self.high, x, c, y)) for step in range(4)
        ]
        self.ring = self.shifts[1]
        self.across = self.perm(lambda z, x, c, y: (z, (x + 1) % self.low, c, y))
        self.corner = self.perm(
            lambda z, x, c, y: (z, (x + 1) % self.low, c, (y + 1) % self.seq)
        )
        self.cores = self.perm(lambda z, x, c, y: (z, x, 1 - c, y))
        self.blocks = self.perm(lambda z, x, c, y: (z, x, c, (y + 1) % self.seq))
        self.across_0 = self.perm(
            lambda z, x, c, y: (z, (x + 1 - c) % self.low, c, (y + c) % self.seq)
        )
        self.across_1 = self.perm(
            lambda z, x, c, y: (z, (x + c) % self.low, c, (y + 1 - c) % self.seq)
        )
        self.chained = self.high == 4 and self.low == 2 and self.seq == 2

    def index(self, z, x, c, y):
        return ((z * self.low + x) * 2 + c) * self.seq + y

    def perm(self, move):
        return [
            (self.index(z, x, c, y), self.index(*move(z, x, c, y)))
            for z in range(self.high)
            for x in range(self.low)
            for c in range(2)
            for y in range(self.seq)
        ]

    def place(self):
        dp = lax.axis_index("dp")
        return dp // (2 * self.low), dp // 2 % self.low, dp % 2, lax.axis_index("seq")


def send(value, perm):
    return lax.ppermute(value, AXES, perm)


def pick(value, index):
    zero = jnp.uint32(0)
    starts = (index,) + (zero,) * (value.ndim - 1)
    return lax.dynamic_slice(value, starts, (1,) + value.shape[1:])[0]


def dot(a, b):
    return jnp.dot(a, b, preferred_element_type=F32)


def dot_nt(a, b):
    return lax.dot_general(a, b, (((1,), (1,)), ((), ())), preferred_element_type=F32)


def dot_tn(a, b):
    return lax.dot_general(a, b, (((0,), (0,)), ((), ())), preferred_element_type=F32)


def params(mib):
    return pltpu.CompilerParams(vmem_limit_bytes=mib * MIB)


def cost(flops, bytes_accessed, transcendentals=0):
    return pl.CostEstimate(
        flops=int(flops), bytes_accessed=int(bytes_accessed), transcendentals=int(transcendentals)
    )


def row_sum(values):
    return jnp.sum(values, axis=0, keepdims=True)


def after(value, *others):
    return lax.optimization_barrier((value,) + others)[0]


def together(*values):
    return lax.optimization_barrier(values)


def device_number(place, distance, flip_x, flip_y, other_core):
    z, x, c, y = place
    zz = lax.rem(z - distance + 4, 4)
    cc = 1 - c if other_core else c
    xx = x + flip_x - 2 * x * flip_x
    yy = y + flip_y - 2 * y * flip_y
    return ((zz * 2 + xx) * 2 + cc) * 2 + yy


def column_slab(part, index, core):
    group = part + index // 4
    flip_x, flip_y = ((0, 0), (1 - core, core), (core, 1 - core), (1, 1))[group]
    return index % 4, flip_x, flip_y


def pair_slab(part, index, core):
    return part // 2, index, part % 2


def copy_slabs(place, refs, slab_of, start_copy):
    for part, ref in enumerate(refs):
        own = len(refs) // 2
        for i in range(ref.shape[0]):
            core = 1 - place[2] if part >= own else place[2]
            where = slab_of(part % own, i, core)
            start_copy(ref.at[i], device_number(place, *where, part >= own))


def vmem_call(kernel, name, out_shape, mib, work, scratch_shapes=(), places=0, anywhere=0, outside=False):
    def call(*operands):
        here = len(operands) - places - anywhere
        return pl.pallas_call(
            kernel,
            name=name,
            in_specs=[pl.BlockSpec(memory_space=pltpu.SMEM)] * places
            + [pl.BlockSpec(memory_space=pltpu.VMEM)] * here
            + [pl.BlockSpec(memory_space=pl.ANY)] * anywhere,
            out_specs=[pl.BlockSpec(memory_space=pl.ANY if outside else pltpu.VMEM)] * len(out_shape),
            out_shape=[jax.ShapeDtypeStruct(*each) for each in out_shape],
            scratch_shapes=list(scratch_shapes),
            compiler_params=params(mib),
            cost_estimate=work,
        )(*operands)

    return call


def tile_rows(index, size):
    return pl.ds(pl.multiple_of(index * size, size), size)


def assemble(place, groups, split):
    _, rows, columns = groups[0].shape
    slabs = sum(group.shape[0] for group in groups)
    return vmem_call(
        functools.partial(assemble_kernel, count=len(groups), split=split),
        "assemble_w_in",
        [((slabs * rows, split), BF16), ((slabs, rows, LANES), BF16)],
        2,
        cost(0, 4 * slabs * rows * columns),
        [pltpu.SemaphoreType.DMA((2 * slabs,))],
        places=1,
        anywhere=len(groups),
    )(place, *groups)


def spread_matrix(size, start, total):
    lane = lax.broadcasted_iota(jnp.int32, (LANES, total), 0)
    column = lax.broadcasted_iota(jnp.int32, (LANES, total), 1)
    return lane == start + lax.rem(column, size)


def owner_mask(owners, total):
    owner = lax.broadcasted_iota(jnp.int32, (owners, total), 0)
    column = lax.broadcasted_iota(jnp.int32, (owners, total), 1)
    return lax.div(column, total // owners) == owner


def first_weight_kernel(place_ref, xhat_ref, *refs, count, split):
    groups = refs[:count]
    full_ref, bias_ref, vec_ref, low_ref, low_t_ref, extra_ref, sem = refs[count:]
    rows = groups[0].shape[1]
    place = tuple(place_ref[i] for i in range(4))
    sides, mains = [], []

    def add(slab, at):
        side = slab.at[:, pl.ds(split, LANES)]
        sides.append(pltpu.make_async_copy(side, extra_ref.at[at], sem.at[2 * len(sides)]))
        target = full_ref.at[tile_rows(at, rows), :]
        main = slab.at[:, pl.ds(0, split)]
        mains.append(pltpu.make_async_copy(main, target, sem.at[2 * len(mains) + 1]))

    copy_slabs(place, groups, column_slab, add)
    for copy in sides + mains:
        copy.start()
    for copy in sides:
        copy.wait()
    owners, width = extra_ref.shape[0], vec_ref.shape[1]
    line = extra_ref[:, 0, :]
    wide = dot(line, spread_matrix(split // owners, 0, split).astype(BF16))
    bias_ref[...] = row_sum(jnp.where(owner_mask(owners, split), wide, 0.0))
    line = extra_ref[:, 1, :]
    mask = owner_mask(owners, width)
    size = width // owners
    vec_ref[...] = jnp.zeros_like(vec_ref)
    for i in range(5):
        wide = dot(line, spread_matrix(size, i * size, width).astype(BF16))
        vec_ref[i : i + 1, :] = row_sum(jnp.where(mask, wide, 0.0))
    low = (xhat_ref[...] * vec_ref[1:2, :] + vec_ref[2:3, :]).astype(BF16)
    low_ref[...] = low
    low_t_ref[...] = low.T
    for copy in mains:
        copy.wait()


def first_weight(place, xhat, groups, split):
    _, rows, columns = groups[0].shape
    slabs = sum(group.shape[0] for group in groups)
    count, width = xhat.shape
    return vmem_call(
        functools.partial(first_weight_kernel, count=len(groups), split=split),
        "first_weight",
        [
            ((slabs * rows, split), BF16),
            ((1, split), F32),
            ((8, width), F32),
            ((count, width), BF16),
            ((width, count), BF16),
        ],
        10,
        cost(2 * count * width, 4 * slabs * rows * columns),
        [pltpu.VMEM((slabs, rows, LANES), BF16), pltpu.SemaphoreType.DMA((2 * slabs,))],
        places=1,
        anywhere=len(groups),
    )(place, xhat, *groups)


def mix_kernel(place_ref, mine_ref, other_ref, seq_ref, hid_ref, xhat_ref, rstd_ref, row_ref):
    half, block, width = other_ref.shape
    length = 2 * block
    y = place_ref[3]

    def step(r, carry):
        row_ref[tile_rows(y, block), :] = mine_ref[half * y + r]
        row_ref[tile_rows(1 - y, block), :] = other_ref[r]
        tokens = row_ref[...]
        for part in range(2):
            at = part * block
            cos_part = dot(seq_ref[at : at + block, :], tokens).astype(BF16)
            sin_part = dot(seq_ref[length + at : length + at + block, :], tokens).astype(BF16)
            mixed = dot(cos_part, hid_ref[:width, :]) + dot(sin_part, hid_ref[width:, :])
            resid = tokens[at : at + block, :].astype(F32) + mixed
            center = resid - jnp.mean(resid, axis=-1, keepdims=True)
            rstd = lax.rsqrt(jnp.mean(center * center, axis=-1, keepdims=True) + EPS)
            rows = tile_rows(2 * r + part, block)
            xhat_ref[rows, :] = center * rstd
            rstd_ref[rows, :] = rstd
        return carry

    lax.fori_loop(0, half, step, 0)


def mix(place, tokens, other, seq_table, hid_table):
    half, block, width = other.shape
    length = 2 * block
    count = half * length
    return vmem_call(
        mix_kernel,
        "mix_norm",
        [((count, width), F32), ((count, 1), F32)],
        14,
        cost(4 * count * width * (length + width), 10 * count * width),
        [pltpu.VMEM((length, width), BF16)],
        places=1,
    )(place, tokens, other, seq_table, hid_table)


def gelu_both(values):
    size = jnp.abs(values)
    t = 1.0 / (1.0 + (ERF_T / math.sqrt(2.0)) * size)
    bell = jnp.exp(-0.5 * (values * values))
    poly = 0.5 * ERF_P[4]
    for term in ERF_P[3::-1]:
        poly = 0.5 * term + t * poly
    tail = t * poly * bell
    phi = jnp.where(values > 0, 1.0 - tail, tail)
    return values * phi, phi + values * (bell * (1.0 / math.sqrt(2.0 * math.pi)))


def ffn_low_kernel(xhat_ref, vec_ref, low_ref, low_t_ref):
    low = (xhat_ref[...] * vec_ref[1:2, :] + vec_ref[2:3, :]).astype(BF16)
    low_ref[...] = low
    low_t_ref[...] = low.T


def ffn_low(xhat, vectors):
    count, width = xhat.shape
    return vmem_call(
        ffn_low_kernel,
        "normed_low",
        [((count, width), BF16), ((width, count), BF16)],
        8,
        cost(2 * count * width, 8 * count * width),
    )(xhat, vectors)


def ffn_in_kernel(low_ref, w_ref, bias_ref, act_ref, slope_ref, *, at, tile, columns):
    hidden = act_ref.shape[1]
    for part in range(0, hidden, columns):
        cut, full = slice(part, part + columns), slice(at + part, at + part + columns)

        def step(i, carry):
            rows = tile_rows(i, tile)
            hidden_pre = dot(low_ref[rows, :], w_ref[:, full]) + bias_ref[:, full]
            act, slope = gelu_both(hidden_pre)
            act_ref[rows, cut] = act.astype(BF16)
            slope_ref[rows, cut] = slope.astype(BF16)
            return carry

        lax.fori_loop(0, low_ref.shape[0] // tile, step, 0)


def ffn_in(low, w_in, bias, part, parts, columns=768, tile=512):
    count, width = low.shape
    hidden = w_in.shape[1] // parts
    return vmem_call(
        functools.partial(ffn_in_kernel, at=part * hidden, tile=tile, columns=columns),
        "ffn_in_gelu",
        [((count, hidden), BF16)] * 2,
        14,
        cost(2 * count * width * hidden, 4 * count * hidden, 2 * count * hidden),
    )(low, w_in, bias)


def ffn_out_kernel(place_ref, act_0_ref, act_1_ref, xhat_ref, mine_ref, other_ref, vec_ref, *refs, count):
    groups = refs[:count]
    send_ref, keep_ref, resid_ref, low_ref, sums_ref, w_ref, branch_ref, sem = refs[count:]
    half, block, _ = other_ref.shape
    y = place_ref[3]
    place = tuple(place_ref[i] for i in range(4))
    copies = []
    if count == 1:
        copies.append(pltpu.make_async_copy(groups[0], w_ref, sem.at[0]))
    else:
        rows = groups[0].shape[1]

        def add(slab, at):
            target = w_ref.at[tile_rows(at, rows), :]
            copies.append(pltpu.make_async_copy(slab, target, sem.at[len(copies)]))

        copy_slabs(place, groups, pair_slab, add)
    for copy in copies:
        copy.start()
    sums_ref[...] = jnp.zeros_like(sums_ref)
    bias, gain_mix, shift_mix = vec_ref[0:1, :], vec_ref[1:2, :], vec_ref[2:3, :]
    gain, shift = vec_ref[3:4, :], vec_ref[4:5, :]
    cut = act_0_ref.shape[1]
    for copy in copies:
        copy.wait()

    def rows_of(step):
        away, r = step < half, step % half
        return tile_rows(2 * r + (1 - y if away else y), block)

    def multiply(step):
        rows = rows_of(step)
        return dot(act_0_ref[rows, :], w_ref[:cut, :]) + dot(act_1_ref[rows, :], w_ref[cut:, :])

    def finish(step, branch):
        away, r = step < half, step % half
        rows = rows_of(step)
        value = xhat_ref[rows, :] * gain_mix + shift_mix + (branch + bias)
        center = value - jnp.mean(value, axis=-1, keepdims=True)
        rstd = lax.rsqrt(jnp.mean(center * center, axis=-1, keepdims=True) + EPS)
        xhat = center * rstd
        result = (xhat * gain + shift).astype(BF16)
        if away:
            send_ref[r] = result
            cot = other_ref[r].astype(F32)
        else:
            keep_ref[r] = result
            cot = mine_ref[half * y + r].astype(F32)
        d_xhat = cot * gain
        d_resid = rstd * (
            d_xhat
            - jnp.mean(d_xhat, axis=-1, keepdims=True)
            - xhat * jnp.mean(d_xhat * xhat, axis=-1, keepdims=True)
        )
        d_low = d_resid.astype(BF16)
        resid_ref[rows, :] = d_resid
        low_ref[rows, :] = d_low
        sums_ref[0:1, :] += row_sum(d_low.astype(F32))
        sums_ref[1:2, :] += row_sum(cot * xhat)
        sums_ref[2:3, :] += row_sum(cot)

    branch_ref[0] = multiply(0)
    for step in range(2 * half):
        if step + 1 < 2 * half:
            branch_ref[(step + 1) % 2] = multiply(step + 1)
        finish(step, branch_ref[step % 2])


def ffn_out(place, acts, xhat, cotangent, cot_other, vectors, blocks):
    count = acts[0].shape[0]
    hidden = 2 * acts[0].shape[1]
    half, block, width = cot_other.shape
    slabs = sum(b.shape[0] for b in blocks) if len(blocks) > 1 else 1
    return vmem_call(
        functools.partial(ffn_out_kernel, count=len(blocks)),
        "ffn_out_norm",
        [
            ((half, block, width), BF16),
            ((half, block, width), BF16),
            ((count, width), F32),
            ((count, width), BF16),
            ((8, width), F32),
            ((hidden, width), BF16),
        ],
        10,
        cost(2 * count * hidden * width, 4 * hidden * width + 2 * count * hidden),
        [pltpu.VMEM((2, block, width), F32), pltpu.SemaphoreType.DMA((slabs,))],
        places=1,
        anywhere=len(blocks),
    )(place, *acts, xhat, cotangent, cot_other, vectors, *blocks)


def slot(place_ref, xx, yy, core):
    same_x = jnp.where(place_ref[1] == xx, 1, 0)
    same_y = jnp.where(place_ref[3] == yy, 1, 0)
    return jnp.where(core == 0, same_y, same_x), jnp.where(core == 0, same_x, same_y)


def grad_out_kernel(place_ref, act_0_ref, act_1_ref, low_ref, send_ref, keep_ref, *, first):
    c = place_ref[2]
    rows = send_ref.shape[2]
    columns = 8 * rows

    def group(xx, yy):
        return jnp.where(place_ref[3] == yy, 0, 1) + jnp.where(place_ref[1] == xx, 0, 2)

    def step(t, carry):
        owner = lax.rem(place_ref[0] + 7 - first - t, 4)
        for z in range(4):

            @pl.when(owner == z)
            def _():
                act_ref = (act_0_ref, act_1_ref)[z // 2]
                for xx in range(2):
                    at = z % 2 * columns + 4 * xx * rows
                    total = dot_tn(act_ref[:, at : at + 4 * rows], low_ref[...])
                    for yy in range(2):
                        one = total[yy * rows : (yy + 1) * rows]
                        two = total[(2 + yy) * rows : (3 + yy) * rows]
                        send_ref[t, group(xx, yy)] = jnp.where(c == 0, two, one).astype(BF16)
                        keep_ref[t, group(xx, yy)] = jnp.where(c == 0, one, two)

        return carry

    lax.fori_loop(0, send_ref.shape[0], step, 0)


def grad_out(place, acts, d_low, rows, first, steps):
    count, width = d_low.shape
    shape = (steps, 4, rows, width)
    return vmem_call(
        functools.partial(grad_out_kernel, first=first),
        "grad_w_out",
        [(shape, BF16), (shape, F32)],
        6,
        cost(16 * steps * count * rows * width, 16 * steps * count * rows),
        places=1,
    )(place, *acts, d_low)


def ffn_back_kernel(place_ref, low_ref, resid_ref, slope_0_ref, slope_1_ref, w_out_ref, w_in_ref, xhat_ref, rstd_ref, vec_ref, low_t_ref, two_ref, *refs, tile, columns):
    if len(refs) == 7:
        mix_ref, one_ref, send_ref, keep_ref, pre_ref, bias_ref, sums_ref = refs
    else:
        mix_ref, one_ref, pre_ref, bias_ref, sums_ref = refs
    hidden = pre_ref.shape[1]
    share = slope_0_ref.shape[1]
    bias_ref[...] = jnp.zeros_like(bias_ref)
    sums_ref[...] = jnp.zeros_like(sums_ref)

    def step(i, carry):
        rows = tile_rows(i, tile)
        d_low = low_ref[rows, :]
        d_normed = resid_ref[rows, :]
        for part in range(0, hidden, columns):
            cut = slice(part, part + columns)
            slope_ref = (slope_0_ref, slope_1_ref)[part // share]
            slope = slope_ref[rows, part % share : part % share + columns].astype(F32)
            d_pre = (dot_nt(d_low, w_out_ref[cut, :]) * slope).astype(BF16)
            pre_ref[rows, cut] = d_pre
            bias_ref[0:1, cut] += row_sum(d_pre.astype(F32))
            d_normed += dot_nt(d_pre, w_in_ref[:, cut])
        xhat = xhat_ref[rows, :]
        sums_ref[0:1, :] += row_sum(d_normed * xhat)
        sums_ref[1:2, :] += row_sum(d_normed)
        d_xhat = d_normed * vec_ref[1:2, :]
        d_one = rstd_ref[rows, :] * (
            d_xhat
            - jnp.mean(d_xhat, axis=-1, keepdims=True)
            - xhat * jnp.mean(d_xhat * xhat, axis=-1, keepdims=True)
        )
        one_ref[rows, :] = d_one
        mix_ref[rows, :] = d_one.astype(BF16)
        return carry

    lax.fori_loop(0, low_ref.shape[0] // tile, step, 0)
    if len(refs) == 7:
        grad_in_part(place_ref, low_t_ref, pre_ref, bias_ref, two_ref, sums_ref, send_ref, keep_ref)


def grad_in_part(place_ref, low_ref, pre_ref, bias_ref, two_ref, one_ref, send_ref, keep_ref):
    c = place_ref[2]
    split = pre_ref.shape[1]
    owners, width = 32, low_ref.shape[0]
    size = width // owners

    def gathered(values, first, part):
        total = values.shape[1]
        high = values.astype(BF16)
        rest = values - high.astype(F32)
        middle = rest.astype(BF16)
        lowest = (rest - middle.astype(F32)).astype(BF16)
        matrix = spread_matrix(part, first, total).astype(BF16)
        mask = owner_mask(total // part, total)
        return sum(dot_nt(jnp.where(mask, piece, 0.0).astype(BF16), matrix) for piece in (high, middle, lowest))

    line_0 = gathered(bias_ref[0:1, :], 0, 4 * size)
    line_1 = jnp.zeros((owners, LANES), F32)
    for i, (ref, row) in enumerate(
        ((two_ref, 0), (one_ref, 0), (one_ref, 1), (two_ref, 1), (two_ref, 2))
    ):
        line_1 += gathered(ref[row : row + 1, :], i * size, size)
    send_ref[:, :, :, :, split:] = jnp.zeros(send_ref.shape[:4] + (LANES,), BF16)
    keep_ref[:, :, :, :, split:] = jnp.zeros(keep_ref.shape[:4] + (LANES,), F32)
    rows = send_ref.shape[3]
    columns = split // 2
    for z in range(4):
        for cut in (slice(0, columns), slice(columns, split)):
            total = dot(low_ref[8 * z * rows : 8 * (z + 1) * rows, :], pre_ref[:, cut])
            for xx in range(2):
                for yy in range(2):
                    at = (4 * xx + yy) * rows
                    first, second = total[at : at + rows], total[at + 2 * rows : at + 3 * rows]
                    away, stay = slot(place_ref, xx, yy, 1 - c), slot(place_ref, xx, yy, c)
                    send_ref[away[0], z, away[1], :, cut] = jnp.where(c == 0, second, first).astype(BF16)
                    keep_ref[stay[0], z, stay[1], :, cut] = jnp.where(c == 0, first, second)
        for xx in range(2):
            for yy in range(2):
                at = 8 * z + 4 * xx + yy
                away, stay = slot(place_ref, xx, yy, 1 - c), slot(place_ref, xx, yy, c)
                for row, line in enumerate((line_0, line_1)):
                    first, second = line[at : at + 1], line[at + 2 : at + 3]
                    side = jnp.where(c == 0, second, first)
                    send_ref[away[0], z, away[1], row : row + 1, split:] = side.astype(BF16)
                    side = jnp.where(c == 0, first, second)
                    keep_ref[stay[0], z, stay[1], row : row + 1, split:] = side


def ffn_back(place, d_low, d_resid, slopes, w_out, w_in, norm, low_t, sums_two, chained, tile=256, columns=768):
    count, width = d_low.shape
    hidden = 2 * slopes[0].shape[1]
    out_shape = [((count, width), BF16), ((count, width), F32)]
    backs = [((count, hidden), BF16), ((8, hidden), F32), ((8, width), F32)]
    scratch_shapes = []
    if chained:
        shape = (2, 4, 2, width // 32, hidden + LANES)
        out_shape += [(shape, BF16), (shape, F32)]
        scratch_shapes = [pltpu.VMEM(*each) for each in backs]
    else:
        out_shape += backs
    return vmem_call(
        functools.partial(ffn_back_kernel, tile=tile, columns=columns),
        "ffn_back",
        out_shape,
        12 if chained else 10,
        cost(6 * count * hidden * width, 6 * count * hidden + 4 * hidden * width),
        scratch_shapes,
        places=1,
    )(place, d_low, d_resid, *slopes, w_out, w_in, *norm, low_t, sums_two)


def mix_back_kernel(place_ref, low_ref, one_ref, hid_ref, seq_ref, send_ref, keep_ref, spec_ref):
    width = low_ref.shape[1]
    length = seq_ref.shape[0]
    block = length // 2
    y = place_ref[3]

    def step(r, carry):
        for part in range(2):
            cut = slice(part * width, (part + 1) * width)
            spec = dot(low_ref[tile_rows(r, length), :], hid_ref[:, cut])
            spec_ref[part * length : (part + 1) * length, :] = spec.astype(BF16)
        for spot, away in ((1 - y, True), (y, False)):
            total = dot(seq_ref[tile_rows(spot, block), :], spec_ref[...])
            total += one_ref[tile_rows(2 * r + spot, block), :]
            if away:
                send_ref[r] = total.astype(BF16)
            else:
                keep_ref[r] = total
        return carry

    lax.fori_loop(0, low_ref.shape[0] // length, step, 0)


def mix_back(place, d_low, d_one, hid_table, seq_table):
    count, width = d_low.shape
    length = seq_table.shape[0]
    half, block = count // length, length // 2
    return vmem_call(
        mix_back_kernel,
        "mix_back",
        [((half, block, width), BF16), ((half, block, width), F32)],
        14,
        cost(4 * count * width * (length + width), 10 * count * width),
        [pltpu.VMEM((2 * length, width), BF16)],
        places=1,
    )(place, d_low, d_one, hid_table, seq_table)


def join_kernel(place_ref, keep_ref, *refs):
    *others, out_ref, wide_ref, sem = refs
    y = place_ref[3]
    half = keep_ref.shape[0]
    copies = [pltpu.make_async_copy(keep_ref, out_ref.at[pl.ds(half * y, half)], sem.at[0])]
    copies[0].start()
    at = half * (1 - y)
    for i, ref in enumerate(others):
        rows = ref.shape[0]
        if ref.dtype == keep_ref.dtype:
            source = ref
        else:
            source = wide_ref.at[pl.ds(i * rows, rows)]
            wide_ref[i * rows : (i + 1) * rows] = ref[...].astype(wide_ref.dtype)
        copies.append(
            pltpu.make_async_copy(source, out_ref.at[pl.ds(at + i * rows, rows)], sem.at[i + 1])
        )
        copies[-1].start()
    for copy in copies:
        copy.wait()


def join(place, keep, *others):
    half, block, width = keep.shape
    wide = keep.shape if others[0].dtype != keep.dtype else (1, 8, LANES)
    return vmem_call(
        join_kernel,
        "join_rows",
        [((2 * half, block, width), keep.dtype)],
        4,
        cost(0, 16 * half * block * width),
        [pltpu.VMEM(wide, keep.dtype), pltpu.SemaphoreType.DMA((1 + len(others),))],
        places=1,
        outside=True,
    )(place, keep, *others)[0]


def finish_kernel(own_ref, *refs, spots):
    parts, (w_ref, *smalls) = refs[:3], refs[3:]
    split = w_ref.shape[1]
    total = own_ref[...]
    for ref in parts:
        total += ref[...].astype(F32)
    w_ref[...] = total[:, :split]
    for ref, (line, at) in zip(smalls, spots):
        ref[...] = total[line : line + 1, split + at : split + at + ref.shape[1]]


def finish(own, parts, split, sizes, spots):
    rows, _ = own.shape
    return vmem_call(
        functools.partial(finish_kernel, spots=spots),
        "finish_w_in",
        [((rows, split), F32)] + [((1, size), F32) for size in sizes],
        4,
        cost(3 * rows * split, 14 * rows * split),
    )(own, *parts)


def add_up(keep, other):
    return keep + other.astype(F32)


def per_device(grid, tokens, weight_in, bias_in, weight_out, bias_out, gain_mix, shift_mix, gain_ffn, shift_ffn, cotangent):
    rows, block, width = tokens.shape
    part_in, hidden = weight_in.shape
    part_out = weight_out.shape[0]
    half = rows // 2
    length = 2 * block
    devices = grid.dp * grid.seq
    z, x, c, y = grid.place()
    place = jnp.stack([z, x, c, y]).astype(jnp.int32)
    zero = jnp.uint32(0)
    across = ((1 - y) * half).astype(jnp.uint32)
    ahead = [((z + step) % 4).astype(jnp.uint32) for step in range(4)]
    place, across, ahead, weight_in = together(place, across, ahead, weight_in)
    chained = grid.chained and part_in % 8 == 0

    def other_rows(value):
        return lax.dynamic_slice(value, (across, zero, zero), (half,) + value.shape[1:])

    def join_rows(keep, other):
        other = other.astype(keep.dtype)
        return jnp.where(
            y == 0, jnp.concatenate([keep, other], 0), jnp.concatenate([other, keep], 0)
        )

    def core(value):
        return send(value, grid.cores)

    smalls = (bias_in, bias_out, gain_mix, shift_mix, gain_ffn, shift_ffn)
    sizes = [v.shape[0] for v in smalls]
    spots = [(0, 0)] + [(1, i * sizes[1]) for i in range(5)]
    lines = [0, 0]
    for value, (line, at) in zip(smalls, spots):
        lines[line] += jnp.pad(value, (at, LANES - at - value.shape[0]))
    strip = jnp.pad(jnp.stack(lines), ((0, part_in - 2), (0, 0)))
    tok_other = send(other_rows(tokens), grid.blocks)

    cos_seq, sin_seq = dft_tables(length)
    cos_hid, sin_hid = dft_tables(width)
    mix_tables = (
        table(np.concatenate([cos_seq, sin_seq], 0)),
        table(np.concatenate([cos_hid, -sin_hid], 0)),
    )
    if chained:
        packed = jnp.concatenate([weight_in, strip], axis=1)
        packed, shard_out = together(packed, weight_out)
        *pieces, near_out, tok_other = together(
            *(send(packed, grid.shifts[step]) for step in range(1, 4)),
            send(shard_out, grid.across),
            tok_other,
        )
        pair = jnp.stack([shard_out, near_out])
        column = jnp.stack([packed] + pieces)
        column, pair, tok_other = together(column, pair, tok_other)
        near, ring_pair, far_pair, (xhat, rstd) = together(
            send(column, grid.across_0),
            send(pair, grid.ring),
            send(pair, grid.blocks),
            mix(place, tokens, tok_other, *mix_tables),
        )
        pairs = [pair, far_pair]
        both = jnp.concatenate([column, near], axis=0)
        both, ring_pair, far_pair = together(both, ring_pair, far_pair)
        pairs.append(ring_pair)
        groups = [column, near, send(both, grid.across_1)]
        twins = [core(column), core(near)]
        groups[2], twins, ring_far, ring_pair = together(
            groups[2], twins, send(far_pair, grid.ring), send(ring_pair, grid.ring)
        )
        pairs += [ring_far, ring_pair]
        ring_far, ring_pair = send(ring_far, grid.ring), send(ring_pair, grid.ring)
        cot_other = send(after(other_rows(cotangent), groups[2]), grid.blocks)
        w_in, bias, vectors, low, low_t = first_weight(
            place, xhat, groups + twins + [core(groups[2])], hidden
        )
    else:
        cot_other = send(other_rows(cotangent), grid.blocks)
        xhat, rstd = mix(place, tokens, tok_other, *mix_tables)
        w_in = lax.all_gather(weight_in, AXES, axis=0, tiled=True)
        blocks = [lax.all_gather(weight_out, AXES, axis=0, tiled=True)]
        extra = lax.all_gather(strip, AXES, axis=0)[:, :2]
        bias, *vectors = [
            extra[:, line, at : at + size].reshape(1, -1).astype(F32)
            for size, (line, at) in zip(sizes, spots)
        ]
        vectors = jnp.concatenate(vectors + [jnp.zeros((3, width), F32)], axis=0)
        low, low_t = ffn_low(xhat, vectors)
    acts, slopes = [], []
    for i in range(2):
        act, slope = ffn_in(low, w_in, bias, i, 2)
        if chained and i == 0:
            act, slope, low, ring_far, ring_pair = together(act, slope, low, ring_far, ring_pair)
            pairs += [ring_far, ring_pair, send(ring_far, grid.ring)]
        if chained and i == 1:
            act, pairs[7], cot_other = together(act, pairs[7], cot_other)
            pairs = [pairs[k] for k in (0, 1, 2, 3, 4, 5, 6, 7)]
            blocks = pairs + [core(p) for p in pairs]
        acts.append(act)
        slopes.append(slope)

    out_send, out_keep, d_resid, d_low, sums_two, w_out = ffn_out(
        place, acts, xhat, cotangent, cot_other, vectors, blocks
    )

    norm = (xhat, rstd, vectors)
    back_tables = (
        table(np.concatenate([cos_hid, -sin_hid], 1)),
        table(np.concatenate([cos_seq, sin_seq], 1)),
    )

    def pack_small(bias_sum, norm_sum):
        grads = (bias_sum, sums_two[0], norm_sum[0], norm_sum[1], sums_two[1], sums_two[2])
        lines = [0, 0]
        for value, (line, at) in zip(grads, spots):
            value = value.reshape(devices, -1)
            lines[line] += jnp.pad(value, ((0, 0), (at, LANES - at - value.shape[1])))
        return jnp.pad(jnp.stack(lines, axis=1), ((0, 0), (0, part_in - 2), (0, 0)))

    def low_send(value, perm):
        return send(value.astype(BF16), perm)

    if chained:
        (away_a, keep_a), start = together(grad_out(place, acts, d_low, part_out, 0, 1), d_low)
        twin_a, (away_b, keep_b) = together(core(away_a), grad_out(place, acts, start, part_out, 1, 3))
        quad = add_up(keep_a[0], twin_a[0])
        start, away_b, quad, out_send = together(start, away_b, quad, out_send)
        twin_b, ring, out_other, (d_mix, d_one, away, keep) = together(
            core(away_b),
            low_send(quad, grid.ring),
            send(out_send, grid.blocks),
            ffn_back(place, start, d_resid, slopes, w_out, w_in, norm, low_t, sums_two, True),
        )
        quad = add_up(add_up(keep_b[0], twin_b[0]), ring)
        twin, (gt_send, gt_keep), quad = together(
            core(away), mix_back(place, d_mix, d_one, *back_tables), quad
        )
        first, ring, output = together(
            low_send(add_up(keep[0], twin[0]), grid.across_1),
            low_send(quad, grid.ring),
            join(place, out_keep, out_other),
        )
        pair = add_up(add_up(keep[1], twin[1]), first)
        quad = add_up(add_up(keep_b[1], twin_b[1]), ring)
        second, ring, gt_0 = together(
            low_send(pair[:, 0], grid.across_0),
            low_send(quad, grid.ring),
            send(gt_send[:1], grid.blocks),
        )
        column = add_up(pair[:, 1], second)
        quad = add_up(add_up(keep_b[2], twin_b[2]), ring)
        gt_1 = send(gt_send[1:], grid.blocks)
        parts = [low_send(pick(column, ahead[step]), grid.shifts[step]) for step in range(1, 4)]
        slabs = [
            low_send(quad[i], perm)
            for i, perm in ((1, grid.blocks), (2, grid.across), (3, grid.corner))
        ]
        grad_tokens = join(place, gt_keep, gt_0, gt_1)
        my_w_out = quad[0]
        for slab in slabs:
            my_w_out = add_up(my_w_out, slab)
        my_w_in, *my_small = finish(pick(column, ahead[0]), parts, hidden, sizes, spots)
        my_small = [v.reshape(-1) for v in my_small]
    else:
        output = join_rows(out_keep, send(out_send, grid.blocks))
        grad_w_out = jnp.concatenate([dot_tn(act, d_low) for act in acts], axis=0)
        my_w_out = lax.psum_scatter(grad_w_out, AXES, scatter_dimension=0, tiled=True)
        d_mix, d_one, pre, bias_sum, norm_sum = ffn_back(
            place, d_low, d_resid, slopes, w_out, w_in, norm, low_t, sums_two, False
        )
        gt_send, gt_keep = mix_back(place, d_mix, d_one, *back_tables)
        grad_tokens = join_rows(gt_keep, send(gt_send, grid.blocks))
        my_w_in = lax.psum_scatter(dot(low_t, pre), AXES, scatter_dimension=0, tiled=True)
        strips = pack_small(bias_sum[0], norm_sum)
        my_strip = lax.psum_scatter(strips, AXES, scatter_dimension=0, tiled=True)[0, :2]
        my_small = [my_strip[line, at : at + size] for size, (line, at) in zip(sizes, spots)]
    return (
        output,
        grad_tokens,
        my_w_in,
        my_small[0],
        my_w_out,
        my_small[1],
        my_small[2],
        my_small[3],
        my_small[4],
        my_small[5],
    )


def solution(mesh):
    grid = Grid(mesh)
    cut, cut2 = P(AXES), P(AXES, None)
    block = P("dp", "seq", None)
    in_specs = (block, cut2, cut, cut2, cut, cut, cut, cut, cut, block)
    out_specs = (block, block, cut2, cut, cut2, cut, cut, cut, cut, cut)

    def program(*arrays):
        return per_device(grid, *arrays)

    return jax.shard_map(
        program, mesh=mesh, in_specs=in_specs, out_specs=out_specs, check_vma=False
    )
```

```python
import functools
import math

import jax
import jax.numpy as jnp
import numpy as np
from jax import lax
from jax.experimental import pallas as pl
from jax.experimental.pallas import tpu as pltpu
from jax.sharding import PartitionSpec as P

EPS = 1e-12
AXES = ("dp", "seq")
BF16 = jnp.bfloat16
F32 = jnp.float32
MIB = 1 << 20
LANES = 128
ERF_T = 0.3275911
ERF_P = (0.254829592, -0.284496736, 1.421413741, -1.453152027, 1.061405429)


def dft_tables(length):
    index = np.arange(length, dtype=np.int64)
    angle = (index[:, None] * index[None, :] % length).astype(np.float64) * (2.0 * math.pi / length)
    scale = length ** (-0.5)
    return np.cos(angle) * scale, np.sin(angle) * scale


def table(values):
    return jnp.asarray(values.astype(np.float32)).astype(BF16)


class Grid:
    def __init__(self, mesh):
        self.dp = mesh.shape["dp"]
        self.seq = mesh.shape["seq"]
        chips = self.dp // 2
        self.low = min(2, chips)
        self.high = chips // self.low
        self.shifts = [
            self.perm(lambda z, x, c, y: ((z + step) % self.high, x, c, y)) for step in range(4)
        ]
        self.ring = self.shifts[1]
        self.across = self.perm(lambda z, x, c, y: (z, (x + 1) % self.low, c, y))
        self.corner = self.perm(
            lambda z, x, c, y: (z, (x + 1) % self.low, c, (y + 1) % self.seq)
        )
        self.cores = self.perm(lambda z, x, c, y: (z, x, 1 - c, y))
        self.blocks = self.perm(lambda z, x, c, y: (z, x, c, (y + 1) % self.seq))
        self.across_0 = self.perm(
            lambda z, x, c, y: (z, (x + 1 - c) % self.low, c, (y + c) % self.seq)
        )
        self.across_1 = self.perm(
            lambda z, x, c, y: (z, (x + c) % self.low, c, (y + 1 - c) % self.seq)
        )
        self.chained = self.high == 4 and self.low == 2 and self.seq == 2

    def index(self, z, x, c, y):
        return ((z * self.low + x) * 2 + c) * self.seq + y

    def perm(self, move):
        return [
            (self.index(z, x, c, y), self.index(*move(z, x, c, y)))
            for z in range(self.high)
            for x in range(self.low)
            for c in range(2)
            for y in range(self.seq)
        ]

    def place(self):
        dp = lax.axis_index("dp")
        return dp // (2 * self.low), dp // 2 % self.low, dp % 2, lax.axis_index("seq")


def send(value, perm):
    return lax.ppermute(value, AXES, perm)


def pick(value, index):
    zero = jnp.uint32(0)
    starts = (index,) + (zero,) * (value.ndim - 1)
    return lax.dynamic_slice(value, starts, (1,) + value.shape[1:])[0]


def dot(a, b):
    return jnp.dot(a, b, preferred_element_type=F32)


def dot_nt(a, b):
    return lax.dot_general(a, b, (((1,), (1,)), ((), ())), preferred_element_type=F32)


def dot_tn(a, b):
    return lax.dot_general(a, b, (((0,), (0,)), ((), ())), preferred_element_type=F32)


def params(mib):
    return pltpu.CompilerParams(vmem_limit_bytes=mib * MIB)


def cost(flops, bytes_accessed, transcendentals=0):
    return pl.CostEstimate(
        flops=int(flops), bytes_accessed=int(bytes_accessed), transcendentals=int(transcendentals)
    )


def row_sum(values):
    return jnp.sum(values, axis=0, keepdims=True)


def after(value, *others):
    return lax.optimization_barrier((value,) + others)[0]


def together(*values):
    return lax.optimization_barrier(values)


def device_number(place, distance, flip_x, flip_y, other_core):
    z, x, c, y = place
    zz = lax.rem(z - distance + 4, 4)
    cc = 1 - c if other_core else c
    xx = x + flip_x - 2 * x * flip_x
    yy = y + flip_y - 2 * y * flip_y
    return ((zz * 2 + xx) * 2 + cc) * 2 + yy


def column_slab(part, index, core):
    group = part + index // 4
    flip_x, flip_y = ((0, 0), (1 - core, core), (core, 1 - core), (1, 1))[group]
    return index % 4, flip_x, flip_y


def pair_slab(part, index, core):
    return part // 2, index, part % 2


def put_slabs(place, refs, slab_of, put):
    for part, ref in enumerate(refs):
        own = len(refs) // 2
        for i in range(ref.shape[0]):
            core = 1 - place[2] if part >= own else place[2]
            where = slab_of(part % own, i, core)
            put(ref, i, device_number(place, *where, part >= own))


def vmem_call(kernel, name, out_shape, mib, work, scratch_shapes=(), places=0, anywhere=0, outside=False, aliases=None):
    def call(*operands):
        here = len(operands) - places - anywhere
        return pl.pallas_call(
            kernel,
            name=name,
            in_specs=[pl.BlockSpec(memory_space=pltpu.SMEM)] * places
            + [pl.BlockSpec(memory_space=pltpu.VMEM)] * here
            + [pl.BlockSpec(memory_space=pl.ANY)] * anywhere,
            out_specs=[pl.BlockSpec(memory_space=pl.ANY if outside else pltpu.VMEM)] * len(out_shape),
            out_shape=[jax.ShapeDtypeStruct(*each) for each in out_shape],
            scratch_shapes=list(scratch_shapes),
            input_output_aliases=aliases or {},
            compiler_params=params(mib),
            cost_estimate=work,
        )(*operands)

    return call


def tile_rows(index, size):
    return pl.ds(pl.multiple_of(index * size, size), size)


def assemble(place, groups, split):
    _, rows, columns = groups[0].shape
    slabs = sum(group.shape[0] for group in groups)
    return vmem_call(
        functools.partial(assemble_kernel, count=len(groups), split=split),
        "assemble_w_in",
        [((slabs * rows, split), BF16), ((slabs, rows, LANES), BF16)],
        2,
        cost(0, 4 * slabs * rows * columns),
        [pltpu.SemaphoreType.DMA((2 * slabs,))],
        places=1,
        anywhere=len(groups),
    )(place, *groups)


def spread_matrix(size, start, total):
    lane = lax.broadcasted_iota(jnp.int32, (LANES, total), 0)
    column = lax.broadcasted_iota(jnp.int32, (LANES, total), 1)
    return lane == start + lax.rem(column, size)


def owner_mask(owners, total):
    owner = lax.broadcasted_iota(jnp.int32, (owners, total), 0)
    column = lax.broadcasted_iota(jnp.int32, (owners, total), 1)
    return lax.div(column, total // owners) == owner


def first_weight_kernel(place_ref, xhat_ref, *refs, count, split):
    groups = refs[:count]
    full_ref, bias_ref, vec_ref, low_ref, low_t_ref, extra_ref = refs[count:]
    rows = groups[0].shape[1]
    place = tuple(place_ref[i] for i in range(4))

    def put(ref, i, at):
        full_ref[tile_rows(at, rows), :] = ref[i, :, :split]
        extra_ref[at] = ref[i, :, split:]

    put_slabs(place, groups, column_slab, put)
    owners, width = extra_ref.shape[0], vec_ref.shape[1]
    line = extra_ref[:, 0, :]
    wide = dot(line, spread_matrix(split // owners, 0, split).astype(BF16))
    bias_ref[...] = row_sum(jnp.where(owner_mask(owners, split), wide, 0.0))
    line = extra_ref[:, 1, :]
    mask = owner_mask(owners, width)
    size = width // owners
    vec_ref[...] = jnp.zeros_like(vec_ref)
    for i in range(5):
        wide = dot(line, spread_matrix(size, i * size, width).astype(BF16))
        vec_ref[i : i + 1, :] = row_sum(jnp.where(mask, wide, 0.0))
    low = (xhat_ref[...] * vec_ref[1:2, :] + vec_ref[2:3, :]).astype(BF16)
    low_ref[...] = low
    low_t_ref[...] = low.T


def first_weight(place, xhat, groups, split):
    _, rows, columns = groups[0].shape
    slabs = sum(group.shape[0] for group in groups)
    count, width = xhat.shape
    return vmem_call(
        functools.partial(first_weight_kernel, count=len(groups), split=split),
        "first_weight",
        [
            ((slabs * rows, split), BF16),
            ((1, split), F32),
            ((8, width), F32),
            ((count, width), BF16),
            ((width, count), BF16),
        ],
        10,
        cost(2 * count * width, 4 * slabs * rows * columns),
        [pltpu.VMEM((slabs, rows, LANES), BF16)],
        places=1,
    )(place, xhat, *groups)


def mix_kernel(place_ref, mine_ref, other_ref, seq_ref, hid_hbm, xhat_ref, rstd_ref, row_ref, hid_ref, sem):
    half, block, width = other_ref.shape
    length = 2 * block
    y = place_ref[3]
    copy = pltpu.make_async_copy(hid_hbm, hid_ref, sem)
    copy.start()

    def spectra(r, part):
        at = part * block
        tokens = row_ref[...]
        cos_part = dot(seq_ref[at : at + block, :], tokens).astype(BF16)
        return cos_part, dot(seq_ref[length + at : length + at + block, :], tokens).astype(BF16)

    for r in range(half):
        row_ref[tile_rows(y, block), :] = mine_ref[half * y + r]
        row_ref[tile_rows(1 - y, block), :] = other_ref[r]
        for part in range(2):
            cos_part, sin_part = spectra(r, part)
            if r == 0 and part == 0:
                copy.wait()
            mixed = dot(cos_part, hid_ref[:width, :]) + dot(sin_part, hid_ref[width:, :])
            resid = row_ref[part * block : (part + 1) * block, :].astype(F32) + mixed
            center = resid - jnp.mean(resid, axis=-1, keepdims=True)
            rstd = lax.rsqrt(jnp.mean(center * center, axis=-1, keepdims=True) + EPS)
            at = (2 * r + part) * block
            xhat_ref[at : at + block, :] = center * rstd
            rstd_ref[at : at + block, :] = rstd


def mix(place, tokens, other, seq_table, hid_table):
    half, block, width = other.shape
    length = 2 * block
    count = half * length
    return vmem_call(
        mix_kernel,
        "mix_norm",
        [((count, width), F32), ((count, 1), F32)],
        14,
        cost(4 * count * width * (length + width), 10 * count * width),
        [
            pltpu.VMEM((length, width), BF16),
            pltpu.VMEM((2 * width, width), BF16),
            pltpu.SemaphoreType.DMA(()),
        ],
        places=1,
        anywhere=1,
    )(place, tokens, other, seq_table, pltpu.with_memory_space_constraint(hid_table, pltpu.HBM))


def gelu_both(values):
    size = jnp.abs(values)
    t = 1.0 / (1.0 + (ERF_T / math.sqrt(2.0)) * size)
    bell = jnp.exp(-0.5 * (values * values))
    poly = 0.5 * ERF_P[4]
    for term in ERF_P[3::-1]:
        poly = 0.5 * term + t * poly
    tail = t * poly * bell
    phi = jnp.where(values > 0, 1.0 - tail, tail)
    return values * phi, phi + values * (bell * (1.0 / math.sqrt(2.0 * math.pi)))


def ffn_low_kernel(xhat_ref, vec_ref, low_ref, low_t_ref):
    low = (xhat_ref[...] * vec_ref[1:2, :] + vec_ref[2:3, :]).astype(BF16)
    low_ref[...] = low
    low_t_ref[...] = low.T


def ffn_low(xhat, vectors):
    count, width = xhat.shape
    return vmem_call(
        ffn_low_kernel,
        "normed_low",
        [((count, width), BF16), ((width, count), BF16)],
        8,
        cost(2 * count * width, 8 * count * width),
    )(xhat, vectors)


def ffn_in_tiles(low_ref, w_ref, bias_ref, act_ref, slope_ref, at, tile, columns):
    tiles = low_ref.shape[0] // tile

    def step(j, carry):
        rows = tile_rows(lax.rem(j, tiles), tile)
        part = j // tiles * columns
        cut = pl.ds(pl.multiple_of(part, LANES), columns)
        full = pl.ds(pl.multiple_of(at + part, LANES), columns)
        act, slope = gelu_both(dot(low_ref[rows, :], w_ref[:, full]) + bias_ref[:, full])
        act_ref[rows, cut] = act.astype(BF16)
        slope_ref[rows, cut] = slope.astype(BF16)
        return carry

    lax.fori_loop(0, tiles * (act_ref.shape[1] // columns), step, 0)


def ffn_in_kernel(low_ref, w_ref, bias_ref, act_ref, slope_ref, *, at, tile, columns):
    ffn_in_tiles(low_ref, w_ref, bias_ref, act_ref, slope_ref, at, tile, columns)


def ffn_in(low, w_in, bias, part, parts, columns=768, tile=512):
    count, width = low.shape
    hidden = w_in.shape[1] // parts
    return vmem_call(
        functools.partial(ffn_in_kernel, at=part * hidden, tile=tile, columns=columns),
        "ffn_in_gelu",
        [((count, hidden), BF16)] * 2,
        14,
        cost(2 * count * width * hidden, 4 * count * hidden, 2 * count * hidden),
    )(low, w_in, bias)


def hidden_block(refs, rows, block):
    width = refs[0].shape[1] // 2
    cut = pl.ds(pl.multiple_of(lax.rem(block, 2) * width, width), width)
    return jnp.where(block >= 2, refs[1][rows, cut], refs[0][rows, cut])


def place_pairs(place_ref, groups, w_ref, first):
    place = tuple(place_ref[i] for i in range(4))
    rows = groups[0].shape[1]

    def put(ref, i, at):
        w_ref[tile_rows(at, rows), :] = ref[i]

    put_slabs(place, groups, lambda part, index, core: pair_slab(part + first, index, core), put)


def ffn_in_last_kernel(place_ref, low_ref, w_in_ref, bias_ref, act_0_ref, *refs, count, at, tile, columns, step):
    groups, (act_1_ref, slope_ref, w_ref, branch_ref) = refs[:count], refs[count:]
    place_pairs(place_ref, groups, w_ref, 0)
    ffn_in_tiles(low_ref, w_in_ref, bias_ref, act_1_ref, slope_ref, at, tile, columns)
    size = w_ref.shape[0] // 4

    def multiply(i, carry):
        rows = tile_rows(i, step)
        total = None
        for distance in range(3):
            block = lax.rem(place_ref[0] + 4 - distance, 4)
            part = hidden_block((act_0_ref, act_1_ref), rows, block)
            part = dot(part, w_ref[tile_rows(block, size), :])
            total = part if total is None else total + part
        branch_ref[rows, :] = total
        return carry

    lax.fori_loop(0, branch_ref.shape[0] // step, multiply, 0)


def ffn_in_last(place, low, w_in, bias, act_0, groups, columns=768, tile=512, step=512):
    count, width = low.shape
    hidden = act_0.shape[1]
    return vmem_call(
        functools.partial(
            ffn_in_last_kernel, count=len(groups), at=hidden, tile=tile, columns=columns, step=step
        ),
        "ffn_in_out",
        [((count, hidden), BF16)] * 2 + [((2 * hidden, width), BF16), ((count, width), F32)],
        14,
        cost(5 * count * width * hidden, 8 * count * hidden, 2 * count * hidden),
        places=1,
    )(place, low, w_in, bias, act_0, *groups)


def ffn_out_kernel(place_ref, *refs, count):
    if count:
        act_0_ref, act_1_ref, _, *refs = refs
    branch_ref, xhat_ref, mine_ref, other_ref, vec_ref, *refs = refs
    groups, refs = refs[:count], refs[count:]
    if count:
        w_ref, *refs = refs
    send_ref, keep_ref, resid_ref, low_ref, sums_ref, part_ref = refs
    half, block, _ = other_ref.shape
    y = place_ref[3]
    if count:
        place_pairs(place_ref, groups, w_ref, 6)
    sums_ref[...] = jnp.zeros_like(sums_ref)
    gain_mix = vec_ref[1:2, :]
    shift_mix = vec_ref[2:3, :] + vec_ref[0:1, :]
    gain, shift = vec_ref[3:4, :], vec_ref[4:5, :]

    def rows_of(step):
        away, r = step < half, step % half
        return tile_rows(2 * r + (1 - y if away else y), block)

    def multiply(step):
        rows = rows_of(step)
        if not count:
            return branch_ref[rows, :]
        last = lax.rem(place_ref[0] + 1, 4)
        part = hidden_block((act_0_ref, act_1_ref), rows, last)
        return branch_ref[rows, :] + dot(part, w_ref[tile_rows(last, w_ref.shape[0] // 4), :])

    def finish(step, branch):
        away, r = step < half, step % half
        rows = rows_of(step)
        value = xhat_ref[rows, :] * gain_mix + (branch + shift_mix)
        center = value - jnp.mean(value, axis=-1, keepdims=True)
        rstd = lax.rsqrt(jnp.mean(center * center, axis=-1, keepdims=True) + EPS)
        xhat = center * rstd
        result = (xhat * gain + shift).astype(BF16)
        if away:
            send_ref[r] = result
            cot = other_ref[r].astype(F32)
        else:
            keep_ref[r] = result
            cot = mine_ref[half * y + r].astype(F32)
        d_xhat = cot * gain
        d_resid = rstd * (
            d_xhat
            - jnp.mean(d_xhat, axis=-1, keepdims=True)
            - xhat * jnp.mean(d_xhat * xhat, axis=-1, keepdims=True)
        )
        d_low = d_resid.astype(BF16)
        resid_ref[rows, :] = d_resid
        low_ref[rows, :] = d_low
        sums_ref[0:1, :] += row_sum(d_low.astype(F32))
        sums_ref[1:2, :] += row_sum(cot * xhat)
        sums_ref[2:3, :] += row_sum(cot)

    part_ref[0] = multiply(0)
    for step in range(2 * half):
        if step + 1 < 2 * half:
            part_ref[(step + 1) % 2] = multiply(step + 1)
        finish(step, part_ref[step % 2])


def ffn_out(place, branch, xhat, cotangent, cot_other, vectors, acts=(), w_out=None, groups=()):
    count, width = xhat.shape
    half, block, _ = cot_other.shape
    hidden = 2 * acts[0].shape[1] if groups else 0
    before = [*acts, w_out] if groups else []
    out_shape = [((hidden, width), BF16)] if groups else []
    out_shape += [
        ((half, block, width), BF16),
        ((half, block, width), BF16),
        ((count, width), F32),
        ((count, width), BF16),
        ((8, width), F32),
    ]
    return vmem_call(
        functools.partial(ffn_out_kernel, count=len(groups)),
        "ffn_out_norm",
        out_shape,
        10,
        cost(count * hidden * width // 2, 30 * count * width),
        [pltpu.VMEM((2, block, width), F32)],
        places=1,
        aliases={3: 0} if groups else None,
    )(place, *before, branch, xhat, cotangent, cot_other, vectors, *groups)


def slot(place_ref, xx, yy, core):
    same_x = jnp.where(place_ref[1] == xx, 1, 0)
    same_y = jnp.where(place_ref[3] == yy, 1, 0)
    return jnp.where(core == 0, same_y, same_x), jnp.where(core == 0, same_x, same_y)


def grad_out_kernel(place_ref, act_0_ref, act_1_ref, low_ref, _, send_ref, keep_ref, *, first):
    c = place_ref[2]
    rows = send_ref.shape[2]
    columns = 8 * rows

    def group(xx, yy):
        return jnp.where(place_ref[3] == yy, 0, 1) + jnp.where(place_ref[1] == xx, 0, 2)

    def step(j, carry):
        t, xx = j // 2, lax.rem(j, 2)
        block = lax.rem(place_ref[0] + 7 - first - t, 4)
        cut = pl.ds(pl.multiple_of(lax.rem(block, 2) * columns + xx * (columns // 2), LANES), columns // 2)
        act = jnp.where(block >= 2, act_1_ref[:, cut], act_0_ref[:, cut])
        total = dot_tn(act, low_ref[...])
        for yy in range(2):
            one = total[yy * rows : (yy + 1) * rows]
            two = total[(2 + yy) * rows : (3 + yy) * rows]
            send_ref[t, group(xx, yy)] = jnp.where(c == 0, two, one).astype(BF16)
            keep_ref[t, group(xx, yy)] = jnp.where(c == 0, one, two)
        return carry

    lax.fori_loop(0, 2 * send_ref.shape[0], step, 0)


def grad_out(place, acts, d_low, nearby, rows, first, steps):
    count, width = d_low.shape
    shape = (steps, 4, rows, width)
    return vmem_call(
        functools.partial(grad_out_kernel, first=first),
        "grad_w_out",
        [(shape, BF16), (shape, F32)],
        6,
        cost(16 * steps * count * rows * width, 16 * steps * count * rows),
        places=1,
    )(place, *acts, d_low, nearby)


def ffn_back_kernel(place_ref, low_ref, resid_ref, slope_0_ref, slope_1_ref, w_out_ref, w_in_ref, xhat_ref, rstd_ref, vec_ref, low_t_ref, two_ref, *refs, tile, columns):
    if len(refs) == 7:
        mix_ref, one_ref, send_ref, keep_ref, pre_ref, bias_ref, sums_ref = refs
    else:
        mix_ref, one_ref, pre_ref, bias_ref, sums_ref = refs
    hidden = pre_ref.shape[1]
    share = slope_0_ref.shape[1]
    bias_ref[...] = jnp.zeros_like(bias_ref)
    sums_ref[...] = jnp.zeros_like(sums_ref)

    def step(i, carry):
        rows = tile_rows(i, tile)
        d_low = low_ref[rows, :]
        d_normed = resid_ref[rows, :]
        for part in range(0, hidden, columns):
            cut = slice(part, part + columns)
            slope_ref = (slope_0_ref, slope_1_ref)[part // share]
            slope = slope_ref[rows, part % share : part % share + columns].astype(F32)
            d_pre = (dot_nt(d_low, w_out_ref[cut, :]) * slope).astype(BF16)
            pre_ref[rows, cut] = d_pre
            bias_ref[0:1, cut] += row_sum(d_pre.astype(F32))
            d_normed += dot_nt(d_pre, w_in_ref[:, cut])
        xhat = xhat_ref[rows, :]
        sums_ref[0:1, :] += row_sum(d_normed * xhat)
        sums_ref[1:2, :] += row_sum(d_normed)
        d_xhat = d_normed * vec_ref[1:2, :]
        d_one = rstd_ref[rows, :] * (
            d_xhat
            - jnp.mean(d_xhat, axis=-1, keepdims=True)
            - xhat * jnp.mean(d_xhat * xhat, axis=-1, keepdims=True)
        )
        one_ref[rows, :] = d_one
        mix_ref[rows, :] = d_one.astype(BF16)
        return carry

    lax.fori_loop(0, low_ref.shape[0] // tile, step, 0)
    if len(refs) == 7:
        grad_in_part(place_ref, low_t_ref, pre_ref, bias_ref, two_ref, sums_ref, send_ref, keep_ref)


def grad_in_part(place_ref, low_ref, pre_ref, bias_ref, two_ref, one_ref, send_ref, keep_ref):
    c = place_ref[2]
    split = pre_ref.shape[1]
    owners, width = 32, low_ref.shape[0]
    size = width // owners

    def gathered(values, first, part):
        total = values.shape[1]
        high = values.astype(BF16)
        rest = values - high.astype(F32)
        middle = rest.astype(BF16)
        lowest = (rest - middle.astype(F32)).astype(BF16)
        matrix = spread_matrix(part, first, total).astype(BF16)
        mask = owner_mask(total // part, total)
        return sum(dot_nt(jnp.where(mask, piece, 0.0).astype(BF16), matrix) for piece in (high, middle, lowest))

    line_0 = gathered(bias_ref[0:1, :], 0, 4 * size)
    line_1 = jnp.zeros((owners, LANES), F32)
    for i, (ref, row) in enumerate(
        ((two_ref, 0), (one_ref, 0), (one_ref, 1), (two_ref, 1), (two_ref, 2))
    ):
        line_1 += gathered(ref[row : row + 1, :], i * size, size)
    send_ref[:, :, :, :, split:] = jnp.zeros(send_ref.shape[:4] + (LANES,), BF16)
    keep_ref[:, :, :, :, split:] = jnp.zeros(keep_ref.shape[:4] + (LANES,), F32)
    rows = send_ref.shape[3]
    columns = split // 2
    for z in range(4):
        for cut in (slice(0, columns), slice(columns, split)):
            total = dot(low_ref[8 * z * rows : 8 * (z + 1) * rows, :], pre_ref[:, cut])
            for xx in range(2):
                for yy in range(2):
                    at = (4 * xx + yy) * rows
                    first, second = total[at : at + rows], total[at + 2 * rows : at + 3 * rows]
                    away, stay = slot(place_ref, xx, yy, 1 - c), slot(place_ref, xx, yy, c)
                    send_ref[away[0], z, away[1], :, cut] = jnp.where(c == 0, second, first).astype(BF16)
                    keep_ref[stay[0], z, stay[1], :, cut] = jnp.where(c == 0, first, second)
        for xx in range(2):
            for yy in range(2):
                at = 8 * z + 4 * xx + yy
                away, stay = slot(place_ref, xx, yy, 1 - c), slot(place_ref, xx, yy, c)
                for row, line in enumerate((line_0, line_1)):
                    first, second = line[at : at + 1], line[at + 2 : at + 3]
                    side = jnp.where(c == 0, second, first)
                    send_ref[away[0], z, away[1], row : row + 1, split:] = side.astype(BF16)
                    side = jnp.where(c == 0, first, second)
                    keep_ref[stay[0], z, stay[1], row : row + 1, split:] = side


def ffn_back(place, d_low, d_resid, slopes, w_out, w_in, norm, low_t, sums_two, chained, tile=512, columns=768):
    count, width = d_low.shape
    hidden = 2 * slopes[0].shape[1]
    out_shape = [((count, width), BF16), ((count, width), F32)]
    backs = [((count, hidden), BF16), ((8, hidden), F32), ((8, width), F32)]
    scratch_shapes = []
    if chained:
        shape = (2, 4, 2, width // 32, hidden + LANES)
        out_shape += [(shape, BF16), (shape, F32)]
        scratch_shapes = [pltpu.VMEM(*each) for each in backs]
    else:
        out_shape += backs
    return vmem_call(
        functools.partial(ffn_back_kernel, tile=tile, columns=columns),
        "ffn_back",
        out_shape,
        12 if chained else 10,
        cost(6 * count * hidden * width, 6 * count * hidden + 4 * hidden * width),
        scratch_shapes,
        places=1,
    )(place, d_low, d_resid, *slopes, w_out, w_in, *norm, low_t, sums_two)


def mix_back_kernel(place_ref, low_ref, one_ref, hid_ref, seq_ref, send_ref, keep_ref, spec_ref):
    width = low_ref.shape[1]
    length = seq_ref.shape[0]
    block = length // 2
    y = place_ref[3]

    def step(r, carry):
        for part in range(2):
            cut = slice(part * width, (part + 1) * width)
            spec = dot(low_ref[tile_rows(r, length), :], hid_ref[:, cut])
            spec_ref[part * length : (part + 1) * length, :] = spec.astype(BF16)
        for spot, away in ((1 - y, True), (y, False)):
            total = dot(seq_ref[tile_rows(spot, block), :], spec_ref[...])
            total += one_ref[tile_rows(2 * r + spot, block), :]
            if away:
                send_ref[r] = total.astype(BF16)
            else:
                keep_ref[r] = total
        return carry

    lax.fori_loop(0, low_ref.shape[0] // length, step, 0)


def mix_back(place, d_low, d_one, hid_table, seq_table):
    count, width = d_low.shape
    length = seq_table.shape[0]
    half, block = count // length, length // 2
    return vmem_call(
        mix_back_kernel,
        "mix_back",
        [((half, block, width), BF16), ((half, block, width), F32)],
        14,
        cost(4 * count * width * (length + width), 10 * count * width),
        [pltpu.VMEM((2 * length, width), BF16)],
        places=1,
    )(place, d_low, d_one, hid_table, seq_table)


def join_kernel(place_ref, keep_ref, *refs):
    *others, out_ref, wide_ref, sem = refs
    y = place_ref[3]
    half = keep_ref.shape[0]
    copies = [pltpu.make_async_copy(keep_ref, out_ref.at[pl.ds(half * y, half)], sem.at[0])]
    copies[0].start()
    at = half * (1 - y)
    for i, ref in enumerate(others):
        rows = ref.shape[0]
        if ref.dtype == keep_ref.dtype:
            source = ref
        else:
            source = wide_ref.at[pl.ds(i * rows, rows)]
            wide_ref[i * rows : (i + 1) * rows] = ref[...].astype(wide_ref.dtype)
        copies.append(
            pltpu.make_async_copy(source, out_ref.at[pl.ds(at + i * rows, rows)], sem.at[i + 1])
        )
        copies[-1].start()
    for copy in copies:
        copy.wait()


def join(place, keep, *others):
    half, block, width = keep.shape
    wide = keep.shape if others[0].dtype != keep.dtype else (1, 8, LANES)
    return vmem_call(
        join_kernel,
        "join_rows",
        [((2 * half, block, width), keep.dtype)],
        4,
        cost(0, 16 * half * block * width),
        [pltpu.VMEM(wide, keep.dtype), pltpu.SemaphoreType.DMA((1 + len(others),))],
        places=1,
        outside=True,
    )(place, keep, *others)[0]


def finish_kernel(own_ref, *refs, spots):
    parts, (w_ref, *smalls) = refs[:3], refs[3:]
    split = w_ref.shape[1]
    total = own_ref[...]
    for ref in parts:
        total += ref[...].astype(F32)
    w_ref[...] = total[:, :split]
    for ref, (line, at) in zip(smalls, spots):
        ref[...] = total[line : line + 1, split + at : split + at + ref.shape[1]]


def finish(own, parts, split, sizes, spots):
    rows, _ = own.shape
    return vmem_call(
        functools.partial(finish_kernel, spots=spots),
        "finish_w_in",
        [((rows, split), F32)] + [((1, size), F32) for size in sizes],
        4,
        cost(3 * rows * split, 14 * rows * split),
    )(own, *parts)


def add_up(keep, other):
    return keep + other.astype(F32)


def per_device(grid, tokens, weight_in, bias_in, weight_out, bias_out, gain_mix, shift_mix, gain_ffn, shift_ffn, cotangent):
    rows, block, width = tokens.shape
    part_in, hidden = weight_in.shape
    part_out = weight_out.shape[0]
    half = rows // 2
    length = 2 * block
    devices = grid.dp * grid.seq
    z, x, c, y = grid.place()
    place = jnp.stack([z, x, c, y]).astype(jnp.int32)
    zero = jnp.uint32(0)
    across = ((1 - y) * half).astype(jnp.uint32)
    ahead = [((z + step) % 4).astype(jnp.uint32) for step in range(4)]
    place, across, ahead, weight_in = together(place, across, ahead, weight_in)
    chained = grid.chained and part_in % 8 == 0

    def other_rows(value):
        return lax.dynamic_slice(value, (across, zero, zero), (half,) + value.shape[1:])

    def join_rows(keep, other):
        other = other.astype(keep.dtype)
        return jnp.where(
            y == 0, jnp.concatenate([keep, other], 0), jnp.concatenate([other, keep], 0)
        )

    def core(value):
        return send(value, grid.cores)

    smalls = (bias_in, bias_out, gain_mix, shift_mix, gain_ffn, shift_ffn)
    sizes = [v.shape[0] for v in smalls]
    spots = [(0, 0)] + [(1, i * sizes[1]) for i in range(5)]
    lines = [0, 0]
    for value, (line, at) in zip(smalls, spots):
        lines[line] += jnp.pad(value, (at, LANES - at - value.shape[0]))
    strip = jnp.pad(jnp.stack(lines), ((0, part_in - 2), (0, 0)))
    tok_other = send(other_rows(tokens), grid.blocks)

    cos_seq, sin_seq = dft_tables(length)
    cos_hid, sin_hid = dft_tables(width)
    mix_tables = (
        table(np.concatenate([cos_seq, sin_seq], 0)),
        table(np.concatenate([cos_hid, -sin_hid], 0)),
    )
    if chained:
        packed = jnp.concatenate([weight_in, strip], axis=1)
        packed, shard_out = together(packed, weight_out)
        *pieces, near_out, tok_other = together(
            *(send(packed, grid.shifts[step]) for step in range(1, 4)),
            send(shard_out, grid.across),
            tok_other,
        )
        pair = jnp.stack([shard_out, near_out])
        column = jnp.stack([packed] + pieces)
        column, pair, tok_other = together(column, pair, tok_other)
        near, ring_pair, far_pair, (xhat, rstd) = together(
            send(column, grid.across_0),
            send(pair, grid.ring),
            send(pair, grid.blocks),
            mix(place, tokens, tok_other, *mix_tables),
        )
        pairs = [pair, far_pair]
        both = jnp.concatenate([column, near], axis=0)
        both, ring_pair, far_pair = together(both, ring_pair, far_pair)
        pairs.append(ring_pair)
        groups = [column, near, send(both, grid.across_1)]
        twins = [core(column), core(near)]
        groups[2], twins, ring_far, ring_pair_2 = together(
            groups[2], twins, send(far_pair, grid.ring), send(ring_pair, grid.ring)
        )
        ring_far_2, ring_pair_3 = send(ring_far, grid.ring), send(ring_pair_2, grid.ring)
        cot_other = send(after(other_rows(cotangent), groups[2]), grid.blocks)
        w_in, bias, vectors, low, low_t = first_weight(
            place, xhat, groups + twins + [core(groups[2])], hidden
        )
    else:
        cot_other = send(other_rows(cotangent), grid.blocks)
        xhat, rstd = mix(place, tokens, tok_other, *mix_tables)
        w_in = lax.all_gather(weight_in, AXES, axis=0, tiled=True)
        w_out = lax.all_gather(weight_out, AXES, axis=0, tiled=True)
        extra = lax.all_gather(strip, AXES, axis=0)[:, :2]
        bias, *vectors = [
            extra[:, line, at : at + size].reshape(1, -1).astype(F32)
            for size, (line, at) in zip(sizes, spots)
        ]
        vectors = jnp.concatenate(vectors + [jnp.zeros((3, width), F32)], axis=0)
        low, low_t = ffn_low(xhat, vectors)
    act_0, slope_0 = ffn_in(low, w_in, bias, 0, 2)
    if chained:
        act_0, slope_0, low, ring_far_2, ring_pair_3 = together(
            act_0, slope_0, low, ring_far_2, ring_pair_3
        )
        ring_far_3 = send(ring_far_2, grid.ring)
    if chained:
        pairs = [pair, far_pair, ring_pair, ring_far, ring_pair_2, ring_far_2]
        pairs += [core(p) for p in pairs]
        act_1, slope_1, w_out, branch = ffn_in_last(place, low, w_in, bias, act_0, pairs)
        ring_far_3, cot_other, branch = together(ring_far_3, cot_other, branch)
    else:
        act_1, slope_1 = ffn_in(low, w_in, bias, 1, 2)
    acts, slopes = [act_0, act_1], [slope_0, slope_1]
    if chained:
        last = [ring_pair_3, ring_far_3]
        w_out, out_send, out_keep, d_resid, d_low, sums_two = ffn_out(
            place, branch, xhat, cotangent, cot_other, vectors, acts, w_out, last + [core(p) for p in last]
        )
    else:
        branch = dot(act_0, w_out[: hidden // 2]) + dot(act_1, w_out[hidden // 2 :])
        out_send, out_keep, d_resid, d_low, sums_two = ffn_out(
            place, branch, xhat, cotangent, cot_other, vectors
        )

    norm = (xhat, rstd, vectors)
    back_tables = (
        table(np.concatenate([cos_hid, -sin_hid], 1)),
        table(np.concatenate([cos_seq, sin_seq], 1)),
    )

    def pack_small(bias_sum, norm_sum):
        grads = (bias_sum, sums_two[0], norm_sum[0], norm_sum[1], sums_two[1], sums_two[2])
        lines = [0, 0]
        for value, (line, at) in zip(grads, spots):
            value = value.reshape(devices, -1)
            lines[line] += jnp.pad(value, ((0, 0), (at, LANES - at - value.shape[1])))
        return jnp.pad(jnp.stack(lines, axis=1), ((0, 0), (0, part_in - 2), (0, 0)))

    def low_send(value, perm):
        return send(value.astype(BF16), perm)

    if chained:
        (away_a, keep_a), start = together(grad_out(place, acts, d_low, w_out, part_out, 0, 1), d_low)
        twin_a, (away_b, keep_b) = together(core(away_a), grad_out(place, acts, start, w_out, part_out, 1, 3))
        quad = add_up(keep_a[0], twin_a[0])
        start, away_b, quad, out_send = together(start, away_b, quad, out_send)
        twin_b, ring, out_other, (d_mix, d_one, away, keep) = together(
            core(away_b),
            low_send(quad, grid.ring),
            send(out_send, grid.blocks),
            ffn_back(place, start, d_resid, slopes, w_out, w_in, norm, low_t, sums_two, True),
        )
        quad = add_up(add_up(keep_b[0], twin_b[0]), ring)
        twin, (gt_send, gt_keep), quad = together(
            core(away), mix_back(place, d_mix, d_one, *back_tables), quad
        )
        first, ring, output = together(
            low_send(add_up(keep[0], twin[0]), grid.across_1),
            low_send(quad, grid.ring),
            join(place, out_keep, out_other),
        )
        pair = add_up(add_up(keep[1], twin[1]), first)
        quad = add_up(add_up(keep_b[1], twin_b[1]), ring)
        second, ring, gt_0 = together(
            low_send(pair[:, 0], grid.across_0),
            low_send(quad, grid.ring),
            send(gt_send[:1], grid.blocks),
        )
        column = add_up(pair[:, 1], second)
        quad = add_up(add_up(keep_b[2], twin_b[2]), ring)
        gt_1 = send(after(gt_send[1:], quad), grid.blocks)
        parts, far = together(
            [low_send(pick(column, ahead[step]), grid.shifts[step]) for step in range(1, 4)],
            low_send(quad[2:], grid.across),
        )
        quad = add_up(quad[:2], far)
        passed, gt_1 = together(quad[1].astype(BF16), gt_1)
        my_w_out = add_up(quad[0], send(passed, grid.blocks))
        grad_tokens = join(place, gt_keep, gt_0, gt_1)
        my_w_in, *my_small = finish(pick(column, ahead[0]), parts, hidden, sizes, spots)
        my_small = [v.reshape(-1) for v in my_small]
    else:
        output = join_rows(out_keep, send(out_send, grid.blocks))
        grad_w_out = jnp.concatenate([dot_tn(act, d_low) for act in acts], axis=0)
        my_w_out = lax.psum_scatter(grad_w_out, AXES, scatter_dimension=0, tiled=True)
        d_mix, d_one, pre, bias_sum, norm_sum = ffn_back(
            place, d_low, d_resid, slopes, w_out, w_in, norm, low_t, sums_two, False
        )
        gt_send, gt_keep = mix_back(place, d_mix, d_one, *back_tables)
        grad_tokens = join_rows(gt_keep, send(gt_send, grid.blocks))
        my_w_in = lax.psum_scatter(dot(low_t, pre), AXES, scatter_dimension=0, tiled=True)
        strips = pack_small(bias_sum[0], norm_sum)
        my_strip = lax.psum_scatter(strips, AXES, scatter_dimension=0, tiled=True)[0, :2]
        my_small = [my_strip[line, at : at + size] for size, (line, at) in zip(sizes, spots)]
    return (
        output,
        grad_tokens,
        my_w_in,
        my_small[0],
        my_w_out,
        my_small[1],
        my_small[2],
        my_small[3],
        my_small[4],
        my_small[5],
    )


def solution(mesh):
    grid = Grid(mesh)
    cut, cut2 = P(AXES), P(AXES, None)
    block = P("dp", "seq", None)
    in_specs = (block, cut2, cut, cut2, cut, cut, cut, cut, cut, block)
    out_specs = (block, block, cut2, cut, cut2, cut, cut, cut, cut, cut)

    def program(*arrays):
        return per_device(grid, *arrays)

    return jax.shard_map(
        program, mesh=mesh, in_specs=in_specs, out_specs=out_specs, check_vma=False
    )
```

```python
import functools
import math

import jax
import jax.numpy as jnp
import numpy as np
from jax import lax
from jax.experimental import pallas as pl
from jax.experimental.pallas import tpu as pltpu
from jax.sharding import PartitionSpec as P

EPS = 1e-12
AXES = ("dp", "seq")
BF16 = jnp.bfloat16
F32 = jnp.float32
MIB = 1 << 20
LANES = 128
ERF_T = 0.3275911
ERF_P = (0.254829592, -0.284496736, 1.421413741, -1.453152027, 1.061405429)


def dft_tables(length):
    index = np.arange(length, dtype=np.int64)
    angle = (index[:, None] * index[None, :] % length).astype(np.float64) * (2.0 * math.pi / length)
    scale = length ** (-0.5)
    return np.cos(angle) * scale, np.sin(angle) * scale


def table(values):
    return jnp.asarray(values.astype(np.float32)).astype(BF16)


class Grid:
    def __init__(self, mesh):
        self.dp = mesh.shape["dp"]
        self.seq = mesh.shape["seq"]
        chips = self.dp // 2
        self.low = min(2, chips)
        self.high = chips // self.low
        self.shifts = [
            self.perm(lambda z, x, c, y: ((z + step) % self.high, x, c, y)) for step in range(4)
        ]
        self.ring = self.shifts[1]
        self.across = self.perm(lambda z, x, c, y: (z, (x + 1) % self.low, c, y))
        self.corner = self.perm(
            lambda z, x, c, y: (z, (x + 1) % self.low, c, (y + 1) % self.seq)
        )
        self.cores = self.perm(lambda z, x, c, y: (z, x, 1 - c, y))
        self.blocks = self.perm(lambda z, x, c, y: (z, x, c, (y + 1) % self.seq))
        self.across_0 = self.perm(
            lambda z, x, c, y: (z, (x + 1 - c) % self.low, c, (y + c) % self.seq)
        )
        self.across_1 = self.perm(
            lambda z, x, c, y: (z, (x + c) % self.low, c, (y + 1 - c) % self.seq)
        )
        self.chained = self.high == 4 and self.low == 2 and self.seq == 2

    def index(self, z, x, c, y):
        return ((z * self.low + x) * 2 + c) * self.seq + y

    def perm(self, move):
        return [
            (self.index(z, x, c, y), self.index(*move(z, x, c, y)))
            for z in range(self.high)
            for x in range(self.low)
            for c in range(2)
            for y in range(self.seq)
        ]

    def place(self):
        dp = lax.axis_index("dp")
        return dp // (2 * self.low), dp // 2 % self.low, dp % 2, lax.axis_index("seq")


def send(value, perm):
    return lax.ppermute(value, AXES, perm)


def pick(value, index):
    zero = jnp.uint32(0)
    starts = (index,) + (zero,) * (value.ndim - 1)
    return lax.dynamic_slice(value, starts, (1,) + value.shape[1:])[0]


def dot(a, b):
    return jnp.dot(a, b, preferred_element_type=F32)


def dot_nt(a, b):
    return lax.dot_general(a, b, (((1,), (1,)), ((), ())), preferred_element_type=F32)


def dot_tn(a, b):
    return lax.dot_general(a, b, (((0,), (0,)), ((), ())), preferred_element_type=F32)


def params(mib):
    return pltpu.CompilerParams(vmem_limit_bytes=mib * MIB)


def cost(flops, bytes_accessed, transcendentals=0):
    return pl.CostEstimate(
        flops=int(flops), bytes_accessed=int(bytes_accessed), transcendentals=int(transcendentals)
    )


def row_sum(values):
    return jnp.sum(values, axis=0, keepdims=True)


def after(value, *others):
    return lax.optimization_barrier((value,) + others)[0]


def together(*values):
    return lax.optimization_barrier(values)


def device_number(place, distance, flip_x, flip_y, other_core):
    z, x, c, y = place
    zz = lax.rem(z - distance + 4, 4)
    cc = 1 - c if other_core else c
    xx = x + flip_x - 2 * x * flip_x
    yy = y + flip_y - 2 * y * flip_y
    return ((zz * 2 + xx) * 2 + cc) * 2 + yy


def column_slab(part, index, core):
    group = part + index // 4
    flip_x, flip_y = ((0, 0), (1 - core, core), (core, 1 - core), (1, 1))[group]
    return index % 4, flip_x, flip_y


def ring_slab(position):
    return position // 4, position % 2, position % 4 // 2


def put_slabs(place, refs, slab_of, put):
    own = len(refs) // 2
    for part, ref in enumerate(refs):
        core = 1 - place[2] if part >= own else place[2]
        for i in range(ref.shape[0]):
            where = slab_of(part % own, i, core)
            put(ref, i, device_number(place, *where, part >= own))


def vmem_call(kernel, name, out_shape, mib, work, scratch_shapes=(), places=0, anywhere=0, outside=False, aliases=None):
    def call(*operands):
        here = len(operands) - places - anywhere
        return pl.pallas_call(
            kernel,
            name=name,
            in_specs=[pl.BlockSpec(memory_space=pltpu.SMEM)] * places
            + [pl.BlockSpec(memory_space=pltpu.VMEM)] * here
            + [pl.BlockSpec(memory_space=pl.ANY)] * anywhere,
            out_specs=[pl.BlockSpec(memory_space=pl.ANY if outside else pltpu.VMEM)] * len(out_shape),
            out_shape=[jax.ShapeDtypeStruct(*each) for each in out_shape],
            scratch_shapes=list(scratch_shapes),
            input_output_aliases=aliases or {},
            compiler_params=params(mib),
            cost_estimate=work,
        )(*operands)

    return call


def tile_rows(index, size):
    return pl.ds(pl.multiple_of(index * size, size), size)


def assemble(place, groups, split):
    _, rows, columns = groups[0].shape
    slabs = sum(group.shape[0] for group in groups)
    return vmem_call(
        functools.partial(assemble_kernel, count=len(groups), split=split),
        "assemble_w_in",
        [((slabs * rows, split), BF16), ((slabs, rows, LANES), BF16)],
        2,
        cost(0, 4 * slabs * rows * columns),
        [pltpu.SemaphoreType.DMA((2 * slabs,))],
        places=1,
        anywhere=len(groups),
    )(place, *groups)


def spread_matrix(size, start, total):
    lane = lax.broadcasted_iota(jnp.int32, (LANES, total), 0)
    column = lax.broadcasted_iota(jnp.int32, (LANES, total), 1)
    return lane == start + lax.rem(column, size)


def owner_mask(owners, total):
    owner = lax.broadcasted_iota(jnp.int32, (owners, total), 0)
    column = lax.broadcasted_iota(jnp.int32, (owners, total), 1)
    return lax.div(column, total // owners) == owner


def first_weight_kernel(place_ref, xhat_ref, *refs, count, split):
    groups = refs[:count]
    full_ref, bias_ref, vec_ref, low_ref, low_t_ref, extra_ref = refs[count:]
    rows = groups[0].shape[1]
    place = tuple(place_ref[i] for i in range(4))

    def put(ref, i, at):
        full_ref[tile_rows(at, rows), :] = ref[i, :, :split]
        extra_ref[at] = ref[i, :, split:]

    put_slabs(place, groups, column_slab, put)
    owners, width = extra_ref.shape[0], vec_ref.shape[1]
    line = extra_ref[:, 0, :]
    wide = dot(line, spread_matrix(split // owners, 0, split).astype(BF16))
    bias_ref[...] = row_sum(jnp.where(owner_mask(owners, split), wide, 0.0))
    line = extra_ref[:, 1, :]
    mask = owner_mask(owners, width)
    size = width // owners
    vec_ref[...] = jnp.zeros_like(vec_ref)
    for i in range(5):
        wide = dot(line, spread_matrix(size, i * size, width).astype(BF16))
        vec_ref[i : i + 1, :] = row_sum(jnp.where(mask, wide, 0.0))
    low = (xhat_ref[...] * vec_ref[1:2, :] + vec_ref[2:3, :]).astype(BF16)
    low_ref[...] = low
    low_t_ref[...] = low.T


def first_weight(place, xhat, groups, split):
    _, rows, columns = groups[0].shape
    slabs = sum(group.shape[0] for group in groups)
    count, width = xhat.shape
    return vmem_call(
        functools.partial(first_weight_kernel, count=len(groups), split=split),
        "first_weight",
        [
            ((slabs * rows, split), BF16),
            ((1, split), F32),
            ((8, width), F32),
            ((count, width), BF16),
            ((width, count), BF16),
        ],
        10,
        cost(2 * count * width, 4 * slabs * rows * columns),
        [pltpu.VMEM((slabs, rows, LANES), BF16)],
        places=1,
    )(place, xhat, *groups)


def mix_kernel(place_ref, mine_ref, other_ref, seq_ref, hid_hbm, xhat_ref, rstd_ref, row_ref, hid_ref, sem):
    half, block, width = other_ref.shape
    length = 2 * block
    y = place_ref[3]
    copy = pltpu.make_async_copy(hid_hbm, hid_ref, sem)
    copy.start()

    def spectra(r, part):
        at = part * block
        tokens = row_ref[...]
        cos_part = dot(seq_ref[at : at + block, :], tokens).astype(BF16)
        return cos_part, dot(seq_ref[length + at : length + at + block, :], tokens).astype(BF16)

    for r in range(half):
        row_ref[tile_rows(y, block), :] = mine_ref[half * y + r]
        row_ref[tile_rows(1 - y, block), :] = other_ref[r]
        for part in range(2):
            cos_part, sin_part = spectra(r, part)
            if r == 0 and part == 0:
                copy.wait()
            mixed = dot(cos_part, hid_ref[:width, :]) + dot(sin_part, hid_ref[width:, :])
            resid = row_ref[part * block : (part + 1) * block, :].astype(F32) + mixed
            center = resid - jnp.mean(resid, axis=-1, keepdims=True)
            rstd = lax.rsqrt(jnp.mean(center * center, axis=-1, keepdims=True) + EPS)
            at = (2 * r + part) * block
            xhat_ref[at : at + block, :] = center * rstd
            rstd_ref[at : at + block, :] = rstd


def mix(place, tokens, other, seq_table, hid_table):
    half, block, width = other.shape
    length = 2 * block
    count = half * length
    return vmem_call(
        mix_kernel,
        "mix_norm",
        [((count, width), F32), ((count, 1), F32)],
        14,
        cost(4 * count * width * (length + width), 10 * count * width),
        [
            pltpu.VMEM((length, width), BF16),
            pltpu.VMEM((2 * width, width), BF16),
            pltpu.SemaphoreType.DMA(()),
        ],
        places=1,
        anywhere=1,
    )(place, tokens, other, seq_table, pltpu.with_memory_space_constraint(hid_table, pltpu.HBM))


def gelu_both(values):
    size = jnp.abs(values)
    t = 1.0 / (1.0 + (ERF_T / math.sqrt(2.0)) * size)
    bell = jnp.exp2((values * values) * (-0.5 * math.log2(math.e)))
    poly = 0.5 * ERF_P[4]
    for term in ERF_P[3::-1]:
        poly = 0.5 * term + t * poly
    tail = t * poly * bell
    phi = jnp.where(values > 0, 1.0 - tail, tail)
    return values * phi, phi + values * (bell * (1.0 / math.sqrt(2.0 * math.pi)))


def ffn_low_kernel(xhat_ref, vec_ref, low_ref, low_t_ref):
    low = (xhat_ref[...] * vec_ref[1:2, :] + vec_ref[2:3, :]).astype(BF16)
    low_ref[...] = low
    low_t_ref[...] = low.T


def ffn_low(xhat, vectors):
    count, width = xhat.shape
    return vmem_call(
        ffn_low_kernel,
        "normed_low",
        [((count, width), BF16), ((width, count), BF16)],
        8,
        cost(2 * count * width, 8 * count * width),
    )(xhat, vectors)


def ffn_in_tiles(low_ref, w_ref, bias_ref, act_ref, slope_ref, at, tile, columns):
    tiles = low_ref.shape[0] // tile

    def step(j, carry):
        rows = tile_rows(lax.rem(j, tiles), tile)
        part = j // tiles * columns
        cut = pl.ds(pl.multiple_of(part, LANES), columns)
        full = pl.ds(pl.multiple_of(at + part, LANES), columns)
        act, slope = gelu_both(dot(low_ref[rows, :], w_ref[:, full]) + bias_ref[:, full])
        act_ref[rows, cut] = act.astype(BF16)
        slope_ref[rows, cut] = slope.astype(BF16)
        return carry

    lax.fori_loop(0, tiles * (act_ref.shape[1] // columns), step, 0)


def ffn_in_kernel(low_ref, w_ref, bias_ref, act_ref, slope_ref, *, at, tile, columns):
    ffn_in_tiles(low_ref, w_ref, bias_ref, act_ref, slope_ref, at, tile, columns)


def ffn_in(low, w_in, bias, part, parts, columns=768, tile=512):
    count, width = low.shape
    hidden = w_in.shape[1] // parts
    return vmem_call(
        functools.partial(ffn_in_kernel, at=part * hidden, tile=tile, columns=columns),
        "ffn_in_gelu",
        [((count, hidden), BF16)] * 2,
        8,
        cost(2 * count * width * hidden, 4 * count * hidden, 2 * count * hidden),
    )(low, w_in, bias)


def hidden_block(refs, rows, block):
    width = refs[0].shape[1] // 2
    cut = pl.ds(pl.multiple_of(lax.rem(block, 2) * width, width), width)
    return jnp.where(block >= 2, refs[1][rows, cut], refs[0][rows, cut])


def place_rows(place_ref, groups, w_ref, first):
    place = tuple(place_ref[i] for i in range(4))
    rows = groups[0].shape[1]
    starts = [first]
    for group in groups[: len(groups) // 2]:
        starts.append(starts[-1] + group.shape[0])

    def put(ref, i, at):
        w_ref[tile_rows(at, rows), :] = ref[i]

    put_slabs(place, groups, lambda part, index, core: ring_slab(starts[part] + index), put)


def ffn_in_last_kernel(place_ref, low_ref, w_in_ref, bias_ref, act_0_ref, *refs, count, at, tile, columns, step):
    groups, (act_1_ref, slope_ref, w_ref, branch_ref) = refs[:count], refs[count:]
    place_rows(place_ref, groups, w_ref, 0)
    ffn_in_tiles(low_ref, w_in_ref, bias_ref, act_1_ref, slope_ref, at, tile, columns)
    size = w_ref.shape[0] // 4

    def multiply(i, carry):
        rows = tile_rows(i, step)
        total = None
        for distance in range(3):
            block = lax.rem(place_ref[0] + 4 - distance, 4)
            part = hidden_block((act_0_ref, act_1_ref), rows, block)
            part = dot(part, w_ref[tile_rows(block, size), :])
            total = part if total is None else total + part
        branch_ref[rows, :] = total
        return carry

    lax.fori_loop(0, branch_ref.shape[0] // step, multiply, 0)


def ffn_in_last(place, low, w_in, bias, act_0, groups, columns=768, tile=512, step=512):
    count, width = low.shape
    hidden = act_0.shape[1]
    return vmem_call(
        functools.partial(
            ffn_in_last_kernel, count=len(groups), at=hidden, tile=tile, columns=columns, step=step
        ),
        "ffn_in_out",
        [((count, hidden), BF16)] * 2 + [((2 * hidden, width), BF16), ((count, width), F32)],
        8,
        cost(5 * count * width * hidden, 8 * count * hidden, 2 * count * hidden),
        places=1,
    )(place, low, w_in, bias, act_0, *groups)


def ffn_out_kernel(place_ref, *refs, count):
    if count:
        act_0_ref, act_1_ref, _, *refs = refs
    branch_ref, xhat_ref, mine_ref, other_0_ref, other_1_ref, vec_ref, *refs = refs
    groups, refs = refs[:count], refs[count:]
    if count:
        w_ref, *refs = refs
    send_ref, keep_ref, resid_ref, low_ref, sums_ref, part_ref = refs
    half, block = 2, other_0_ref.shape[1]
    y = place_ref[3]
    if count:
        place_rows(place_ref, groups, w_ref, 14)
    sums_ref[...] = jnp.zeros_like(sums_ref)
    gain_mix = vec_ref[1:2, :]
    shift_mix = vec_ref[2:3, :] + vec_ref[0:1, :]
    gain, shift = vec_ref[3:4, :], vec_ref[4:5, :]

    def rows_of(step):
        away, r = step < half, step % half
        return tile_rows(2 * r + (1 - y if away else y), block)

    def multiply(step):
        rows = rows_of(step)
        if not count:
            return branch_ref[rows, :]
        last = lax.rem(place_ref[0] + 1, 4)
        part = hidden_block((act_0_ref, act_1_ref), rows, last)
        return branch_ref[rows, :] + dot(part, w_ref[tile_rows(last, w_ref.shape[0] // 4), :])

    def finish(step, branch):
        away, r = step < half, step % half
        rows = rows_of(step)
        value = xhat_ref[rows, :] * gain_mix + (branch + shift_mix)
        center = value - jnp.mean(value, axis=-1, keepdims=True)
        rstd = lax.rsqrt(jnp.mean(center * center, axis=-1, keepdims=True) + EPS)
        xhat = center * rstd
        result = (xhat * gain + shift).astype(BF16)
        if away:
            send_ref[r] = result
            cot = (other_0_ref, other_1_ref)[r][0].astype(F32)
        else:
            keep_ref[r] = result
            cot = mine_ref[half * y + r].astype(F32)
        d_xhat = cot * gain
        d_resid = rstd * (
            d_xhat
            - jnp.mean(d_xhat, axis=-1, keepdims=True)
            - xhat * jnp.mean(d_xhat * xhat, axis=-1, keepdims=True)
        )
        d_low = d_resid.astype(BF16)
        resid_ref[rows, :] = d_resid
        low_ref[rows, :] = d_low
        sums_ref[0:1, :] += row_sum(d_low.astype(F32))
        sums_ref[1:2, :] += row_sum(cot * xhat)
        sums_ref[2:3, :] += row_sum(cot)

    part_ref[0] = multiply(0)
    for step in range(2 * half):
        if step + 1 < 2 * half:
            part_ref[(step + 1) % 2] = multiply(step + 1)
        finish(step, part_ref[step % 2])


def ffn_out(place, branch, xhat, cotangent, cot_others, vectors, acts=(), w_out=None, groups=()):
    count, width = xhat.shape
    half, block = len(cot_others), cot_others[0].shape[1]
    hidden = 2 * acts[0].shape[1] if groups else 0
    before = [*acts, w_out] if groups else []
    out_shape = [((hidden, width), BF16)] if groups else []
    out_shape += [
        ((half, block, width), BF16),
        ((half, block, width), BF16),
        ((count, width), F32),
        ((count, width), BF16),
        ((8, width), F32),
    ]
    return vmem_call(
        functools.partial(ffn_out_kernel, count=len(groups)),
        "ffn_out_norm",
        out_shape,
        10,
        cost(count * hidden * width // 2, 30 * count * width),
        [pltpu.VMEM((2, block, width), F32)],
        places=1,
        aliases={3: 0} if groups else None,
    )(place, *before, branch, xhat, cotangent, *cot_others, vectors, *groups)


def slot(place_ref, xx, yy, core):
    same_x = jnp.where(place_ref[1] == xx, 1, 0)
    same_y = jnp.where(place_ref[3] == yy, 1, 0)
    return jnp.where(core == 0, same_y, same_x), jnp.where(core == 0, same_x, same_y)


def grad_out_kernel(place_ref, act_0_ref, act_1_ref, low_ref, _, send_ref, keep_ref, *, first):
    c = place_ref[2]
    rows = send_ref.shape[2]
    columns = 8 * rows

    def group(xx, yy):
        return jnp.where(place_ref[3] == yy, 0, 1) + jnp.where(place_ref[1] == xx, 0, 2)

    def step(j, carry):
        t, xx = j // 2, lax.rem(j, 2)
        block = lax.rem(place_ref[0] + 7 - first - t, 4)
        cut = pl.ds(pl.multiple_of(lax.rem(block, 2) * columns + xx * (columns // 2), LANES), columns // 2)
        act = jnp.where(block >= 2, act_1_ref[:, cut], act_0_ref[:, cut])
        total = dot_tn(act, low_ref[...])
        for yy in range(2):
            one = total[yy * rows : (yy + 1) * rows]
            two = total[(2 + yy) * rows : (3 + yy) * rows]
            send_ref[t, group(xx, yy)] = jnp.where(c == 0, two, one).astype(BF16)
            keep_ref[t, group(xx, yy)] = jnp.where(c == 0, one, two).astype(BF16)
        return carry

    lax.fori_loop(0, 2 * send_ref.shape[0], step, 0)


def grad_out(place, acts, d_low, nearby, rows, first, steps):
    count, width = d_low.shape
    shape = (steps, 4, rows, width)
    return vmem_call(
        functools.partial(grad_out_kernel, first=first),
        "grad_w_out",
        [(shape, BF16), (shape, BF16)],
        6,
        cost(16 * steps * count * rows * width, 16 * steps * count * rows),
        places=1,
    )(place, *acts, d_low, nearby)


def ffn_back_kernel(place_ref, low_ref, resid_ref, slope_0_ref, slope_1_ref, w_out_ref, w_in_ref, xhat_ref, rstd_ref, vec_ref, low_t_ref, two_ref, *refs, tile, columns):
    if len(refs) == 7:
        mix_ref, one_ref, send_ref, keep_ref, pre_ref, bias_ref, sums_ref = refs
    else:
        mix_ref, one_ref, pre_ref, bias_ref, sums_ref = refs
    hidden = pre_ref.shape[1]
    share = slope_0_ref.shape[1]
    bias_ref[...] = jnp.zeros_like(bias_ref)
    sums_ref[...] = jnp.zeros_like(sums_ref)

    def step(i, carry):
        rows = tile_rows(i, tile)
        d_low = low_ref[rows, :]
        d_normed = resid_ref[rows, :]
        for part in range(0, hidden, columns):
            cut = slice(part, part + columns)
            slope_ref = (slope_0_ref, slope_1_ref)[part // share]
            slope = slope_ref[rows, part % share : part % share + columns].astype(F32)
            d_pre = (dot_nt(d_low, w_out_ref[cut, :]) * slope).astype(BF16)
            pre_ref[rows, cut] = d_pre
            bias_ref[0:1, cut] += row_sum(d_pre.astype(F32))
            d_normed += dot_nt(d_pre, w_in_ref[:, cut])
        xhat = xhat_ref[rows, :]
        sums_ref[0:1, :] += row_sum(d_normed * xhat)
        sums_ref[1:2, :] += row_sum(d_normed)
        d_xhat = d_normed * vec_ref[1:2, :]
        d_one = rstd_ref[rows, :] * (
            d_xhat
            - jnp.mean(d_xhat, axis=-1, keepdims=True)
            - xhat * jnp.mean(d_xhat * xhat, axis=-1, keepdims=True)
        )
        one_ref[rows, :] = d_one
        mix_ref[rows, :] = d_one.astype(BF16)
        return carry

    lax.fori_loop(0, low_ref.shape[0] // tile, step, 0)
    if len(refs) == 7:
        grad_in_part(place_ref, low_t_ref, pre_ref, bias_ref, two_ref, sums_ref, send_ref, keep_ref)


def grad_in_part(place_ref, low_ref, pre_ref, bias_ref, two_ref, one_ref, send_ref, keep_ref):
    c = place_ref[2]
    split = pre_ref.shape[1]
    owners, width = 32, low_ref.shape[0]
    size = width // owners

    def gathered(values, first, part):
        total = values.shape[1]
        high = values.astype(BF16)
        rest = values - high.astype(F32)
        middle = rest.astype(BF16)
        lowest = (rest - middle.astype(F32)).astype(BF16)
        matrix = spread_matrix(part, first, total).astype(BF16)
        mask = owner_mask(total // part, total)
        return sum(dot_nt(jnp.where(mask, piece, 0.0).astype(BF16), matrix) for piece in (high, middle, lowest))

    line_0 = gathered(bias_ref[0:1, :], 0, 4 * size)
    line_1 = jnp.zeros((owners, LANES), F32)
    for i, (ref, row) in enumerate(
        ((two_ref, 0), (one_ref, 0), (one_ref, 1), (two_ref, 1), (two_ref, 2))
    ):
        line_1 += gathered(ref[row : row + 1, :], i * size, size)
    send_ref[:, :, :, :, split:] = jnp.zeros(send_ref.shape[:4] + (LANES,), BF16)
    keep_ref[:, :, :, :, split:] = jnp.zeros(keep_ref.shape[:4] + (LANES,), BF16)
    rows = send_ref.shape[3]
    columns = split // 2
    for z in range(4):
        for cut in (slice(0, columns), slice(columns, split)):
            total = dot(low_ref[8 * z * rows : 8 * (z + 1) * rows, :], pre_ref[:, cut])
            for xx in range(2):
                for yy in range(2):
                    at = (4 * xx + yy) * rows
                    first, second = total[at : at + rows], total[at + 2 * rows : at + 3 * rows]
                    away, stay = slot(place_ref, xx, yy, 1 - c), slot(place_ref, xx, yy, c)
                    send_ref[away[0], z, away[1], :, cut] = jnp.where(c == 0, second, first).astype(BF16)
                    keep_ref[stay[0], z, stay[1], :, cut] = jnp.where(c == 0, first, second).astype(BF16)
        for xx in range(2):
            for yy in range(2):
                at = 8 * z + 4 * xx + yy
                away, stay = slot(place_ref, xx, yy, 1 - c), slot(place_ref, xx, yy, c)
                for row, line in enumerate((line_0, line_1)):
                    first, second = line[at : at + 1], line[at + 2 : at + 3]
                    side = jnp.where(c == 0, second, first)
                    send_ref[away[0], z, away[1], row : row + 1, split:] = side.astype(BF16)
                    side = jnp.where(c == 0, first, second)
                    keep_ref[stay[0], z, stay[1], row : row + 1, split:] = side.astype(BF16)


def ffn_back(place, d_low, d_resid, slopes, w_out, w_in, norm, low_t, sums_two, chained, tile=512, columns=768):
    count, width = d_low.shape
    hidden = 2 * slopes[0].shape[1]
    out_shape = [((count, width), BF16), ((count, width), F32)]
    backs = [((count, hidden), BF16), ((8, hidden), F32), ((8, width), F32)]
    scratch_shapes = []
    if chained:
        shape = (2, 4, 2, width // 32, hidden + LANES)
        out_shape += [(shape, BF16), (shape, BF16)]
        scratch_shapes = [pltpu.VMEM(*each) for each in backs]
    else:
        out_shape += backs
    return vmem_call(
        functools.partial(ffn_back_kernel, tile=tile, columns=columns),
        "ffn_back",
        out_shape,
        12,
        cost(6 * count * hidden * width, 6 * count * hidden + 4 * hidden * width),
        scratch_shapes,
        places=1,
    )(place, d_low, d_resid, *slopes, w_out, w_in, *norm, low_t, sums_two)


def mix_back_kernel(place_ref, low_ref, one_ref, hid_ref, seq_ref, send_ref, keep_ref, spec_ref):
    width = low_ref.shape[1]
    length = seq_ref.shape[0]
    block = length // 2
    y = place_ref[3]

    def step(r, carry):
        for part in range(2):
            cut = slice(part * width, (part + 1) * width)
            spec = dot(low_ref[tile_rows(r, length), :], hid_ref[:, cut])
            spec_ref[part * length : (part + 1) * length, :] = spec.astype(BF16)
        for spot, away in ((1 - y, True), (y, False)):
            total = dot(seq_ref[tile_rows(spot, block), :], spec_ref[...])
            total += one_ref[tile_rows(2 * r + spot, block), :]
            if away:
                send_ref[r] = total.astype(BF16)
            else:
                keep_ref[r] = total
        return carry

    lax.fori_loop(0, low_ref.shape[0] // length, step, 0)


def mix_back(place, d_low, d_one, hid_table, seq_table):
    count, width = d_low.shape
    length = seq_table.shape[0]
    half, block = count // length, length // 2
    return vmem_call(
        mix_back_kernel,
        "mix_back",
        [((half, block, width), BF16), ((half, block, width), F32)],
        14,
        cost(4 * count * width * (length + width), 10 * count * width),
        [pltpu.VMEM((2 * length, width), BF16)],
        places=1,
    )(place, d_low, d_one, hid_table, seq_table)


def join_kernel(place_ref, *refs, first, earlier):
    *ins, out_ref, wide_ref, sem = refs
    ins = ins[: len(ins) - earlier]
    y = place_ref[3]
    half = out_ref.shape[0] // 2
    copies = []
    for i, ref in enumerate(ins):
        rows = ref.shape[0]
        source = ref
        if ref.dtype != out_ref.dtype:
            source = wide_ref.at[pl.ds(0, rows)]
            wide_ref[:rows] = ref[...].astype(wide_ref.dtype)
        at = half * y if rows == half and first == 0 and i == 0 else half * (1 - y) + first
        copies.append(pltpu.make_async_copy(source, out_ref.at[pl.ds(at, rows)], sem.at[i]))
        copies[-1].start()
    for copy in copies:
        copy.wait()


def join(place, keep, other, first=0, joined=None):
    half, block, width = keep.shape
    ins = [other] if joined is not None else [keep, other]
    wide = other.shape if other.dtype != keep.dtype else (1, 8, LANES)
    earlier = [] if joined is None else [joined]
    return vmem_call(
        functools.partial(join_kernel, first=first, earlier=len(earlier)),
        "join_rows",
        [((2 * half, block, width), keep.dtype)],
        4,
        cost(0, 16 * half * block * width),
        [pltpu.VMEM(wide, keep.dtype), pltpu.SemaphoreType.DMA((2,))],
        places=1,
        anywhere=len(earlier),
        outside=True,
        aliases={2: 0} if earlier else None,
    )(place, *ins, *earlier)[0]


def finish_kernel(own_ref, *refs, spots):
    parts, (w_ref, *smalls) = refs[:3], refs[3:]
    split = w_ref.shape[1]
    total = own_ref[...]
    for ref in parts:
        total += ref[...].astype(F32)
    w_ref[...] = total[:, :split]
    for ref, (line, at) in zip(smalls, spots):
        ref[...] = total[line : line + 1, split + at : split + at + ref.shape[1]]


def finish(own, parts, split, sizes, spots):
    rows, _ = own.shape
    return vmem_call(
        functools.partial(finish_kernel, spots=spots),
        "finish_w_in",
        [((rows, split), F32)] + [((1, size), F32) for size in sizes],
        4,
        cost(3 * rows * split, 14 * rows * split),
    )(own, *parts)


def add_up(keep, other):
    return keep.astype(F32) + other.astype(F32)


def per_device(grid, tokens, weight_in, bias_in, weight_out, bias_out, gain_mix, shift_mix, gain_ffn, shift_ffn, cotangent):
    rows, block, width = tokens.shape
    part_in, hidden = weight_in.shape
    part_out = weight_out.shape[0]
    half = rows // 2
    length = 2 * block
    devices = grid.dp * grid.seq
    z, x, c, y = grid.place()
    place = jnp.stack([z, x, c, y]).astype(jnp.int32)
    zero = jnp.uint32(0)
    across = ((1 - y) * half).astype(jnp.uint32)
    ahead = [((z + step) % 4).astype(jnp.uint32) for step in range(4)]
    place, across, ahead, weight_in = together(place, across, ahead, weight_in)
    chained = grid.chained and part_in % 8 == 0

    def other_rows(value):
        return lax.dynamic_slice(value, (across, zero, zero), (half,) + value.shape[1:])

    def join_rows(keep, other):
        other = other.astype(keep.dtype)
        return jnp.where(
            y == 0, jnp.concatenate([keep, other], 0), jnp.concatenate([other, keep], 0)
        )

    def core(value):
        return send(value, grid.cores)

    smalls = (bias_in, bias_out, gain_mix, shift_mix, gain_ffn, shift_ffn)
    sizes = [v.shape[0] for v in smalls]
    spots = [(0, 0)] + [(1, i * sizes[1]) for i in range(5)]
    lines = [0, 0]
    for value, (line, at) in zip(smalls, spots):
        lines[line] += jnp.pad(value, (at, LANES - at - value.shape[0]))
    strip = jnp.pad(jnp.stack(lines), ((0, part_in - 2), (0, 0)))
    tok_other = send(other_rows(tokens), grid.blocks)

    cos_seq, sin_seq = dft_tables(length)
    cos_hid, sin_hid = dft_tables(width)
    mix_tables = (
        table(np.concatenate([cos_seq, sin_seq], 0)),
        table(np.concatenate([cos_hid, -sin_hid], 0)),
    )
    if chained:
        packed = jnp.concatenate([weight_in, strip], axis=1)
        packed, shard_out = together(packed, weight_out)
        *pieces, near_out, tok_other = together(
            *(send(packed, grid.shifts[step]) for step in range(1, 4)),
            send(shard_out, grid.across),
            tok_other,
        )
        pair = jnp.stack([shard_out, near_out])
        column = jnp.stack([packed] + pieces)
        column, pair, tok_other = together(column, pair, tok_other)
        near, ring_1, far_pair, twin_column, (xhat, rstd) = together(
            send(column, grid.across_0),
            send(pair, grid.ring),
            send(pair, grid.blocks),
            core(column),
            mix(place, tokens, tok_other, *mix_tables),
        )
        both = jnp.concatenate([column, near], axis=0)
        both, pairs = together(both, jnp.concatenate([far_pair, ring_1], axis=0))
        far, ring_2 = together(send(both, grid.across_1), send(pairs, grid.ring))
        ring_3 = send(ring_2, grid.ring)
        groups = [column, near, far, twin_column, core(after(near, far)), core(far)]
        w_in, bias, vectors, low, low_t = first_weight(place, xhat, groups, hidden)
        cot_part = after(other_rows(cotangent), vectors)
        cot_0 = send(cot_part[:1], grid.blocks)
    else:
        cot_other = send(other_rows(cotangent), grid.blocks)
        xhat, rstd = mix(place, tokens, tok_other, *mix_tables)
        w_in = lax.all_gather(weight_in, AXES, axis=0, tiled=True)
        w_out = lax.all_gather(weight_out, AXES, axis=0, tiled=True)
        extra = lax.all_gather(strip, AXES, axis=0)[:, :2]
        bias, *vectors = [
            extra[:, line, at : at + size].reshape(1, -1).astype(F32)
            for size, (line, at) in zip(sizes, spots)
        ]
        vectors = jnp.concatenate(vectors + [jnp.zeros((3, width), F32)], axis=0)
        low, low_t = ffn_low(xhat, vectors)
    act_0, slope_0 = ffn_in(low, w_in, bias, 0, 2)
    if chained:
        early = [pair, far_pair, ring_1, ring_2]
        act_0, slope_0, low, ring_3, cot_0, twins = together(
            act_0, slope_0, low, ring_3, cot_0, [core(p) for p in early]
        )
        ring_4 = send(ring_3[:2], grid.ring)
        cot_1 = send(after(cot_part[1:], cot_0), grid.blocks)
        pairs = early + [ring_3] + twins + [core(ring_3)]
        act_1, slope_1, w_out, branch = ffn_in_last(place, low, w_in, bias, act_0, pairs)
        ring_4, cot_1, branch = together(ring_4, cot_1, branch)
    else:
        act_1, slope_1 = ffn_in(low, w_in, bias, 1, 2)
    acts, slopes = [act_0, act_1], [slope_0, slope_1]
    if chained:
        w_out, out_send, out_keep, d_resid, d_low, sums_two = ffn_out(
            place, branch, xhat, cotangent, (cot_0, cot_1), vectors, acts, w_out, [ring_4, core(ring_4)]
        )
    else:
        branch = dot(act_0, w_out[: hidden // 2]) + dot(act_1, w_out[hidden // 2 :])
        out_send, out_keep, d_resid, d_low, sums_two = ffn_out(
            place, branch, xhat, cotangent, (cot_other[:1], cot_other[1:]), vectors
        )

    norm = (xhat, rstd, vectors)
    back_tables = (
        table(np.concatenate([cos_hid, -sin_hid], 1)),
        table(np.concatenate([cos_seq, sin_seq], 1)),
    )

    def pack_small(bias_sum, norm_sum):
        grads = (bias_sum, sums_two[0], norm_sum[0], norm_sum[1], sums_two[1], sums_two[2])
        lines = [0, 0]
        for value, (line, at) in zip(grads, spots):
            value = value.reshape(devices, -1)
            lines[line] += jnp.pad(value, ((0, 0), (at, LANES - at - value.shape[1])))
        return jnp.pad(jnp.stack(lines, axis=1), ((0, 0), (0, part_in - 2), (0, 0)))

    def low_send(value, perm):
        return send(value.astype(BF16), perm)

    if chained:
        (away_a, keep_a), start = together(grad_out(place, acts, d_low, w_out, part_out, 0, 1), d_low)
        twin_a, (away_b, keep_b) = together(core(away_a), grad_out(place, acts, start, w_out, part_out, 1, 3))
        quad = add_up(keep_a[0], twin_a[0])
        start, away_b, quad, out_send = together(start, away_b, quad, out_send)
        twin_b, ring, out_other, (d_mix, d_one, away, keep) = together(
            core(away_b),
            low_send(quad, grid.ring),
            send(out_send, grid.blocks),
            ffn_back(place, start, d_resid, slopes, w_out, w_in, norm, low_t, sums_two, True),
        )
        quad = add_up(add_up(keep_b[0], twin_b[0]), ring)
        twin, quad = together(core(away), quad)
        first, ring, output, (gt_send, gt_keep) = together(
            low_send(add_up(keep[0], twin[0]), grid.across_1),
            low_send(quad, grid.ring),
            join(place, out_keep, out_other),
            mix_back(place, d_mix, d_one, *back_tables),
        )
        pair = add_up(add_up(keep[1], twin[1]), first)
        quad = add_up(add_up(keep_b[1], twin_b[1]), ring)
        second, ring, gt_0 = together(
            low_send(pair[:, 0], grid.across_0),
            low_send(quad, grid.ring),
            send(gt_send[:1], grid.blocks),
        )
        column = add_up(pair[:, 1], second)
        quad = add_up(add_up(keep_b[2], twin_b[2]), ring)
        gt_1 = send(after(gt_send[1:], quad), grid.blocks)
        grad_tokens = join(place, gt_keep, gt_0)
        parts, far, gt_1, grad_tokens = together(
            [low_send(pick(column, ahead[step]), grid.shifts[step]) for step in range(1, 4)],
            low_send(quad[2:], grid.across),
            gt_1,
            grad_tokens,
        )
        quad = add_up(quad[:2], far)
        my_w_out = add_up(quad[0], low_send(quad[1], grid.blocks))
        grad_tokens = join(place, gt_keep, gt_1, 1, grad_tokens)
        my_w_in, *my_small = finish(pick(column, ahead[0]), parts, hidden, sizes, spots)
        my_small = [v.reshape(-1) for v in my_small]
    else:
        output = join_rows(out_keep, send(out_send, grid.blocks))
        grad_w_out = jnp.concatenate([dot_tn(act, d_low) for act in acts], axis=0)
        my_w_out = lax.psum_scatter(grad_w_out, AXES, scatter_dimension=0, tiled=True)
        d_mix, d_one, pre, bias_sum, norm_sum = ffn_back(
            place, d_low, d_resid, slopes, w_out, w_in, norm, low_t, sums_two, False
        )
        gt_send, gt_keep = mix_back(place, d_mix, d_one, *back_tables)
        grad_tokens = join_rows(gt_keep, send(gt_send, grid.blocks))
        my_w_in = lax.psum_scatter(dot(low_t, pre), AXES, scatter_dimension=0, tiled=True)
        strips = pack_small(bias_sum[0], norm_sum)
        my_strip = lax.psum_scatter(strips, AXES, scatter_dimension=0, tiled=True)[0, :2]
        my_small = [my_strip[line, at : at + size] for size, (line, at) in zip(sizes, spots)]
    return (
        output,
        grad_tokens,
        my_w_in,
        my_small[0],
        my_w_out,
        my_small[1],
        my_small[2],
        my_small[3],
        my_small[4],
        my_small[5],
    )


def solution(mesh):
    grid = Grid(mesh)
    cut, cut2 = P(AXES), P(AXES, None)
    block = P("dp", "seq", None)
    in_specs = (block, cut2, cut, cut2, cut, cut, cut, cut, cut, block)
    out_specs = (block, block, cut2, cut, cut2, cut, cut, cut, cut, cut)

    def program(*arrays):
        return per_device(grid, *arrays)

    return jax.shard_map(
        program, mesh=mesh, in_specs=in_specs, out_specs=out_specs, check_vma=False
    )
```

```python
import functools
import math

import jax
import jax.numpy as jnp
import numpy as np
from jax import lax
from jax.experimental import pallas as pl
from jax.experimental.pallas import tpu as pltpu
from jax.sharding import PartitionSpec as P

EPS = 1e-12
AXES = ("dp", "seq")
BF16 = jnp.bfloat16
F32 = jnp.float32
MIB = 1 << 20
LANES = 128
ERF_T = 0.3275911
ERF_P = (0.254829592, -0.284496736, 1.421413741, -1.453152027, 1.061405429)


def dft_tables(length):
    index = np.arange(length, dtype=np.int64)
    angle = (index[:, None] * index[None, :] % length).astype(np.float64) * (2.0 * math.pi / length)
    scale = length ** (-0.5)
    return np.cos(angle) * scale, np.sin(angle) * scale


def table(values):
    return jnp.asarray(values.astype(np.float32)).astype(BF16)


class Grid:
    def __init__(self, mesh):
        self.dp = mesh.shape["dp"]
        self.seq = mesh.shape["seq"]
        chips = self.dp // 2
        self.low = min(2, chips)
        self.high = chips // self.low
        self.shifts = [
            self.perm(lambda z, x, c, y: ((z + step) % self.high, x, c, y)) for step in range(4)
        ]
        self.ring = self.shifts[1]
        self.across = self.perm(lambda z, x, c, y: (z, (x + 1) % self.low, c, y))
        self.corner = self.perm(
            lambda z, x, c, y: (z, (x + 1) % self.low, c, (y + 1) % self.seq)
        )
        self.cores = self.perm(lambda z, x, c, y: (z, x, 1 - c, y))
        self.blocks = self.perm(lambda z, x, c, y: (z, x, c, (y + 1) % self.seq))
        self.across_0 = self.perm(
            lambda z, x, c, y: (z, (x + 1 - c) % self.low, c, (y + c) % self.seq)
        )
        self.across_1 = self.perm(
            lambda z, x, c, y: (z, (x + c) % self.low, c, (y + 1 - c) % self.seq)
        )
        self.chained = self.high == 4 and self.low == 2 and self.seq == 2

    def index(self, z, x, c, y):
        return ((z * self.low + x) * 2 + c) * self.seq + y

    def perm(self, move):
        return [
            (self.index(z, x, c, y), self.index(*move(z, x, c, y)))
            for z in range(self.high)
            for x in range(self.low)
            for c in range(2)
            for y in range(self.seq)
        ]

    def place(self):
        dp = lax.axis_index("dp")
        return dp // (2 * self.low), dp // 2 % self.low, dp % 2, lax.axis_index("seq")


def send(value, perm):
    return lax.ppermute(value, AXES, perm)


def pick(value, index):
    zero = jnp.uint32(0)
    starts = (index,) + (zero,) * (value.ndim - 1)
    return lax.dynamic_slice(value, starts, (1,) + value.shape[1:])[0]


def dot(a, b):
    return jnp.dot(a, b, preferred_element_type=F32)


def dot_nt(a, b):
    return lax.dot_general(a, b, (((1,), (1,)), ((), ())), preferred_element_type=F32)


def dot_tn(a, b):
    return lax.dot_general(a, b, (((0,), (0,)), ((), ())), preferred_element_type=F32)


def params(mib):
    return pltpu.CompilerParams(vmem_limit_bytes=mib * MIB)


def cost(flops, bytes_accessed, transcendentals=0):
    return pl.CostEstimate(
        flops=int(flops), bytes_accessed=int(bytes_accessed), transcendentals=int(transcendentals)
    )


def row_sum(values):
    return jnp.sum(values, axis=0, keepdims=True)


def after(value, *others):
    return lax.optimization_barrier((value,) + others)[0]


def together(*values):
    return lax.optimization_barrier(values)


def device_number(place, distance, flip_x, flip_y, other_core):
    z, x, c, y = place
    zz = lax.rem(z - distance + 4, 4)
    cc = 1 - c if other_core else c
    xx = x + flip_x - 2 * x * flip_x
    yy = y + flip_y - 2 * y * flip_y
    return ((zz * 2 + xx) * 2 + cc) * 2 + yy


def column_slab(part, index, core):
    group = part + index // 4
    flip_x, flip_y = ((0, 0), (1 - core, core), (core, 1 - core), (1, 1))[group]
    return index % 4, flip_x, flip_y


def ring_slab(position):
    return position // 4, position % 2, position % 4 // 2


def put_slabs(place, refs, slab_of, put):
    own = len(refs) // 2
    for part, ref in enumerate(refs):
        core = 1 - place[2] if part >= own else place[2]
        for i in range(ref.shape[0]):
            where = slab_of(part % own, i, core)
            put(ref, i, device_number(place, *where, part >= own))


def vmem_call(kernel, name, out_shape, mib, work, scratch_shapes=(), places=0, anywhere=0, outside=False, aliases=None):
    def call(*operands):
        here = len(operands) - places - anywhere
        return pl.pallas_call(
            kernel,
            name=name,
            in_specs=[pl.BlockSpec(memory_space=pltpu.SMEM)] * places
            + [pl.BlockSpec(memory_space=pltpu.VMEM)] * here
            + [pl.BlockSpec(memory_space=pl.ANY)] * anywhere,
            out_specs=[pl.BlockSpec(memory_space=pl.ANY if outside else pltpu.VMEM)] * len(out_shape),
            out_shape=[jax.ShapeDtypeStruct(*each) for each in out_shape],
            scratch_shapes=list(scratch_shapes),
            input_output_aliases=aliases or {},
            compiler_params=params(mib),
            cost_estimate=work,
        )(*operands)

    return call


def tile_rows(index, size):
    return pl.ds(pl.multiple_of(index * size, size), size)


def assemble(place, groups, split):
    _, rows, columns = groups[0].shape
    slabs = sum(group.shape[0] for group in groups)
    return vmem_call(
        functools.partial(assemble_kernel, count=len(groups), split=split),
        "assemble_w_in",
        [((slabs * rows, split), BF16), ((slabs, rows, LANES), BF16)],
        2,
        cost(0, 4 * slabs * rows * columns),
        [pltpu.SemaphoreType.DMA((2 * slabs,))],
        places=1,
        anywhere=len(groups),
    )(place, *groups)


def spread_matrix(size, start, total):
    lane = lax.broadcasted_iota(jnp.int32, (LANES, total), 0)
    column = lax.broadcasted_iota(jnp.int32, (LANES, total), 1)
    return lane == start + lax.rem(column, size)


def owner_mask(owners, total):
    owner = lax.broadcasted_iota(jnp.int32, (owners, total), 0)
    column = lax.broadcasted_iota(jnp.int32, (owners, total), 1)
    return lax.div(column, total // owners) == owner


def first_weight_kernel(place_ref, xhat_ref, *refs, count, split):
    groups = refs[:count]
    full_ref, bias_ref, vec_ref, low_ref, low_t_ref, extra_ref = refs[count:]
    rows = groups[0].shape[1]
    place = tuple(place_ref[i] for i in range(4))

    def put(ref, i, at):
        full_ref[tile_rows(at, rows), :] = ref[i, :, :split]
        extra_ref[at] = ref[i, :, split:]

    put_slabs(place, groups, column_slab, put)
    owners, width = extra_ref.shape[0], vec_ref.shape[1]
    line = extra_ref[:, 0, :]
    wide = dot(line, spread_matrix(split // owners, 0, split).astype(BF16))
    bias_ref[...] = row_sum(jnp.where(owner_mask(owners, split), wide, 0.0))
    line = extra_ref[:, 1, :]
    mask = owner_mask(owners, width)
    size = width // owners
    vec_ref[...] = jnp.zeros_like(vec_ref)
    for i in range(5):
        wide = dot(line, spread_matrix(size, i * size, width).astype(BF16))
        vec_ref[i : i + 1, :] = row_sum(jnp.where(mask, wide, 0.0))
    low = (xhat_ref[...] * vec_ref[1:2, :] + vec_ref[2:3, :]).astype(BF16)
    low_ref[...] = low
    low_t_ref[...] = low.T


def first_weight(place, xhat, groups, split):
    _, rows, columns = groups[0].shape
    slabs = sum(group.shape[0] for group in groups)
    count, width = xhat.shape
    return vmem_call(
        functools.partial(first_weight_kernel, count=len(groups), split=split),
        "first_weight",
        [
            ((slabs * rows, split), BF16),
            ((1, split), F32),
            ((8, width), F32),
            ((count, width), BF16),
            ((width, count), BF16),
        ],
        10,
        cost(2 * count * width, 4 * slabs * rows * columns),
        [pltpu.VMEM((slabs, rows, LANES), BF16)],
        places=1,
    )(place, xhat, *groups)


def mix_kernel(place_ref, mine_ref, other_ref, seq_ref, hid_hbm, xhat_ref, rstd_ref, row_ref, hid_ref, sem):
    half, block, width = other_ref.shape
    length = 2 * block
    y = place_ref[3]
    copy = pltpu.make_async_copy(hid_hbm, hid_ref, sem)
    copy.start()

    def spectra(r, part):
        at = part * block
        tokens = row_ref[...]
        cos_part = dot(seq_ref[at : at + block, :], tokens).astype(BF16)
        return cos_part, dot(seq_ref[length + at : length + at + block, :], tokens).astype(BF16)

    for r in range(half):
        row_ref[tile_rows(y, block), :] = mine_ref[half * y + r]
        row_ref[tile_rows(1 - y, block), :] = other_ref[r]
        for part in range(2):
            cos_part, sin_part = spectra(r, part)
            if r == 0 and part == 0:
                copy.wait()
            mixed = dot(cos_part, hid_ref[:width, :]) + dot(sin_part, hid_ref[width:, :])
            resid = row_ref[part * block : (part + 1) * block, :].astype(F32) + mixed
            center = resid - jnp.mean(resid, axis=-1, keepdims=True)
            rstd = lax.rsqrt(jnp.mean(center * center, axis=-1, keepdims=True) + EPS)
            at = (2 * r + part) * block
            xhat_ref[at : at + block, :] = center * rstd
            rstd_ref[at : at + block, :] = rstd


def mix(place, tokens, other, seq_table, hid_table):
    half, block, width = other.shape
    length = 2 * block
    count = half * length
    return vmem_call(
        mix_kernel,
        "mix_norm",
        [((count, width), F32), ((count, 1), F32)],
        14,
        cost(4 * count * width * (length + width), 10 * count * width),
        [
            pltpu.VMEM((length, width), BF16),
            pltpu.VMEM((2 * width, width), BF16),
            pltpu.SemaphoreType.DMA(()),
        ],
        places=1,
        anywhere=1,
    )(place, tokens, other, seq_table, pltpu.with_memory_space_constraint(hid_table, pltpu.HBM))


def gelu_both(values):
    size = jnp.abs(values)
    t = 1.0 / (1.0 + (ERF_T / math.sqrt(2.0)) * size)
    bell = jnp.exp2((values * values) * (-0.5 * math.log2(math.e)))
    poly = 0.5 * ERF_P[4]
    for term in ERF_P[3::-1]:
        poly = 0.5 * term + t * poly
    tail = t * poly * bell
    phi = jnp.where(values > 0, 1.0 - tail, tail)
    return values * phi, phi + values * (bell * (1.0 / math.sqrt(2.0 * math.pi)))


def ffn_low_kernel(xhat_ref, vec_ref, low_ref, low_t_ref):
    low = (xhat_ref[...] * vec_ref[1:2, :] + vec_ref[2:3, :]).astype(BF16)
    low_ref[...] = low
    low_t_ref[...] = low.T


def ffn_low(xhat, vectors):
    count, width = xhat.shape
    return vmem_call(
        ffn_low_kernel,
        "normed_low",
        [((count, width), BF16), ((width, count), BF16)],
        8,
        cost(2 * count * width, 8 * count * width),
    )(xhat, vectors)


def ffn_in_tiles(low_ref, w_ref, bias_ref, act_ref, slope_ref, at, tile, columns):
    tiles = low_ref.shape[0] // tile

    def step(j, carry):
        rows = tile_rows(lax.rem(j, tiles), tile)
        part = j // tiles * columns
        cut = pl.ds(pl.multiple_of(part, LANES), columns)
        full = pl.ds(pl.multiple_of(at + part, LANES), columns)
        act, slope = gelu_both(dot(low_ref[rows, :], w_ref[:, full]) + bias_ref[:, full])
        act_ref[rows, cut] = act.astype(BF16)
        slope_ref[rows, cut] = slope.astype(BF16)
        return carry

    lax.fori_loop(0, tiles * (act_ref.shape[1] // columns), step, 0)


def ffn_in_kernel(low_ref, w_ref, bias_ref, act_ref, slope_ref, *, at, tile, columns):
    ffn_in_tiles(low_ref, w_ref, bias_ref, act_ref, slope_ref, at, tile, columns)


def ffn_in(low, w_in, bias, part, parts, columns=768, tile=512):
    count, width = low.shape
    hidden = w_in.shape[1] // parts
    return vmem_call(
        functools.partial(ffn_in_kernel, at=part * hidden, tile=tile, columns=columns),
        "ffn_in_gelu",
        [((count, hidden), BF16)] * 2,
        8,
        cost(2 * count * width * hidden, 4 * count * hidden, 2 * count * hidden),
    )(low, w_in, bias)


def hidden_block(refs, rows, block):
    width = refs[0].shape[1] // 2
    cut = pl.ds(pl.multiple_of(lax.rem(block, 2) * width, width), width)
    return jnp.where(block >= 2, refs[1][rows, cut], refs[0][rows, cut])


def place_rows(place_ref, groups, w_ref, first):
    place = tuple(place_ref[i] for i in range(4))
    rows = groups[0].shape[1]
    starts = [first]
    for group in groups[: len(groups) // 2]:
        starts.append(starts[-1] + group.shape[0])

    def put(ref, i, at):
        w_ref[tile_rows(at, rows), :] = ref[i]

    put_slabs(place, groups, lambda part, index, core: ring_slab(starts[part] + index), put)


def ffn_in_last_kernel(place_ref, low_ref, w_in_ref, bias_ref, act_0_ref, *refs, count, at, tile, columns, step):
    groups, (act_1_ref, slope_ref, w_ref, branch_ref) = refs[:count], refs[count:]
    place_rows(place_ref, groups, w_ref, 0)
    ffn_in_tiles(low_ref, w_in_ref, bias_ref, act_1_ref, slope_ref, at, tile, columns)
    size = w_ref.shape[0] // 4

    def multiply(i, carry):
        rows = tile_rows(i, step)
        total = None
        for distance in range(3):
            block = lax.rem(place_ref[0] + 4 - distance, 4)
            part = hidden_block((act_0_ref, act_1_ref), rows, block)
            part = dot(part, w_ref[tile_rows(block, size), :])
            total = part if total is None else total + part
        branch_ref[rows, :] = total
        return carry

    lax.fori_loop(0, branch_ref.shape[0] // step, multiply, 0)


def ffn_in_last(place, low, w_in, bias, act_0, groups, columns=768, tile=512, step=512):
    count, width = low.shape
    hidden = act_0.shape[1]
    return vmem_call(
        functools.partial(
            ffn_in_last_kernel, count=len(groups), at=hidden, tile=tile, columns=columns, step=step
        ),
        "ffn_in_out",
        [((count, hidden), BF16)] * 2 + [((2 * hidden, width), BF16), ((count, width), F32)],
        8,
        cost(5 * count * width * hidden, 8 * count * hidden, 2 * count * hidden),
        places=1,
    )(place, low, w_in, bias, act_0, *groups)


def ffn_out_kernel(place_ref, *refs, count):
    if count:
        act_0_ref, act_1_ref, _, *refs = refs
    branch_ref, xhat_ref, mine_ref, other_0_ref, other_1_ref, vec_ref, *refs = refs
    groups, refs = refs[:count], refs[count:]
    if count:
        w_ref, *refs = refs
    send_ref, keep_ref, resid_ref, low_ref, sums_ref, part_ref = refs
    half, block = 2, other_0_ref.shape[1]
    y = place_ref[3]
    if count:
        place_rows(place_ref, groups, w_ref, 14)
    sums_ref[...] = jnp.zeros_like(sums_ref)
    gain_mix = vec_ref[1:2, :]
    shift_mix = vec_ref[2:3, :] + vec_ref[0:1, :]
    gain, shift = vec_ref[3:4, :], vec_ref[4:5, :]

    def rows_of(step):
        away, r = step < half, step % half
        return tile_rows(2 * r + (1 - y if away else y), block)

    def multiply(step):
        rows = rows_of(step)
        if not count:
            return branch_ref[rows, :]
        last = lax.rem(place_ref[0] + 1, 4)
        part = hidden_block((act_0_ref, act_1_ref), rows, last)
        return branch_ref[rows, :] + dot(part, w_ref[tile_rows(last, w_ref.shape[0] // 4), :])

    def finish(step, branch):
        away, r = step < half, step % half
        rows = rows_of(step)
        value = xhat_ref[rows, :] * gain_mix + (branch + shift_mix)
        center = value - jnp.mean(value, axis=-1, keepdims=True)
        rstd = lax.rsqrt(jnp.mean(center * center, axis=-1, keepdims=True) + EPS)
        xhat = center * rstd
        result = (xhat * gain + shift).astype(BF16)
        if away:
            send_ref[r] = result
            cot = (other_0_ref, other_1_ref)[r][0].astype(F32)
        else:
            keep_ref[r] = result
            cot = mine_ref[half * y + r].astype(F32)
        d_xhat = cot * gain
        d_resid = rstd * (
            d_xhat
            - jnp.mean(d_xhat, axis=-1, keepdims=True)
            - xhat * jnp.mean(d_xhat * xhat, axis=-1, keepdims=True)
        )
        d_low = d_resid.astype(BF16)
        resid_ref[rows, :] = d_resid
        low_ref[rows, :] = d_low
        sums_ref[0:1, :] += row_sum(d_low.astype(F32))
        sums_ref[1:2, :] += row_sum(cot * xhat)
        sums_ref[2:3, :] += row_sum(cot)

    part_ref[0] = multiply(0)
    for step in range(2 * half):
        if step + 1 < 2 * half:
            part_ref[(step + 1) % 2] = multiply(step + 1)
        finish(step, part_ref[step % 2])


def ffn_out(place, branch, xhat, cotangent, cot_others, vectors, acts=(), w_out=None, groups=()):
    count, width = xhat.shape
    half, block = len(cot_others), cot_others[0].shape[1]
    hidden = 2 * acts[0].shape[1] if groups else 0
    before = [*acts, w_out] if groups else []
    out_shape = [((hidden, width), BF16)] if groups else []
    out_shape += [
        ((half, block, width), BF16),
        ((half, block, width), BF16),
        ((count, width), F32),
        ((count, width), BF16),
        ((8, width), F32),
    ]
    return vmem_call(
        functools.partial(ffn_out_kernel, count=len(groups)),
        "ffn_out_norm",
        out_shape,
        10,
        cost(count * hidden * width // 2, 30 * count * width),
        [pltpu.VMEM((2, block, width), F32)],
        places=1,
        aliases={3: 0} if groups else None,
    )(place, *before, branch, xhat, cotangent, *cot_others, vectors, *groups)


def slot(place_ref, xx, yy, core):
    same_x = jnp.where(place_ref[1] == xx, 1, 0)
    same_y = jnp.where(place_ref[3] == yy, 1, 0)
    return jnp.where(core == 0, same_y, same_x), jnp.where(core == 0, same_x, same_y)


def grad_out_kernel(place_ref, act_0_ref, act_1_ref, low_ref, _, send_ref, keep_ref, *, first):
    c = place_ref[2]
    rows = send_ref.shape[2]
    columns = 8 * rows

    def group(xx, yy):
        return jnp.where(place_ref[3] == yy, 0, 1) + jnp.where(place_ref[1] == xx, 0, 2)

    def step(j, carry):
        t, xx = j // 2, lax.rem(j, 2)
        block = lax.rem(place_ref[0] + 7 - first - t, 4)
        cut = pl.ds(pl.multiple_of(lax.rem(block, 2) * columns + xx * (columns // 2), LANES), columns // 2)
        act = jnp.where(block >= 2, act_1_ref[:, cut], act_0_ref[:, cut])
        total = dot_tn(act, low_ref[...])
        for yy in range(2):
            one = total[yy * rows : (yy + 1) * rows]
            two = total[(2 + yy) * rows : (3 + yy) * rows]
            send_ref[t, group(xx, yy)] = jnp.where(c == 0, two, one).astype(BF16)
            keep_ref[t, group(xx, yy)] = jnp.where(c == 0, one, two).astype(BF16)
        return carry

    lax.fori_loop(0, 2 * send_ref.shape[0], step, 0)


def grad_out(place, acts, d_low, nearby, rows, first, steps):
    count, width = d_low.shape
    shape = (steps, 4, rows, width)
    return vmem_call(
        functools.partial(grad_out_kernel, first=first),
        "grad_w_out",
        [(shape, BF16), (shape, BF16)],
        6,
        cost(16 * steps * count * rows * width, 16 * steps * count * rows),
        places=1,
    )(place, *acts, d_low, nearby)


def ffn_back_kernel(place_ref, low_ref, resid_ref, slope_0_ref, slope_1_ref, w_out_ref, w_in_ref, xhat_ref, rstd_ref, vec_ref, low_t_ref, two_ref, *refs, tile, columns):
    if len(refs) == 7:
        mix_ref, one_ref, send_ref, keep_ref, pre_ref, bias_ref, sums_ref = refs
    else:
        mix_ref, one_ref, pre_ref, bias_ref, sums_ref = refs
    hidden = pre_ref.shape[1]
    share = slope_0_ref.shape[1]
    bias_ref[...] = jnp.zeros_like(bias_ref)
    sums_ref[...] = jnp.zeros_like(sums_ref)

    def step(i, carry):
        rows = tile_rows(i, tile)
        d_low = low_ref[rows, :]
        d_normed = resid_ref[rows, :]
        for part in range(0, hidden, columns):
            cut = slice(part, part + columns)
            slope_ref = (slope_0_ref, slope_1_ref)[part // share]
            slope = slope_ref[rows, part % share : part % share + columns].astype(F32)
            d_pre = (dot_nt(d_low, w_out_ref[cut, :]) * slope).astype(BF16)
            pre_ref[rows, cut] = d_pre
            bias_ref[0:1, cut] += row_sum(d_pre.astype(F32))
            d_normed += dot_nt(d_pre, w_in_ref[:, cut])
        xhat = xhat_ref[rows, :]
        sums_ref[0:1, :] += row_sum(d_normed * xhat)
        sums_ref[1:2, :] += row_sum(d_normed)
        d_xhat = d_normed * vec_ref[1:2, :]
        d_one = rstd_ref[rows, :] * (
            d_xhat
            - jnp.mean(d_xhat, axis=-1, keepdims=True)
            - xhat * jnp.mean(d_xhat * xhat, axis=-1, keepdims=True)
        )
        one_ref[rows, :] = d_one
        mix_ref[rows, :] = d_one.astype(BF16)
        return carry

    lax.fori_loop(0, low_ref.shape[0] // tile, step, 0)
    if len(refs) == 7:
        grad_in_part(place_ref, low_t_ref, pre_ref, bias_ref, two_ref, sums_ref, send_ref, keep_ref)


def grad_in_part(place_ref, low_ref, pre_ref, bias_ref, two_ref, one_ref, send_ref, keep_ref):
    c = place_ref[2]
    split = pre_ref.shape[1]
    owners, width = 32, low_ref.shape[0]
    size = width // owners

    def gathered(values, first, part):
        total = values.shape[1]
        high = values.astype(BF16)
        rest = values - high.astype(F32)
        middle = rest.astype(BF16)
        lowest = (rest - middle.astype(F32)).astype(BF16)
        matrix = spread_matrix(part, first, total).astype(BF16)
        mask = owner_mask(total // part, total)
        return sum(dot_nt(jnp.where(mask, piece, 0.0).astype(BF16), matrix) for piece in (high, middle, lowest))

    line_0 = gathered(bias_ref[0:1, :], 0, 4 * size)
    line_1 = jnp.zeros((owners, LANES), F32)
    for i, (ref, row) in enumerate(
        ((two_ref, 0), (one_ref, 0), (one_ref, 1), (two_ref, 1), (two_ref, 2))
    ):
        line_1 += gathered(ref[row : row + 1, :], i * size, size)
    send_ref[:, :, :, :, split:] = jnp.zeros(send_ref.shape[:4] + (LANES,), BF16)
    keep_ref[:, :, :, :, split:] = jnp.zeros(keep_ref.shape[:4] + (LANES,), BF16)
    rows = send_ref.shape[3]
    columns = split // 2
    for z in range(4):
        for cut in (slice(0, columns), slice(columns, split)):
            total = dot(low_ref[8 * z * rows : 8 * (z + 1) * rows, :], pre_ref[:, cut])
            for xx in range(2):
                for yy in range(2):
                    at = (4 * xx + yy) * rows
                    first, second = total[at : at + rows], total[at + 2 * rows : at + 3 * rows]
                    away, stay = slot(place_ref, xx, yy, 1 - c), slot(place_ref, xx, yy, c)
                    send_ref[away[0], z, away[1], :, cut] = jnp.where(c == 0, second, first).astype(BF16)
                    keep_ref[stay[0], z, stay[1], :, cut] = jnp.where(c == 0, first, second).astype(BF16)
        for xx in range(2):
            for yy in range(2):
                at = 8 * z + 4 * xx + yy
                away, stay = slot(place_ref, xx, yy, 1 - c), slot(place_ref, xx, yy, c)
                for row, line in enumerate((line_0, line_1)):
                    first, second = line[at : at + 1], line[at + 2 : at + 3]
                    side = jnp.where(c == 0, second, first)
                    send_ref[away[0], z, away[1], row : row + 1, split:] = side.astype(BF16)
                    side = jnp.where(c == 0, first, second)
                    keep_ref[stay[0], z, stay[1], row : row + 1, split:] = side.astype(BF16)


def ffn_back(place, d_low, d_resid, slopes, w_out, w_in, norm, low_t, sums_two, chained, tile=512, columns=768):
    count, width = d_low.shape
    hidden = 2 * slopes[0].shape[1]
    out_shape = [((count, width), BF16), ((count, width), F32)]
    backs = [((count, hidden), BF16), ((8, hidden), F32), ((8, width), F32)]
    scratch_shapes = []
    if chained:
        shape = (2, 4, 2, width // 32, hidden + LANES)
        out_shape += [(shape, BF16), (shape, BF16)]
        scratch_shapes = [pltpu.VMEM(*each) for each in backs]
    else:
        out_shape += backs
    return vmem_call(
        functools.partial(ffn_back_kernel, tile=tile, columns=columns),
        "ffn_back",
        out_shape,
        12,
        cost(6 * count * hidden * width, 6 * count * hidden + 4 * hidden * width),
        scratch_shapes,
        places=1,
    )(place, d_low, d_resid, *slopes, w_out, w_in, *norm, low_t, sums_two)


def mix_back_kernel(place_ref, low_ref, one_ref, hid_ref, seq_ref, send_ref, keep_ref, spec_ref):
    width = low_ref.shape[1]
    length = seq_ref.shape[0]
    block = length // 2
    y = place_ref[3]

    def step(r, carry):
        for part in range(2):
            cut = slice(part * width, (part + 1) * width)
            spec = dot(low_ref[tile_rows(r, length), :], hid_ref[:, cut])
            spec_ref[part * length : (part + 1) * length, :] = spec.astype(BF16)
        for spot, away in ((1 - y, True), (y, False)):
            total = dot(seq_ref[tile_rows(spot, block), :], spec_ref[...])
            total += one_ref[tile_rows(2 * r + spot, block), :]
            if away:
                send_ref[r] = total.astype(BF16)
            else:
                keep_ref[r] = total
        return carry

    lax.fori_loop(0, low_ref.shape[0] // length, step, 0)


def mix_back(place, d_low, d_one, hid_table, seq_table):
    count, width = d_low.shape
    length = seq_table.shape[0]
    half, block = count // length, length // 2
    return vmem_call(
        mix_back_kernel,
        "mix_back",
        [((half, block, width), BF16), ((half, block, width), F32)],
        14,
        cost(4 * count * width * (length + width), 10 * count * width),
        [pltpu.VMEM((2 * length, width), BF16)],
        places=1,
    )(place, d_low, d_one, hid_table, seq_table)


def join_kernel(place_ref, *refs, first, earlier):
    *ins, out_ref, wide_ref, sem = refs
    ins = ins[: len(ins) - earlier]
    y = place_ref[3]
    half = out_ref.shape[0] // 2
    copies = []
    for i, ref in enumerate(ins):
        rows = ref.shape[0]
        source = ref
        if ref.dtype != out_ref.dtype:
            source = wide_ref.at[pl.ds(0, rows)]
            wide_ref[:rows] = ref[...].astype(wide_ref.dtype)
        at = half * y if rows == half and first == 0 and i == 0 else half * (1 - y) + first
        copies.append(pltpu.make_async_copy(source, out_ref.at[pl.ds(at, rows)], sem.at[i]))
        copies[-1].start()
    for copy in copies:
        copy.wait()


def join(place, keep, other, first=0, joined=None):
    half, block, width = keep.shape
    ins = [other] if joined is not None else [keep, other]
    wide = other.shape if other.dtype != keep.dtype else (1, 8, LANES)
    earlier = [] if joined is None else [joined]
    return vmem_call(
        functools.partial(join_kernel, first=first, earlier=len(earlier)),
        "join_rows",
        [((2 * half, block, width), keep.dtype)],
        4,
        cost(0, 16 * half * block * width),
        [pltpu.VMEM(wide, keep.dtype), pltpu.SemaphoreType.DMA((2,))],
        places=1,
        anywhere=len(earlier),
        outside=True,
        aliases={2: 0} if earlier else None,
    )(place, *ins, *earlier)[0]


def finish_kernel(own_ref, *refs, spots):
    parts, (first_ref, near_ref, out_ref, w_ref, *smalls) = refs[:3], refs[3:]
    split = w_ref.shape[1]
    out_ref[...] = first_ref[...] + near_ref[...].astype(F32)
    total = own_ref[...]
    for ref in parts:
        total += ref[...].astype(F32)
    w_ref[...] = total[:, :split]
    for ref, (line, at) in zip(smalls, spots):
        ref[...] = total[line : line + 1, split + at : split + at + ref.shape[1]]


def finish(own, parts, first, near, split, sizes, spots):
    rows, _ = own.shape
    return vmem_call(
        functools.partial(finish_kernel, spots=spots),
        "finish_sums",
        [(first.shape, F32), ((rows, split), F32)] + [((1, size), F32) for size in sizes],
        4,
        cost(3 * rows * split, 14 * rows * split),
    )(own, *parts, first, near)


def add_up(keep, other):
    return keep.astype(F32) + other.astype(F32)


def per_device(grid, tokens, weight_in, bias_in, weight_out, bias_out, gain_mix, shift_mix, gain_ffn, shift_ffn, cotangent):
    rows, block, width = tokens.shape
    part_in, hidden = weight_in.shape
    part_out = weight_out.shape[0]
    half = rows // 2
    length = 2 * block
    devices = grid.dp * grid.seq
    z, x, c, y = grid.place()
    place = jnp.stack([z, x, c, y]).astype(jnp.int32)
    zero = jnp.uint32(0)
    across = ((1 - y) * half).astype(jnp.uint32)
    ahead = [((z + step) % 4).astype(jnp.uint32) for step in range(4)]
    place, across, ahead, weight_in = together(place, across, ahead, weight_in)
    chained = grid.chained and part_in % 8 == 0

    def other_rows(value):
        return lax.dynamic_slice(value, (across, zero, zero), (half,) + value.shape[1:])

    def join_rows(keep, other):
        other = other.astype(keep.dtype)
        return jnp.where(
            y == 0, jnp.concatenate([keep, other], 0), jnp.concatenate([other, keep], 0)
        )

    def core(value):
        return send(value, grid.cores)

    smalls = (bias_in, bias_out, gain_mix, shift_mix, gain_ffn, shift_ffn)
    sizes = [v.shape[0] for v in smalls]
    spots = [(0, 0)] + [(1, i * sizes[1]) for i in range(5)]
    lines = [0, 0]
    for value, (line, at) in zip(smalls, spots):
        lines[line] += jnp.pad(value, (at, LANES - at - value.shape[0]))
    strip = jnp.pad(jnp.stack(lines), ((0, part_in - 2), (0, 0)))
    tok_other = send(other_rows(tokens), grid.blocks)

    cos_seq, sin_seq = dft_tables(length)
    cos_hid, sin_hid = dft_tables(width)
    mix_tables = (
        table(np.concatenate([cos_seq, sin_seq], 0)),
        table(np.concatenate([cos_hid, -sin_hid], 0)),
    )
    if chained:
        packed = jnp.concatenate([weight_in, strip], axis=1)
        packed, shard_out = together(packed, weight_out)
        *pieces, near_out, tok_other = together(
            *(send(packed, grid.shifts[step]) for step in range(1, 4)),
            send(shard_out, grid.across),
            tok_other,
        )
        pair = jnp.stack([shard_out, near_out])
        column = jnp.stack([packed] + pieces)
        column, pair, tok_other = together(column, pair, tok_other)
        near, ring_1, far_pair, twin_column, (xhat, rstd) = together(
            send(column, grid.across_0),
            send(pair, grid.ring),
            send(pair, grid.blocks),
            core(column),
            mix(place, tokens, tok_other, *mix_tables),
        )
        both = jnp.concatenate([column, near], axis=0)
        both, pairs = together(both, jnp.concatenate([far_pair, ring_1], axis=0))
        far, ring_2 = together(send(both, grid.across_1), send(pairs, grid.ring))
        ring_3 = send(ring_2, grid.ring)
        groups = [column, near, far, twin_column, core(after(near, far)), core(far)]
        w_in, bias, vectors, low, low_t = first_weight(place, xhat, groups, hidden)
        cot_part = after(other_rows(cotangent), vectors)
        cot_0 = send(cot_part[:1], grid.blocks)
    else:
        cot_other = send(other_rows(cotangent), grid.blocks)
        xhat, rstd = mix(place, tokens, tok_other, *mix_tables)
        w_in = lax.all_gather(weight_in, AXES, axis=0, tiled=True)
        w_out = lax.all_gather(weight_out, AXES, axis=0, tiled=True)
        extra = lax.all_gather(strip, AXES, axis=0)[:, :2]
        bias, *vectors = [
            extra[:, line, at : at + size].reshape(1, -1).astype(F32)
            for size, (line, at) in zip(sizes, spots)
        ]
        vectors = jnp.concatenate(vectors + [jnp.zeros((3, width), F32)], axis=0)
        low, low_t = ffn_low(xhat, vectors)
    act_0, slope_0 = ffn_in(low, w_in, bias, 0, 2)
    if chained:
        early = [pair, far_pair, ring_1, ring_2]
        act_0, slope_0, low, ring_3, cot_0, twins = together(
            act_0, slope_0, low, ring_3, cot_0, [core(p) for p in early]
        )
        ring_4 = send(ring_3[:2], grid.ring)
        cot_1 = send(after(cot_part[1:], cot_0), grid.blocks)
        pairs = early + [ring_3] + twins + [core(ring_3)]
        act_1, slope_1, w_out, branch = ffn_in_last(place, low, w_in, bias, act_0, pairs)
        ring_4, cot_1, branch = together(ring_4, cot_1, branch)
    else:
        act_1, slope_1 = ffn_in(low, w_in, bias, 1, 2)
    acts, slopes = [act_0, act_1], [slope_0, slope_1]
    if chained:
        w_out, out_send, out_keep, d_resid, d_low, sums_two = ffn_out(
            place, branch, xhat, cotangent, (cot_0, cot_1), vectors, acts, w_out, [ring_4, core(ring_4)]
        )
    else:
        branch = dot(act_0, w_out[: hidden // 2]) + dot(act_1, w_out[hidden // 2 :])
        out_send, out_keep, d_resid, d_low, sums_two = ffn_out(
            place, branch, xhat, cotangent, (cot_other[:1], cot_other[1:]), vectors
        )

    norm = (xhat, rstd, vectors)
    back_tables = (
        table(np.concatenate([cos_hid, -sin_hid], 1)),
        table(np.concatenate([cos_seq, sin_seq], 1)),
    )

    def pack_small(bias_sum, norm_sum):
        grads = (bias_sum, sums_two[0], norm_sum[0], norm_sum[1], sums_two[1], sums_two[2])
        lines = [0, 0]
        for value, (line, at) in zip(grads, spots):
            value = value.reshape(devices, -1)
            lines[line] += jnp.pad(value, ((0, 0), (at, LANES - at - value.shape[1])))
        return jnp.pad(jnp.stack(lines, axis=1), ((0, 0), (0, part_in - 2), (0, 0)))

    def low_send(value, perm):
        return send(value.astype(BF16), perm)

    if chained:
        (away_a, keep_a), start = together(grad_out(place, acts, d_low, w_out, part_out, 0, 1), d_low)
        twin_a, (away_b, keep_b) = together(core(away_a), grad_out(place, acts, start, w_out, part_out, 1, 3))
        quad = add_up(keep_a[0], twin_a[0])
        start, away_b, quad, out_send = together(start, away_b, quad, out_send)
        twin_b, ring, out_other, (d_mix, d_one, away, keep) = together(
            core(away_b),
            low_send(quad, grid.ring),
            send(out_send, grid.blocks),
            ffn_back(place, start, d_resid, slopes, w_out, w_in, norm, low_t, sums_two, True),
        )
        quad = add_up(add_up(keep_b[0], twin_b[0]), ring)
        twin, quad = together(core(away[0]), quad)
        first, ring, output, twin_1, (gt_send, gt_keep) = together(
            low_send(add_up(keep[0], twin), grid.across_1),
            low_send(quad, grid.ring),
            join(place, out_keep, out_other),
            core(away[1]),
            mix_back(place, d_mix, d_one, *back_tables),
        )
        pair = add_up(add_up(keep[1], twin_1), first)
        quad = add_up(add_up(keep_b[1], twin_b[1]), ring)
        second, ring, gt_0 = together(
            low_send(pair[:, 0], grid.across_0),
            low_send(quad, grid.ring),
            send(gt_send[:1], grid.blocks),
        )
        column = add_up(pair[:, 1], second)
        quad = add_up(add_up(keep_b[2], twin_b[2]), ring)
        gt_1 = send(after(gt_send[1:], quad), grid.blocks)
        grad_tokens = join(place, gt_keep, gt_0)
        parts, far, gt_1, grad_tokens, column = together(
            [low_send(pick(column, ahead[step]), grid.shifts[step]) for step in (2, 3)],
            low_send(quad[2:], grid.across),
            gt_1,
            grad_tokens,
            column,
        )
        quad = add_up(quad[:2], far)
        near, last, grad_tokens = together(
            low_send(quad[1], grid.blocks),
            low_send(pick(column, ahead[1]), grid.shifts[1]),
            join(place, gt_keep, gt_1, 1, grad_tokens),
        )
        my_w_out, my_w_in, *my_small = finish(
            pick(column, ahead[0]), parts + [last], quad[0], near, hidden, sizes, spots
        )
        my_small = [v.reshape(-1) for v in my_small]
    else:
        output = join_rows(out_keep, send(out_send, grid.blocks))
        grad_w_out = jnp.concatenate([dot_tn(act, d_low) for act in acts], axis=0)
        my_w_out = lax.psum_scatter(grad_w_out, AXES, scatter_dimension=0, tiled=True)
        d_mix, d_one, pre, bias_sum, norm_sum = ffn_back(
            place, d_low, d_resid, slopes, w_out, w_in, norm, low_t, sums_two, False
        )
        gt_send, gt_keep = mix_back(place, d_mix, d_one, *back_tables)
        grad_tokens = join_rows(gt_keep, send(gt_send, grid.blocks))
        my_w_in = lax.psum_scatter(dot(low_t, pre), AXES, scatter_dimension=0, tiled=True)
        strips = pack_small(bias_sum[0], norm_sum)
        my_strip = lax.psum_scatter(strips, AXES, scatter_dimension=0, tiled=True)[0, :2]
        my_small = [my_strip[line, at : at + size] for size, (line, at) in zip(sizes, spots)]
    return (
        output,
        grad_tokens,
        my_w_in,
        my_small[0],
        my_w_out,
        my_small[1],
        my_small[2],
        my_small[3],
        my_small[4],
        my_small[5],
    )


def solution(mesh):
    grid = Grid(mesh)
    cut, cut2 = P(AXES), P(AXES, None)
    block = P("dp", "seq", None)
    in_specs = (block, cut2, cut, cut2, cut, cut, cut, cut, cut, block)
    out_specs = (block, block, cut2, cut, cut2, cut, cut, cut, cut, cut)

    def program(*arrays):
        return per_device(grid, *arrays)

    return jax.shard_map(
        program, mesh=mesh, in_specs=in_specs, out_specs=out_specs, check_vma=False
    )
```

```python
import functools
import math

import jax
import jax.numpy as jnp
import numpy as np
from jax import lax
from jax.experimental import pallas as pl
from jax.experimental.pallas import tpu as pltpu
from jax.sharding import PartitionSpec as P

EPS = 1e-12
AXES = ("dp", "seq")
BF16 = jnp.bfloat16
F32 = jnp.float32
MIB = 1 << 20
LANES = 128
ERF_T = 0.3275911
ERF_P = (0.254829592, -0.284496736, 1.421413741, -1.453152027, 1.061405429)


def dft_tables(length):
    index = np.arange(length, dtype=np.int64)
    angle = (index[:, None] * index[None, :] % length).astype(np.float64) * (2.0 * math.pi / length)
    scale = length ** (-0.5)
    return np.cos(angle) * scale, np.sin(angle) * scale


def table(values):
    return jnp.asarray(values.astype(np.float32)).astype(BF16)


class Grid:
    def __init__(self, mesh):
        self.dp = mesh.shape["dp"]
        self.seq = mesh.shape["seq"]
        chips = self.dp // 2
        self.low = min(2, chips)
        self.high = chips // self.low
        self.shifts = [
            self.perm(lambda z, x, c, y: ((z + step) % self.high, x, c, y)) for step in range(4)
        ]
        self.ring = self.shifts[1]
        self.across = self.perm(lambda z, x, c, y: (z, (x + 1) % self.low, c, y))
        self.corner = self.perm(
            lambda z, x, c, y: (z, (x + 1) % self.low, c, (y + 1) % self.seq)
        )
        self.cores = self.perm(lambda z, x, c, y: (z, x, 1 - c, y))
        self.blocks = self.perm(lambda z, x, c, y: (z, x, c, (y + 1) % self.seq))
        self.across_0 = self.perm(
            lambda z, x, c, y: (z, (x + 1 - c) % self.low, c, (y + c) % self.seq)
        )
        self.across_1 = self.perm(
            lambda z, x, c, y: (z, (x + c) % self.low, c, (y + 1 - c) % self.seq)
        )
        self.chained = self.high == 4 and self.low == 2 and self.seq == 2

    def index(self, z, x, c, y):
        return ((z * self.low + x) * 2 + c) * self.seq + y

    def perm(self, move):
        return [
            (self.index(z, x, c, y), self.index(*move(z, x, c, y)))
            for z in range(self.high)
            for x in range(self.low)
            for c in range(2)
            for y in range(self.seq)
        ]

    def place(self):
        dp = lax.axis_index("dp")
        return dp // (2 * self.low), dp // 2 % self.low, dp % 2, lax.axis_index("seq")


def send(value, perm):
    return lax.ppermute(value, AXES, perm)


def pick(value, index):
    zero = jnp.uint32(0)
    starts = (index,) + (zero,) * (value.ndim - 1)
    return lax.dynamic_slice(value, starts, (1,) + value.shape[1:])[0]


def dot(a, b):
    return jnp.dot(a, b, preferred_element_type=F32)


def dot_nt(a, b):
    return lax.dot_general(a, b, (((1,), (1,)), ((), ())), preferred_element_type=F32)


def dot_tn(a, b):
    return lax.dot_general(a, b, (((0,), (0,)), ((), ())), preferred_element_type=F32)


def params(mib):
    return pltpu.CompilerParams(vmem_limit_bytes=mib * MIB)


def cost(flops, bytes_accessed, transcendentals=0):
    return pl.CostEstimate(
        flops=int(flops), bytes_accessed=int(bytes_accessed), transcendentals=int(transcendentals)
    )


def row_sum(values):
    return jnp.sum(values, axis=0, keepdims=True)


def after(value, *others):
    return lax.optimization_barrier((value,) + others)[0]


def together(*values):
    return lax.optimization_barrier(values)


def device_number(place, distance, flip_x, flip_y, other_core):
    z, x, c, y = place
    zz = lax.rem(z - distance + 4, 4)
    cc = 1 - c if other_core else c
    xx = x + flip_x - 2 * x * flip_x
    yy = y + flip_y - 2 * y * flip_y
    return ((zz * 2 + xx) * 2 + cc) * 2 + yy


def column_slab(part, index, core):
    group = part + index // 4
    flip_x, flip_y = ((0, 0), (1 - core, core), (core, 1 - core), (1, 1))[group]
    return index % 4, flip_x, flip_y


def ring_slab(position):
    return position // 4, position % 2, position % 4 // 2


def put_slabs(place, refs, slab_of, put):
    own = len(refs) // 2
    for part, ref in enumerate(refs):
        core = 1 - place[2] if part >= own else place[2]
        for i in range(ref.shape[0]):
            where = slab_of(part % own, i, core)
            put(ref, i, device_number(place, *where, part >= own))


def vmem_call(kernel, name, out_shape, mib, work, scratch_shapes=(), places=0, anywhere=0, outside=False, aliases=None):
    def call(*operands):
        here = len(operands) - places - anywhere
        return pl.pallas_call(
            kernel,
            name=name,
            in_specs=[pl.BlockSpec(memory_space=pltpu.SMEM)] * places
            + [pl.BlockSpec(memory_space=pltpu.VMEM)] * here
            + [pl.BlockSpec(memory_space=pl.ANY)] * anywhere,
            out_specs=[pl.BlockSpec(memory_space=pl.ANY if outside else pltpu.VMEM)] * len(out_shape),
            out_shape=[jax.ShapeDtypeStruct(*each) for each in out_shape],
            scratch_shapes=list(scratch_shapes),
            input_output_aliases=aliases or {},
            compiler_params=params(mib),
            cost_estimate=work,
        )(*operands)

    return call


def tile_rows(index, size):
    return pl.ds(pl.multiple_of(index * size, size), size)


def assemble(place, groups, split):
    _, rows, columns = groups[0].shape
    slabs = sum(group.shape[0] for group in groups)
    return vmem_call(
        functools.partial(assemble_kernel, count=len(groups), split=split),
        "assemble_w_in",
        [((slabs * rows, split), BF16), ((slabs, rows, LANES), BF16)],
        2,
        cost(0, 4 * slabs * rows * columns),
        [pltpu.SemaphoreType.DMA((2 * slabs,))],
        places=1,
        anywhere=len(groups),
    )(place, *groups)


def spread_matrix(size, start, total):
    lane = lax.broadcasted_iota(jnp.int32, (LANES, total), 0)
    column = lax.broadcasted_iota(jnp.int32, (LANES, total), 1)
    return lane == start + lax.rem(column, size)


def owner_mask(owners, total):
    owner = lax.broadcasted_iota(jnp.int32, (owners, total), 0)
    column = lax.broadcasted_iota(jnp.int32, (owners, total), 1)
    return lax.div(column, total // owners) == owner


def first_weight_kernel(place_ref, xhat_ref, *refs, count, split):
    groups = refs[:count]
    full_ref, bias_ref, vec_ref, low_ref, low_t_ref, extra_ref = refs[count:]
    rows = groups[0].shape[1]
    place = tuple(place_ref[i] for i in range(4))

    def put(ref, i, at):
        full_ref[tile_rows(at, rows), :] = ref[i, :, :split]
        extra_ref[at] = ref[i, :, split:]

    put_slabs(place, groups, column_slab, put)
    owners, width = extra_ref.shape[0], vec_ref.shape[1]
    line = extra_ref[:, 0, :]
    wide = dot(line, spread_matrix(split // owners, 0, split).astype(BF16))
    bias_ref[...] = row_sum(jnp.where(owner_mask(owners, split), wide, 0.0))
    line = extra_ref[:, 1, :]
    mask = owner_mask(owners, width)
    size = width // owners
    vec_ref[...] = jnp.zeros_like(vec_ref)
    for i in range(5):
        wide = dot(line, spread_matrix(size, i * size, width).astype(BF16))
        vec_ref[i : i + 1, :] = row_sum(jnp.where(mask, wide, 0.0))
    low = (xhat_ref[...] * vec_ref[1:2, :] + vec_ref[2:3, :]).astype(BF16)
    low_ref[...] = low
    low_t_ref[...] = low.T


def first_weight(place, xhat, groups, split):
    _, rows, columns = groups[0].shape
    slabs = sum(group.shape[0] for group in groups)
    count, width = xhat.shape
    return vmem_call(
        functools.partial(first_weight_kernel, count=len(groups), split=split),
        "first_weight",
        [
            ((slabs * rows, split), BF16),
            ((1, split), F32),
            ((8, width), F32),
            ((count, width), BF16),
            ((width, count), BF16),
        ],
        10,
        cost(2 * count * width, 4 * slabs * rows * columns),
        [pltpu.VMEM((slabs, rows, LANES), BF16)],
        places=1,
    )(place, xhat, *groups)


def mix_kernel(place_ref, mine_ref, other_ref, seq_ref, hid_hbm, xhat_ref, rstd_ref, row_ref, hid_ref, sem):
    half, block, width = other_ref.shape
    length = 2 * block
    y = place_ref[3]
    copy = pltpu.make_async_copy(hid_hbm, hid_ref, sem)
    copy.start()

    def spectra(r, part):
        at = part * block
        tokens = row_ref[...]
        cos_part = dot(seq_ref[at : at + block, :], tokens).astype(BF16)
        return cos_part, dot(seq_ref[length + at : length + at + block, :], tokens).astype(BF16)

    for r in range(half):
        row_ref[tile_rows(y, block), :] = mine_ref[half * y + r]
        row_ref[tile_rows(1 - y, block), :] = other_ref[r]
        for part in range(2):
            cos_part, sin_part = spectra(r, part)
            if r == 0 and part == 0:
                copy.wait()
            mixed = dot(cos_part, hid_ref[:width, :]) + dot(sin_part, hid_ref[width:, :])
            resid = row_ref[part * block : (part + 1) * block, :].astype(F32) + mixed
            center = resid - jnp.mean(resid, axis=-1, keepdims=True)
            rstd = lax.rsqrt(jnp.mean(center * center, axis=-1, keepdims=True) + EPS)
            at = (2 * r + part) * block
            xhat_ref[at : at + block, :] = center * rstd
            rstd_ref[at : at + block, :] = rstd


def mix(place, tokens, other, seq_table, hid_table):
    half, block, width = other.shape
    length = 2 * block
    count = half * length
    return vmem_call(
        mix_kernel,
        "mix_norm",
        [((count, width), F32), ((count, 1), F32)],
        14,
        cost(4 * count * width * (length + width), 10 * count * width),
        [
            pltpu.VMEM((length, width), BF16),
            pltpu.VMEM((2 * width, width), BF16),
            pltpu.SemaphoreType.DMA(()),
        ],
        places=1,
        anywhere=1,
    )(place, tokens, other, seq_table, pltpu.with_memory_space_constraint(hid_table, pltpu.HBM))


def gelu_both(values):
    size = jnp.abs(values)
    t = 1.0 / (1.0 + (ERF_T / math.sqrt(2.0)) * size)
    bell = jnp.exp2((values * values) * (-0.5 * math.log2(math.e)))
    poly = 0.5 * ERF_P[4]
    for term in ERF_P[3::-1]:
        poly = 0.5 * term + t * poly
    tail = t * poly * bell
    phi = jnp.where(values > 0, 1.0 - tail, tail)
    return values * phi, phi + values * (bell * (1.0 / math.sqrt(2.0 * math.pi)))


def ffn_low_kernel(xhat_ref, vec_ref, low_ref, low_t_ref):
    low = (xhat_ref[...] * vec_ref[1:2, :] + vec_ref[2:3, :]).astype(BF16)
    low_ref[...] = low
    low_t_ref[...] = low.T


def ffn_low(xhat, vectors):
    count, width = xhat.shape
    return vmem_call(
        ffn_low_kernel,
        "normed_low",
        [((count, width), BF16), ((width, count), BF16)],
        8,
        cost(2 * count * width, 8 * count * width),
    )(xhat, vectors)


def ffn_in_tiles(low_ref, w_ref, bias_ref, act_ref, slope_ref, at, tile, columns):
    tiles = low_ref.shape[0] // tile

    def step(j, carry):
        rows = tile_rows(lax.rem(j, tiles), tile)
        part = j // tiles * columns
        cut = pl.ds(pl.multiple_of(part, LANES), columns)
        full = pl.ds(pl.multiple_of(at + part, LANES), columns)
        act, slope = gelu_both(dot(low_ref[rows, :], w_ref[:, full]) + bias_ref[:, full])
        act_ref[rows, cut] = act.astype(BF16)
        slope_ref[rows, cut] = slope.astype(BF16)
        return carry

    lax.fori_loop(0, tiles * (act_ref.shape[1] // columns), step, 0)


def ffn_in_kernel(low_ref, w_ref, bias_ref, act_ref, slope_ref, *, at, tile, columns):
    ffn_in_tiles(low_ref, w_ref, bias_ref, act_ref, slope_ref, at, tile, columns)


def ffn_in(low, w_in, bias, part, parts, columns=768, tile=512):
    count, width = low.shape
    hidden = w_in.shape[1] // parts
    return vmem_call(
        functools.partial(ffn_in_kernel, at=part * hidden, tile=tile, columns=columns),
        "ffn_in_gelu",
        [((count, hidden), BF16)] * 2,
        8,
        cost(2 * count * width * hidden, 4 * count * hidden, 2 * count * hidden),
    )(low, w_in, bias)


def hidden_block(refs, rows, block):
    width = refs[0].shape[1] // 2
    cut = pl.ds(pl.multiple_of(lax.rem(block, 2) * width, width), width)
    return jnp.where(block >= 2, refs[1][rows, cut], refs[0][rows, cut])


def place_rows(place_ref, groups, w_ref, first):
    place = tuple(place_ref[i] for i in range(4))
    rows = groups[0].shape[1]
    starts = [first]
    for group in groups[: len(groups) // 2]:
        starts.append(starts[-1] + group.shape[0])

    def put(ref, i, at):
        w_ref[tile_rows(at, rows), :] = ref[i]

    put_slabs(place, groups, lambda part, index, core: ring_slab(starts[part] + index), put)


def ffn_in_last_kernel(place_ref, low_ref, w_in_ref, bias_ref, act_0_ref, *refs, count, at, tile, columns, step):
    groups, (act_1_ref, slope_ref, w_ref, branch_ref) = refs[:count], refs[count:]
    place_rows(place_ref, groups, w_ref, 0)
    ffn_in_tiles(low_ref, w_in_ref, bias_ref, act_1_ref, slope_ref, at, tile, columns)
    size = w_ref.shape[0] // 4

    def multiply(i, carry):
        rows = tile_rows(i, step)
        total = None
        for distance in range(3):
            block = lax.rem(place_ref[0] + 4 - distance, 4)
            part = hidden_block((act_0_ref, act_1_ref), rows, block)
            part = dot(part, w_ref[tile_rows(block, size), :])
            total = part if total is None else total + part
        branch_ref[rows, :] = total
        return carry

    lax.fori_loop(0, branch_ref.shape[0] // step, multiply, 0)


def ffn_in_last(place, low, w_in, bias, act_0, groups, columns=768, tile=512, step=512):
    count, width = low.shape
    hidden = act_0.shape[1]
    return vmem_call(
        functools.partial(
            ffn_in_last_kernel, count=len(groups), at=hidden, tile=tile, columns=columns, step=step
        ),
        "ffn_in_out",
        [((count, hidden), BF16)] * 2 + [((2 * hidden, width), BF16), ((count, width), F32)],
        8,
        cost(5 * count * width * hidden, 8 * count * hidden, 2 * count * hidden),
        places=1,
    )(place, low, w_in, bias, act_0, *groups)


def ffn_out_kernel(place_ref, *refs, count):
    if count:
        act_0_ref, act_1_ref, _, *refs = refs
    branch_ref, xhat_ref, mine_ref, other_0_ref, other_1_ref, vec_ref, *refs = refs
    groups, refs = refs[:count], refs[count:]
    if count:
        w_ref, *refs = refs
    send_ref, keep_ref, resid_ref, low_ref, sums_ref, part_ref = refs
    half, block = 2, other_0_ref.shape[1]
    y = place_ref[3]
    if count:
        place_rows(place_ref, groups, w_ref, 14)
    sums_ref[...] = jnp.zeros_like(sums_ref)
    gain_mix = vec_ref[1:2, :]
    shift_mix = vec_ref[2:3, :] + vec_ref[0:1, :]
    gain, shift = vec_ref[3:4, :], vec_ref[4:5, :]

    def rows_of(step):
        away, r = step < half, step % half
        return tile_rows(2 * r + (1 - y if away else y), block)

    def multiply(step):
        rows = rows_of(step)
        if not count:
            return branch_ref[rows, :]
        last = lax.rem(place_ref[0] + 1, 4)
        part = hidden_block((act_0_ref, act_1_ref), rows, last)
        return branch_ref[rows, :] + dot(part, w_ref[tile_rows(last, w_ref.shape[0] // 4), :])

    def finish(step, branch):
        away, r = step < half, step % half
        rows = rows_of(step)
        value = xhat_ref[rows, :] * gain_mix + (branch + shift_mix)
        center = value - jnp.mean(value, axis=-1, keepdims=True)
        rstd = lax.rsqrt(jnp.mean(center * center, axis=-1, keepdims=True) + EPS)
        xhat = center * rstd
        result = (xhat * gain + shift).astype(BF16)
        if away:
            send_ref[r] = result
            cot = (other_0_ref, other_1_ref)[r][0].astype(F32)
        else:
            keep_ref[r] = result
            cot = mine_ref[half * y + r].astype(F32)
        d_xhat = cot * gain
        d_resid = rstd * (
            d_xhat
            - jnp.mean(d_xhat, axis=-1, keepdims=True)
            - xhat * jnp.mean(d_xhat * xhat, axis=-1, keepdims=True)
        )
        d_low = d_resid.astype(BF16)
        resid_ref[rows, :] = d_resid
        low_ref[rows, :] = d_low
        sums_ref[0:1, :] += row_sum(d_low.astype(F32))
        sums_ref[1:2, :] += row_sum(cot * xhat)
        sums_ref[2:3, :] += row_sum(cot)

    part_ref[0] = multiply(0)
    for step in range(2 * half):
        if step + 1 < 2 * half:
            part_ref[(step + 1) % 2] = multiply(step + 1)
        finish(step, part_ref[step % 2])


def ffn_out(place, branch, xhat, cotangent, cot_others, vectors, acts=(), w_out=None, groups=()):
    count, width = xhat.shape
    half, block = len(cot_others), cot_others[0].shape[1]
    hidden = 2 * acts[0].shape[1] if groups else 0
    before = [*acts, w_out] if groups else []
    out_shape = [((hidden, width), BF16)] if groups else []
    out_shape += [
        ((half, block, width), BF16),
        ((half, block, width), BF16),
        ((count, width), F32),
        ((count, width), BF16),
        ((8, width), F32),
    ]
    return vmem_call(
        functools.partial(ffn_out_kernel, count=len(groups)),
        "ffn_out_norm",
        out_shape,
        10,
        cost(count * hidden * width // 2, 30 * count * width),
        [pltpu.VMEM((2, block, width), F32)],
        places=1,
        aliases={3: 0} if groups else None,
    )(place, *before, branch, xhat, cotangent, *cot_others, vectors, *groups)


def slot(place_ref, xx, yy, core):
    same_x = jnp.where(place_ref[1] == xx, 1, 0)
    same_y = jnp.where(place_ref[3] == yy, 1, 0)
    return jnp.where(core == 0, same_y, same_x), jnp.where(core == 0, same_x, same_y)


def grad_out_kernel(place_ref, act_0_ref, act_1_ref, low_ref, _, send_ref, keep_ref, *, first):
    c = place_ref[2]
    rows = send_ref.shape[2]
    columns = 8 * rows

    def group(xx, yy):
        return jnp.where(place_ref[3] == yy, 0, 1) + jnp.where(place_ref[1] == xx, 0, 2)

    def step(t, carry):
        block = lax.rem(place_ref[0] + 7 - first - t, 4)
        cut = pl.ds(pl.multiple_of(lax.rem(block, 2) * columns, LANES), columns)
        act = jnp.where(block >= 2, act_1_ref[:, cut], act_0_ref[:, cut])
        total = dot_tn(act, low_ref[...])
        for xx in range(2):
            for yy in range(2):
                at = (4 * xx + yy) * rows
                one, two = total[at : at + rows], total[at + 2 * rows : at + 3 * rows]
                send_ref[t, group(xx, yy)] = jnp.where(c == 0, two, one).astype(BF16)
                keep_ref[t, group(xx, yy)] = jnp.where(c == 0, one, two).astype(BF16)
        return carry

    lax.fori_loop(0, send_ref.shape[0], step, 0)


def grad_out(place, acts, d_low, nearby, rows, first, steps):
    count, width = d_low.shape
    shape = (steps, 4, rows, width)
    return vmem_call(
        functools.partial(grad_out_kernel, first=first),
        "grad_w_out",
        [(shape, BF16), (shape, BF16)],
        9,
        cost(16 * steps * count * rows * width, 16 * steps * count * rows),
        places=1,
    )(place, *acts, d_low, nearby)


def ffn_back_kernel(place_ref, low_ref, resid_ref, slope_0_ref, slope_1_ref, w_out_ref, w_in_ref, xhat_ref, rstd_ref, vec_ref, low_t_ref, two_ref, *refs, tile, columns):
    if len(refs) == 7:
        mix_ref, one_ref, send_ref, keep_ref, pre_ref, bias_ref, sums_ref = refs
    else:
        mix_ref, one_ref, pre_ref, bias_ref, sums_ref = refs
    hidden = pre_ref.shape[1]
    share = slope_0_ref.shape[1]
    bias_ref[...] = jnp.zeros_like(bias_ref)
    sums_ref[...] = jnp.zeros_like(sums_ref)

    def step(i, carry):
        rows = tile_rows(i, tile)
        d_low = low_ref[rows, :]
        d_normed = resid_ref[rows, :]
        for part in range(0, hidden, columns):
            cut = slice(part, part + columns)
            slope_ref = (slope_0_ref, slope_1_ref)[part // share]
            slope = slope_ref[rows, part % share : part % share + columns].astype(F32)
            d_pre = (dot_nt(d_low, w_out_ref[cut, :]) * slope).astype(BF16)
            pre_ref[rows, cut] = d_pre
            bias_ref[0:1, cut] += row_sum(d_pre.astype(F32))
            d_normed += dot_nt(d_pre, w_in_ref[:, cut])
        xhat = xhat_ref[rows, :]
        sums_ref[0:1, :] += row_sum(d_normed * xhat)
        sums_ref[1:2, :] += row_sum(d_normed)
        d_xhat = d_normed * vec_ref[1:2, :]
        d_one = rstd_ref[rows, :] * (
            d_xhat
            - jnp.mean(d_xhat, axis=-1, keepdims=True)
            - xhat * jnp.mean(d_xhat * xhat, axis=-1, keepdims=True)
        )
        one_ref[rows, :] = d_one
        mix_ref[rows, :] = d_one.astype(BF16)
        return carry

    lax.fori_loop(0, low_ref.shape[0] // tile, step, 0)
    if len(refs) == 7:
        grad_in_part(place_ref, low_t_ref, pre_ref, bias_ref, two_ref, sums_ref, send_ref, keep_ref)


def grad_in_part(place_ref, low_ref, pre_ref, bias_ref, two_ref, one_ref, send_ref, keep_ref):
    c = place_ref[2]
    split = pre_ref.shape[1]
    owners, width = 32, low_ref.shape[0]
    size = width // owners

    def gathered(values, first, part):
        total = values.shape[1]
        high = values.astype(BF16)
        rest = values - high.astype(F32)
        middle = rest.astype(BF16)
        lowest = (rest - middle.astype(F32)).astype(BF16)
        matrix = spread_matrix(part, first, total).astype(BF16)
        mask = owner_mask(total // part, total)
        return sum(dot_nt(jnp.where(mask, piece, 0.0).astype(BF16), matrix) for piece in (high, middle, lowest))

    line_0 = gathered(bias_ref[0:1, :], 0, 4 * size)
    line_1 = jnp.zeros((owners, LANES), F32)
    for i, (ref, row) in enumerate(
        ((two_ref, 0), (one_ref, 0), (one_ref, 1), (two_ref, 1), (two_ref, 2))
    ):
        line_1 += gathered(ref[row : row + 1, :], i * size, size)
    send_ref[:, :, :, :, split:] = jnp.zeros(send_ref.shape[:4] + (LANES,), BF16)
    keep_ref[:, :, :, :, split:] = jnp.zeros(keep_ref.shape[:4] + (LANES,), BF16)
    rows = send_ref.shape[3]
    columns = 768
    for cut in (slice(at, at + columns) for at in range(0, split, columns)):
        total = dot(low_ref[...], pre_ref[:, cut])
        for z in range(4):
            for xx in range(2):
                for yy in range(2):
                    at = (8 * z + 4 * xx + yy) * rows
                    first, second = total[at : at + rows], total[at + 2 * rows : at + 3 * rows]
                    away, stay = slot(place_ref, xx, yy, 1 - c), slot(place_ref, xx, yy, c)
                    send_ref[away[0], z, away[1], :, cut] = jnp.where(c == 0, second, first).astype(BF16)
                    keep_ref[stay[0], z, stay[1], :, cut] = jnp.where(c == 0, first, second).astype(BF16)
    for z in range(4):
        for xx in range(2):
            for yy in range(2):
                at = 8 * z + 4 * xx + yy
                away, stay = slot(place_ref, xx, yy, 1 - c), slot(place_ref, xx, yy, c)
                for row, line in enumerate((line_0, line_1)):
                    first, second = line[at : at + 1], line[at + 2 : at + 3]
                    side = jnp.where(c == 0, second, first)
                    send_ref[away[0], z, away[1], row : row + 1, split:] = side.astype(BF16)
                    side = jnp.where(c == 0, first, second)
                    keep_ref[stay[0], z, stay[1], row : row + 1, split:] = side.astype(BF16)


def ffn_back(place, d_low, d_resid, slopes, w_out, w_in, norm, low_t, sums_two, chained, tile=512, columns=768):
    count, width = d_low.shape
    hidden = 2 * slopes[0].shape[1]
    out_shape = [((count, width), BF16), ((count, width), F32)]
    backs = [((count, hidden), BF16), ((8, hidden), F32), ((8, width), F32)]
    scratch_shapes = []
    if chained:
        shape = (2, 4, 2, width // 32, hidden + LANES)
        out_shape += [(shape, BF16), (shape, BF16)]
        scratch_shapes = [pltpu.VMEM(*each) for each in backs]
    else:
        out_shape += backs
    return vmem_call(
        functools.partial(ffn_back_kernel, tile=tile, columns=columns),
        "ffn_back",
        out_shape,
        12,
        cost(6 * count * hidden * width, 6 * count * hidden + 4 * hidden * width),
        scratch_shapes,
        places=1,
    )(place, d_low, d_resid, *slopes, w_out, w_in, *norm, low_t, sums_two)


def mix_back_kernel(place_ref, low_ref, one_ref, hid_ref, seq_ref, send_ref, keep_ref, spec_ref):
    width = low_ref.shape[1]
    length = seq_ref.shape[0]
    block = length // 2
    y = place_ref[3]

    def step(r, carry):
        for part in range(2):
            cut = slice(part * width, (part + 1) * width)
            spec = dot(low_ref[tile_rows(r, length), :], hid_ref[:, cut])
            spec_ref[part * length : (part + 1) * length, :] = spec.astype(BF16)
        for spot, away in ((1 - y, True), (y, False)):
            total = dot(seq_ref[tile_rows(spot, block), :], spec_ref[...])
            total += one_ref[tile_rows(2 * r + spot, block), :]
            if away:
                send_ref[r] = total.astype(BF16)
            else:
                keep_ref[r] = total
        return carry

    lax.fori_loop(0, low_ref.shape[0] // length, step, 0)


def mix_back(place, d_low, d_one, hid_table, seq_table):
    count, width = d_low.shape
    length = seq_table.shape[0]
    half, block = count // length, length // 2
    return vmem_call(
        mix_back_kernel,
        "mix_back",
        [((half, block, width), BF16), ((half, block, width), F32)],
        14,
        cost(4 * count * width * (length + width), 10 * count * width),
        [pltpu.VMEM((2 * length, width), BF16)],
        places=1,
    )(place, d_low, d_one, hid_table, seq_table)


def join_kernel(place_ref, *refs, first, earlier):
    *ins, out_ref, wide_ref, sem = refs
    ins = ins[: len(ins) - earlier]
    y = place_ref[3]
    half = out_ref.shape[0] // 2
    copies = []
    for i, ref in enumerate(ins):
        rows = ref.shape[0]
        source = ref
        if ref.dtype != out_ref.dtype:
            source = wide_ref.at[pl.ds(0, rows)]
            wide_ref[:rows] = ref[...].astype(wide_ref.dtype)
        at = half * y if rows == half and first == 0 and i == 0 else half * (1 - y) + first
        copies.append(pltpu.make_async_copy(source, out_ref.at[pl.ds(at, rows)], sem.at[i]))
        copies[-1].start()
    for copy in copies:
        copy.wait()


def join(place, keep, other, first=0, joined=None):
    half, block, width = keep.shape
    ins = [other] if joined is not None else [keep, other]
    wide = other.shape if other.dtype != keep.dtype else (1, 8, LANES)
    earlier = [] if joined is None else [joined]
    return vmem_call(
        functools.partial(join_kernel, first=first, earlier=len(earlier)),
        "join_rows",
        [((2 * half, block, width), keep.dtype)],
        4,
        cost(0, 16 * half * block * width),
        [pltpu.VMEM(wide, keep.dtype), pltpu.SemaphoreType.DMA((2,))],
        places=1,
        anywhere=len(earlier),
        outside=True,
        aliases={2: 0} if earlier else None,
    )(place, *ins, *earlier)[0]


def finish_kernel(own_ref, *refs, spots):
    parts, (first_ref, near_ref, out_ref, w_ref, *smalls) = refs[:3], refs[3:]
    split = w_ref.shape[1]
    out_ref[...] = first_ref[...] + near_ref[...].astype(F32)
    total = own_ref[...]
    for ref in parts:
        total += ref[...].astype(F32)
    w_ref[...] = total[:, :split]
    for ref, (line, at) in zip(smalls, spots):
        ref[...] = total[line : line + 1, split + at : split + at + ref.shape[1]]


def finish(own, parts, first, near, split, sizes, spots):
    rows, _ = own.shape
    return vmem_call(
        functools.partial(finish_kernel, spots=spots),
        "finish_sums",
        [(first.shape, F32), ((rows, split), F32)] + [((1, size), F32) for size in sizes],
        4,
        cost(3 * rows * split, 14 * rows * split),
    )(own, *parts, first, near)


def add_up(keep, other):
    return keep.astype(F32) + other.astype(F32)


def per_device(grid, tokens, weight_in, bias_in, weight_out, bias_out, gain_mix, shift_mix, gain_ffn, shift_ffn, cotangent):
    rows, block, width = tokens.shape
    part_in, hidden = weight_in.shape
    part_out = weight_out.shape[0]
    half = rows // 2
    length = 2 * block
    devices = grid.dp * grid.seq
    z, x, c, y = grid.place()
    place = jnp.stack([z, x, c, y]).astype(jnp.int32)
    zero = jnp.uint32(0)
    across = ((1 - y) * half).astype(jnp.uint32)
    ahead = [((z + step) % 4).astype(jnp.uint32) for step in range(4)]
    place, across, ahead, weight_in = together(place, across, ahead, weight_in)
    chained = grid.chained and part_in % 8 == 0

    def other_rows(value):
        return lax.dynamic_slice(value, (across, zero, zero), (half,) + value.shape[1:])

    def join_rows(keep, other):
        other = other.astype(keep.dtype)
        return jnp.where(
            y == 0, jnp.concatenate([keep, other], 0), jnp.concatenate([other, keep], 0)
        )

    def core(value):
        return send(value, grid.cores)

    smalls = (bias_in, bias_out, gain_mix, shift_mix, gain_ffn, shift_ffn)
    sizes = [v.shape[0] for v in smalls]
    spots = [(0, 0)] + [(1, i * sizes[1]) for i in range(5)]
    lines = [0, 0]
    for value, (line, at) in zip(smalls, spots):
        lines[line] += jnp.pad(value, (at, LANES - at - value.shape[0]))
    strip = jnp.pad(jnp.stack(lines), ((0, part_in - 2), (0, 0)))
    tok_other = send(other_rows(tokens), grid.blocks)

    cos_seq, sin_seq = dft_tables(length)
    cos_hid, sin_hid = dft_tables(width)
    mix_tables = (
        table(np.concatenate([cos_seq, sin_seq], 0)),
        table(np.concatenate([cos_hid, -sin_hid], 0)),
    )
    if chained:
        packed = jnp.concatenate([weight_in, strip], axis=1)
        packed, shard_out = together(packed, weight_out)
        *pieces, near_out, tok_other = together(
            *(send(packed, grid.shifts[step]) for step in range(1, 4)),
            send(shard_out, grid.across),
            tok_other,
        )
        pair = jnp.stack([shard_out, near_out])
        column = jnp.stack([packed] + pieces)
        column, pair, tok_other = together(column, pair, tok_other)
        near, ring_1, far_pair, twin_column, (xhat, rstd) = together(
            send(column, grid.across_0),
            send(pair, grid.ring),
            send(pair, grid.blocks),
            core(column),
            mix(place, tokens, tok_other, *mix_tables),
        )
        both = jnp.concatenate([column, near], axis=0)
        both, pairs = together(both, jnp.concatenate([far_pair, ring_1], axis=0))
        far, ring_2 = together(send(both, grid.across_1), send(pairs, grid.ring))
        ring_3 = send(ring_2, grid.ring)
        groups = [column, near, far, twin_column, core(after(near, far)), core(far)]
        w_in, bias, vectors, low, low_t = first_weight(place, xhat, groups, hidden)
        cot_part = after(other_rows(cotangent), vectors)
        cot_0 = send(cot_part[:1], grid.blocks)
    else:
        cot_other = send(other_rows(cotangent), grid.blocks)
        xhat, rstd = mix(place, tokens, tok_other, *mix_tables)
        w_in = lax.all_gather(weight_in, AXES, axis=0, tiled=True)
        w_out = lax.all_gather(weight_out, AXES, axis=0, tiled=True)
        extra = lax.all_gather(strip, AXES, axis=0)[:, :2]
        bias, *vectors = [
            extra[:, line, at : at + size].reshape(1, -1).astype(F32)
            for size, (line, at) in zip(sizes, spots)
        ]
        vectors = jnp.concatenate(vectors + [jnp.zeros((3, width), F32)], axis=0)
        low, low_t = ffn_low(xhat, vectors)
    act_0, slope_0 = ffn_in(low, w_in, bias, 0, 2)
    if chained:
        early = [pair, far_pair, ring_1, ring_2]
        act_0, slope_0, low, ring_3, cot_0, twins = together(
            act_0, slope_0, low, ring_3, cot_0, [core(p) for p in early]
        )
        ring_4 = send(ring_3[:2], grid.ring)
        cot_1 = send(after(cot_part[1:], cot_0), grid.blocks)
        pairs = early + [ring_3] + twins + [core(ring_3)]
        act_1, slope_1, w_out, branch = ffn_in_last(place, low, w_in, bias, act_0, pairs)
        ring_4, cot_1, branch = together(ring_4, cot_1, branch)
    else:
        act_1, slope_1 = ffn_in(low, w_in, bias, 1, 2)
    acts, slopes = [act_0, act_1], [slope_0, slope_1]
    if chained:
        w_out, out_send, out_keep, d_resid, d_low, sums_two = ffn_out(
            place, branch, xhat, cotangent, (cot_0, cot_1), vectors, acts, w_out, [ring_4, core(ring_4)]
        )
    else:
        branch = dot(act_0, w_out[: hidden // 2]) + dot(act_1, w_out[hidden // 2 :])
        out_send, out_keep, d_resid, d_low, sums_two = ffn_out(
            place, branch, xhat, cotangent, (cot_other[:1], cot_other[1:]), vectors
        )

    norm = (xhat, rstd, vectors)
    back_tables = (
        table(np.concatenate([cos_hid, -sin_hid], 1)),
        table(np.concatenate([cos_seq, sin_seq], 1)),
    )

    def pack_small(bias_sum, norm_sum):
        grads = (bias_sum, sums_two[0], norm_sum[0], norm_sum[1], sums_two[1], sums_two[2])
        lines = [0, 0]
        for value, (line, at) in zip(grads, spots):
            value = value.reshape(devices, -1)
            lines[line] += jnp.pad(value, ((0, 0), (at, LANES - at - value.shape[1])))
        return jnp.pad(jnp.stack(lines, axis=1), ((0, 0), (0, part_in - 2), (0, 0)))

    def low_send(value, perm):
        return send(value.astype(BF16), perm)

    if chained:
        (away_a, keep_a), start = together(grad_out(place, acts, d_low, w_out, part_out, 0, 1), d_low)
        twin_a, (away_b, keep_b) = together(core(away_a), grad_out(place, acts, start, w_out, part_out, 1, 3))
        quad = add_up(keep_a[0], twin_a[0])
        start, away_b, quad, out_send = together(start, away_b, quad, out_send)
        twin_b, ring, out_other, (d_mix, d_one, away, keep) = together(
            core(away_b),
            low_send(quad, grid.ring),
            send(out_send, grid.blocks),
            ffn_back(place, start, d_resid, slopes, w_out, w_in, norm, low_t, sums_two, True),
        )
        quad = add_up(add_up(keep_b[0], twin_b[0]), ring)
        twin, quad = together(core(away[0]), quad)
        first, ring, output, twin_1, (gt_send, gt_keep) = together(
            low_send(add_up(keep[0], twin), grid.across_1),
            low_send(quad, grid.ring),
            join(place, out_keep, out_other),
            core(away[1]),
            mix_back(place, d_mix, d_one, *back_tables),
        )
        pair = add_up(add_up(keep[1], twin_1), first)
        quad = add_up(add_up(keep_b[1], twin_b[1]), ring)
        second, ring, gt_0 = together(
            low_send(pair[:, 0], grid.across_0),
            low_send(quad, grid.ring),
            send(gt_send[:1], grid.blocks),
        )
        column = add_up(pair[:, 1], second)
        quad = add_up(add_up(keep_b[2], twin_b[2]), ring)
        gt_1 = send(after(gt_send[1:], quad), grid.blocks)
        grad_tokens = join(place, gt_keep, gt_0)
        parts, far, gt_1, grad_tokens, column = together(
            [low_send(pick(column, ahead[step]), grid.shifts[step]) for step in (2, 3)],
            low_send(quad[2:], grid.across),
            gt_1,
            grad_tokens,
            column,
        )
        quad = add_up(quad[:2], far)
        near, last, grad_tokens = together(
            low_send(quad[1], grid.blocks),
            low_send(pick(column, ahead[1]), grid.shifts[1]),
            join(place, gt_keep, gt_1, 1, grad_tokens),
        )
        my_w_out, my_w_in, *my_small = finish(
            pick(column, ahead[0]), parts + [last], quad[0], near, hidden, sizes, spots
        )
        my_small = [v.reshape(-1) for v in my_small]
    else:
        output = join_rows(out_keep, send(out_send, grid.blocks))
        grad_w_out = jnp.concatenate([dot_tn(act, d_low) for act in acts], axis=0)
        my_w_out = lax.psum_scatter(grad_w_out, AXES, scatter_dimension=0, tiled=True)
        d_mix, d_one, pre, bias_sum, norm_sum = ffn_back(
            place, d_low, d_resid, slopes, w_out, w_in, norm, low_t, sums_two, False
        )
        gt_send, gt_keep = mix_back(place, d_mix, d_one, *back_tables)
        grad_tokens = join_rows(gt_keep, send(gt_send, grid.blocks))
        my_w_in = lax.psum_scatter(dot(low_t, pre), AXES, scatter_dimension=0, tiled=True)
        strips = pack_small(bias_sum[0], norm_sum)
        my_strip = lax.psum_scatter(strips, AXES, scatter_dimension=0, tiled=True)[0, :2]
        my_small = [my_strip[line, at : at + size] for size, (line, at) in zip(sizes, spots)]
    return (
        output,
        grad_tokens,
        my_w_in,
        my_small[0],
        my_w_out,
        my_small[1],
        my_small[2],
        my_small[3],
        my_small[4],
        my_small[5],
    )


def solution(mesh):
    grid = Grid(mesh)
    cut, cut2 = P(AXES), P(AXES, None)
    block = P("dp", "seq", None)
    in_specs = (block, cut2, cut, cut2, cut, cut, cut, cut, cut, block)
    out_specs = (block, block, cut2, cut, cut2, cut, cut, cut, cut, cut)

    def program(*arrays):
        return per_device(grid, *arrays)

    return jax.shard_map(
        program, mesh=mesh, in_specs=in_specs, out_specs=out_specs, check_vma=False
    )
```

```python
import functools
import math

import jax
import jax.numpy as jnp
import numpy as np
from jax import lax
from jax.experimental import pallas as pl
from jax.experimental.pallas import tpu as pltpu
from jax.sharding import PartitionSpec as P

EPS = 1e-12
AXES = ("dp", "seq")
BF16 = jnp.bfloat16
F32 = jnp.float32
MIB = 1 << 20
LANES = 128
ERF_T = 0.3275911
ERF_P = (0.254829592, -0.284496736, 1.421413741, -1.453152027, 1.061405429)


def dft_tables(length):
    index = np.arange(length, dtype=np.int64)
    angle = (index[:, None] * index[None, :] % length).astype(np.float64) * (2.0 * math.pi / length)
    scale = length ** (-0.5)
    return np.cos(angle) * scale, np.sin(angle) * scale


def table(values):
    return jnp.asarray(values.astype(np.float32)).astype(BF16)


class Grid:
    def __init__(self, mesh):
        self.dp = mesh.shape["dp"]
        self.seq = mesh.shape["seq"]
        chips = self.dp // 2
        self.low = min(2, chips)
        self.high = chips // self.low
        self.shifts = [
            self.perm(lambda z, x, c, y: ((z + step) % self.high, x, c, y)) for step in range(4)
        ]
        self.ring = self.shifts[1]
        self.across = self.perm(lambda z, x, c, y: (z, (x + 1) % self.low, c, y))
        self.corner = self.perm(
            lambda z, x, c, y: (z, (x + 1) % self.low, c, (y + 1) % self.seq)
        )
        self.cores = self.perm(lambda z, x, c, y: (z, x, 1 - c, y))
        self.blocks = self.perm(lambda z, x, c, y: (z, x, c, (y + 1) % self.seq))
        self.across_0 = self.perm(
            lambda z, x, c, y: (z, (x + 1 - c) % self.low, c, (y + c) % self.seq)
        )
        self.across_1 = self.perm(
            lambda z, x, c, y: (z, (x + c) % self.low, c, (y + 1 - c) % self.seq)
        )
        self.chained = self.high == 4 and self.low == 2 and self.seq == 2

    def index(self, z, x, c, y):
        return ((z * self.low + x) * 2 + c) * self.seq + y

    def perm(self, move):
        return [
            (self.index(z, x, c, y), self.index(*move(z, x, c, y)))
            for z in range(self.high)
            for x in range(self.low)
            for c in range(2)
            for y in range(self.seq)
        ]

    def place(self):
        dp = lax.axis_index("dp")
        return dp // (2 * self.low), dp // 2 % self.low, dp % 2, lax.axis_index("seq")


def send(value, perm):
    return lax.ppermute(value, AXES, perm)


def pick(value, index):
    zero = jnp.uint32(0)
    starts = (index,) + (zero,) * (value.ndim - 1)
    return lax.dynamic_slice(value, starts, (1,) + value.shape[1:])[0]


def dot(a, b):
    return jnp.dot(a, b, preferred_element_type=F32)


def dot_nt(a, b):
    return lax.dot_general(a, b, (((1,), (1,)), ((), ())), preferred_element_type=F32)


def dot_tn(a, b):
    return lax.dot_general(a, b, (((0,), (0,)), ((), ())), preferred_element_type=F32)


def params(mib):
    return pltpu.CompilerParams(vmem_limit_bytes=mib * MIB)


def cost(flops, bytes_accessed, transcendentals=0):
    return pl.CostEstimate(
        flops=int(flops), bytes_accessed=int(bytes_accessed), transcendentals=int(transcendentals)
    )


def row_sum(values):
    return jnp.sum(values, axis=0, keepdims=True)


def after(value, *others):
    return lax.optimization_barrier((value,) + others)[0]


def together(*values):
    return lax.optimization_barrier(values)


def device_number(place, distance, flip_x, flip_y, other_core):
    z, x, c, y = place
    zz = lax.rem(z - distance + 4, 4)
    cc = 1 - c if other_core else c
    xx = x + flip_x - 2 * x * flip_x
    yy = y + flip_y - 2 * y * flip_y
    return ((zz * 2 + xx) * 2 + cc) * 2 + yy


def column_slab(part, index, core):
    group = part + index // 4
    flip_x, flip_y = ((0, 0), (1 - core, core), (core, 1 - core), (1, 1))[group]
    return index % 4, flip_x, flip_y


def ring_slab(position):
    return position // 4, position % 2, position % 4 // 2


def put_slabs(place, refs, slab_of, put):
    own = len(refs) // 2
    for part, ref in enumerate(refs):
        core = 1 - place[2] if part >= own else place[2]
        for i in range(ref.shape[0]):
            where = slab_of(part % own, i, core)
            put(ref, i, device_number(place, *where, part >= own))


def vmem_call(kernel, name, out_shape, mib, work, scratch_shapes=(), places=0, anywhere=0, outside=False, aliases=None):
    def call(*operands):
        here = len(operands) - places - anywhere
        return pl.pallas_call(
            kernel,
            name=name,
            in_specs=[pl.BlockSpec(memory_space=pltpu.SMEM)] * places
            + [pl.BlockSpec(memory_space=pltpu.VMEM)] * here
            + [pl.BlockSpec(memory_space=pl.ANY)] * anywhere,
            out_specs=[pl.BlockSpec(memory_space=pl.ANY if outside else pltpu.VMEM)] * len(out_shape),
            out_shape=[jax.ShapeDtypeStruct(*each) for each in out_shape],
            scratch_shapes=list(scratch_shapes),
            input_output_aliases=aliases or {},
            compiler_params=params(mib),
            cost_estimate=work,
        )(*operands)

    return call


def tile_rows(index, size):
    return pl.ds(pl.multiple_of(index * size, size), size)


def assemble(place, groups, split):
    _, rows, columns = groups[0].shape
    slabs = sum(group.shape[0] for group in groups)
    return vmem_call(
        functools.partial(assemble_kernel, count=len(groups), split=split),
        "assemble_w_in",
        [((slabs * rows, split), BF16), ((slabs, rows, LANES), BF16)],
        2,
        cost(0, 4 * slabs * rows * columns),
        [pltpu.SemaphoreType.DMA((2 * slabs,))],
        places=1,
        anywhere=len(groups),
    )(place, *groups)


def spread_matrix(size, start, total):
    lane = lax.broadcasted_iota(jnp.int32, (LANES, total), 0)
    column = lax.broadcasted_iota(jnp.int32, (LANES, total), 1)
    return lane == start + lax.rem(column, size)


def owner_mask(owners, total):
    owner = lax.broadcasted_iota(jnp.int32, (owners, total), 0)
    column = lax.broadcasted_iota(jnp.int32, (owners, total), 1)
    return lax.div(column, total // owners) == owner


def first_weight_kernel(place_ref, xhat_ref, *refs, count, split):
    groups = refs[:count]
    full_ref, bias_ref, vec_ref, low_ref, low_t_ref, extra_ref = refs[count:]
    rows = groups[0].shape[1]
    place = tuple(place_ref[i] for i in range(4))

    def put(ref, i, at):
        full_ref[tile_rows(at, rows), :] = ref[i, :, :split]
        extra_ref[at] = ref[i, :, split:]

    put_slabs(place, groups, column_slab, put)
    owners, width = extra_ref.shape[0], vec_ref.shape[1]
    line = extra_ref[:, 0, :]
    wide = dot(line, spread_matrix(split // owners, 0, split).astype(BF16))
    bias_ref[...] = row_sum(jnp.where(owner_mask(owners, split), wide, 0.0))
    line = extra_ref[:, 1, :]
    mask = owner_mask(owners, width)
    size = width // owners
    vec_ref[...] = jnp.zeros_like(vec_ref)
    for i in range(5):
        wide = dot(line, spread_matrix(size, i * size, width).astype(BF16))
        vec_ref[i : i + 1, :] = row_sum(jnp.where(mask, wide, 0.0))
    low = (xhat_ref[...] * vec_ref[1:2, :] + vec_ref[2:3, :]).astype(BF16)
    low_ref[...] = low
    low_t_ref[...] = low.T


def first_weight(place, xhat, groups, split):
    _, rows, columns = groups[0].shape
    slabs = sum(group.shape[0] for group in groups)
    count, width = xhat.shape
    return vmem_call(
        functools.partial(first_weight_kernel, count=len(groups), split=split),
        "first_weight",
        [
            ((slabs * rows, split), BF16),
            ((1, split), F32),
            ((8, width), F32),
            ((count, width), BF16),
            ((width, count), BF16),
        ],
        10,
        cost(2 * count * width, 4 * slabs * rows * columns),
        [pltpu.VMEM((slabs, rows, LANES), BF16)],
        places=1,
    )(place, xhat, *groups)


def mix_kernel(place_ref, mine_ref, other_ref, seq_ref, hid_hbm, xhat_ref, rstd_ref, row_ref, hid_ref, sem):
    half, block, width = other_ref.shape
    length = 2 * block
    y = place_ref[3]
    copy = pltpu.make_async_copy(hid_hbm, hid_ref, sem)
    copy.start()

    def spectra(r, part):
        at = part * block
        tokens = row_ref[...]
        cos_part = dot(seq_ref[at : at + block, :], tokens).astype(BF16)
        return cos_part, dot(seq_ref[length + at : length + at + block, :], tokens).astype(BF16)

    for r in range(half):
        row_ref[tile_rows(y, block), :] = mine_ref[half * y + r]
        row_ref[tile_rows(1 - y, block), :] = other_ref[r]
        for part in range(2):
            cos_part, sin_part = spectra(r, part)
            if r == 0 and part == 0:
                copy.wait()
            mixed = dot(cos_part, hid_ref[:width, :]) + dot(sin_part, hid_ref[width:, :])
            resid = row_ref[part * block : (part + 1) * block, :].astype(F32) + mixed
            center = resid - jnp.mean(resid, axis=-1, keepdims=True)
            rstd = lax.rsqrt(jnp.mean(center * center, axis=-1, keepdims=True) + EPS)
            at = (2 * r + part) * block
            xhat_ref[at : at + block, :] = center * rstd
            rstd_ref[at : at + block, :] = rstd


def mix(place, tokens, other, seq_table, hid_table):
    half, block, width = other.shape
    length = 2 * block
    count = half * length
    return vmem_call(
        mix_kernel,
        "mix_norm",
        [((count, width), F32), ((count, 1), F32)],
        14,
        cost(4 * count * width * (length + width), 10 * count * width),
        [
            pltpu.VMEM((length, width), BF16),
            pltpu.VMEM((2 * width, width), BF16),
            pltpu.SemaphoreType.DMA(()),
        ],
        places=1,
        anywhere=1,
    )(place, tokens, other, seq_table, pltpu.with_memory_space_constraint(hid_table, pltpu.HBM))


def gelu_both(values):
    size = jnp.abs(values)
    t = 1.0 / (1.0 + (ERF_T / math.sqrt(2.0)) * size)
    bell = jnp.exp2((values * values) * (-0.5 * math.log2(math.e)))
    poly = 0.5 * ERF_P[4]
    for term in ERF_P[3::-1]:
        poly = 0.5 * term + t * poly
    tail = t * poly * bell
    phi = jnp.where(values > 0, 1.0 - tail, tail)
    return values * phi, phi + values * (bell * (1.0 / math.sqrt(2.0 * math.pi)))


def ffn_low_kernel(xhat_ref, vec_ref, low_ref, low_t_ref):
    low = (xhat_ref[...] * vec_ref[1:2, :] + vec_ref[2:3, :]).astype(BF16)
    low_ref[...] = low
    low_t_ref[...] = low.T


def ffn_low(xhat, vectors):
    count, width = xhat.shape
    return vmem_call(
        ffn_low_kernel,
        "normed_low",
        [((count, width), BF16), ((width, count), BF16)],
        8,
        cost(2 * count * width, 8 * count * width),
    )(xhat, vectors)


def ffn_in_tiles(low_ref, w_ref, bias_ref, act_ref, slope_ref, at, tile, columns):
    tiles = low_ref.shape[0] // tile

    def step(j, carry):
        rows = tile_rows(lax.rem(j, tiles), tile)
        part = j // tiles * columns
        cut = pl.ds(pl.multiple_of(part, LANES), columns)
        full = pl.ds(pl.multiple_of(at + part, LANES), columns)
        act, slope = gelu_both(dot(low_ref[rows, :], w_ref[:, full]) + bias_ref[:, full])
        act_ref[rows, cut] = act.astype(BF16)
        slope_ref[rows, cut] = slope.astype(BF16)
        return carry

    lax.fori_loop(0, tiles * (act_ref.shape[1] // columns), step, 0)


def ffn_in_kernel(low_ref, w_ref, bias_ref, act_ref, slope_ref, *, at, tile, columns):
    ffn_in_tiles(low_ref, w_ref, bias_ref, act_ref, slope_ref, at, tile, columns)


def ffn_in(low, w_in, bias, part, parts, columns=768, tile=1024):
    count, width = low.shape
    hidden = w_in.shape[1] // parts
    return vmem_call(
        functools.partial(ffn_in_kernel, at=part * hidden, tile=tile, columns=columns),
        "ffn_in_gelu",
        [((count, hidden), BF16)] * 2,
        8,
        cost(2 * count * width * hidden, 4 * count * hidden, 2 * count * hidden),
    )(low, w_in, bias)


def hidden_block(refs, rows, block):
    width = refs[0].shape[1] // 2
    cut = pl.ds(pl.multiple_of(lax.rem(block, 2) * width, width), width)
    return jnp.where(block >= 2, refs[1][rows, cut], refs[0][rows, cut])


def place_rows(place_ref, groups, w_ref, first):
    place = tuple(place_ref[i] for i in range(4))
    rows = groups[0].shape[1]
    starts = [first]
    for group in groups[: len(groups) // 2]:
        starts.append(starts[-1] + group.shape[0])

    def put(ref, i, at):
        w_ref[tile_rows(at, rows), :] = ref[i]

    put_slabs(place, groups, lambda part, index, core: ring_slab(starts[part] + index), put)


def ffn_in_last_kernel(place_ref, low_ref, w_in_ref, bias_ref, act_0_ref, *refs, count, at, tile, columns, step):
    groups, (act_1_ref, slope_ref, w_ref, branch_ref) = refs[:count], refs[count:]
    place_rows(place_ref, groups, w_ref, 0)
    ffn_in_tiles(low_ref, w_in_ref, bias_ref, act_1_ref, slope_ref, at, tile, columns)
    size = w_ref.shape[0] // 4

    def multiply(i, carry):
        rows = tile_rows(i, step)
        total = None
        for distance in range(3):
            block = lax.rem(place_ref[0] + 4 - distance, 4)
            part = hidden_block((act_0_ref, act_1_ref), rows, block)
            part = dot(part, w_ref[tile_rows(block, size), :])
            total = part if total is None else total + part
        branch_ref[rows, :] = total
        return carry

    lax.fori_loop(0, branch_ref.shape[0] // step, multiply, 0)


def ffn_in_last(place, low, w_in, bias, act_0, groups, columns=768, tile=1024, step=512):
    count, width = low.shape
    hidden = act_0.shape[1]
    return vmem_call(
        functools.partial(
            ffn_in_last_kernel, count=len(groups), at=hidden, tile=tile, columns=columns, step=step
        ),
        "ffn_in_out",
        [((count, hidden), BF16)] * 2 + [((2 * hidden, width), BF16), ((count, width), F32)],
        8,
        cost(5 * count * width * hidden, 8 * count * hidden, 2 * count * hidden),
        places=1,
    )(place, low, w_in, bias, act_0, *groups)


def ffn_out_kernel(place_ref, *refs, count):
    if count:
        act_0_ref, act_1_ref, _, *refs = refs
    branch_ref, xhat_ref, mine_ref, other_0_ref, other_1_ref, vec_ref, *refs = refs
    groups, refs = refs[:count], refs[count:]
    if count:
        w_ref, *refs = refs
    send_ref, keep_ref, resid_ref, low_ref, sums_ref, part_ref = refs
    half, block = 2, other_0_ref.shape[1]
    y = place_ref[3]
    if count:
        place_rows(place_ref, groups, w_ref, 14)
    sums_ref[...] = jnp.zeros_like(sums_ref)
    gain_mix = vec_ref[1:2, :]
    shift_mix = vec_ref[2:3, :] + vec_ref[0:1, :]
    gain, shift = vec_ref[3:4, :], vec_ref[4:5, :]

    def rows_of(step):
        away, r = step < half, step % half
        return tile_rows(2 * r + (1 - y if away else y), block)

    def multiply(step):
        rows = rows_of(step)
        if not count:
            return branch_ref[rows, :]
        last = lax.rem(place_ref[0] + 1, 4)
        part = hidden_block((act_0_ref, act_1_ref), rows, last)
        return branch_ref[rows, :] + dot(part, w_ref[tile_rows(last, w_ref.shape[0] // 4), :])

    def finish(step, branch):
        away, r = step < half, step % half
        rows = rows_of(step)
        value = xhat_ref[rows, :] * gain_mix + (branch + shift_mix)
        center = value - jnp.mean(value, axis=-1, keepdims=True)
        rstd = lax.rsqrt(jnp.mean(center * center, axis=-1, keepdims=True) + EPS)
        xhat = center * rstd
        result = (xhat * gain + shift).astype(BF16)
        if away:
            send_ref[r] = result
            cot = (other_0_ref, other_1_ref)[r][0].astype(F32)
        else:
            keep_ref[r] = result
            cot = mine_ref[half * y + r].astype(F32)
        d_xhat = cot * gain
        d_resid = rstd * (
            d_xhat
            - jnp.mean(d_xhat, axis=-1, keepdims=True)
            - xhat * jnp.mean(d_xhat * xhat, axis=-1, keepdims=True)
        )
        d_low = d_resid.astype(BF16)
        resid_ref[rows, :] = d_resid
        low_ref[rows, :] = d_low
        sums_ref[0:1, :] += row_sum(d_low.astype(F32))
        sums_ref[1:2, :] += row_sum(cot * xhat)
        sums_ref[2:3, :] += row_sum(cot)

    part_ref[0] = multiply(0)
    for step in range(2 * half):
        if step + 1 < 2 * half:
            part_ref[(step + 1) % 2] = multiply(step + 1)
        finish(step, part_ref[step % 2])


def ffn_out(place, branch, xhat, cotangent, cot_others, vectors, acts=(), w_out=None, groups=()):
    count, width = xhat.shape
    half, block = len(cot_others), cot_others[0].shape[1]
    hidden = 2 * acts[0].shape[1] if groups else 0
    before = [*acts, w_out] if groups else []
    out_shape = [((hidden, width), BF16)] if groups else []
    out_shape += [
        ((half, block, width), BF16),
        ((half, block, width), BF16),
        ((count, width), F32),
        ((count, width), BF16),
        ((8, width), F32),
    ]
    return vmem_call(
        functools.partial(ffn_out_kernel, count=len(groups)),
        "ffn_out_norm",
        out_shape,
        10,
        cost(count * hidden * width // 2, 30 * count * width),
        [pltpu.VMEM((2, block, width), F32)],
        places=1,
        aliases={3: 0} if groups else None,
    )(place, *before, branch, xhat, cotangent, *cot_others, vectors, *groups)


def slot(place_ref, xx, yy, core):
    same_x = jnp.where(place_ref[1] == xx, 1, 0)
    same_y = jnp.where(place_ref[3] == yy, 1, 0)
    return jnp.where(core == 0, same_y, same_x), jnp.where(core == 0, same_x, same_y)


def grad_out_kernel(place_ref, act_0_ref, act_1_ref, low_ref, _, send_ref, keep_ref, *, first):
    c = place_ref[2]
    rows = send_ref.shape[2]
    columns = 8 * rows

    def group(xx, yy):
        return jnp.where(place_ref[3] == yy, 0, 1) + jnp.where(place_ref[1] == xx, 0, 2)

    def step(t, carry):
        block = lax.rem(place_ref[0] + 7 - first - t, 4)
        cut = pl.ds(pl.multiple_of(lax.rem(block, 2) * columns, LANES), columns)
        act = jnp.where(block >= 2, act_1_ref[:, cut], act_0_ref[:, cut])
        total = dot_tn(act, low_ref[...])
        for xx in range(2):
            for yy in range(2):
                at = (4 * xx + yy) * rows
                one, two = total[at : at + rows], total[at + 2 * rows : at + 3 * rows]
                send_ref[t, group(xx, yy)] = jnp.where(c == 0, two, one).astype(BF16)
                keep_ref[t, group(xx, yy)] = jnp.where(c == 0, one, two).astype(BF16)
        return carry

    lax.fori_loop(0, send_ref.shape[0], step, 0)


def grad_out(place, acts, d_low, nearby, rows, first, steps):
    count, width = d_low.shape
    shape = (steps, 4, rows, width)
    return vmem_call(
        functools.partial(grad_out_kernel, first=first),
        "grad_w_out",
        [(shape, BF16), (shape, BF16)],
        9,
        cost(16 * steps * count * rows * width, 16 * steps * count * rows),
        places=1,
    )(place, *acts, d_low, nearby)


def ffn_back_kernel(place_ref, low_ref, resid_ref, slope_0_ref, slope_1_ref, w_out_ref, w_in_ref, xhat_ref, rstd_ref, vec_ref, low_t_ref, two_ref, *refs, tile, columns):
    if len(refs) == 7:
        mix_ref, one_ref, send_ref, keep_ref, pre_ref, bias_ref, sums_ref = refs
    else:
        mix_ref, one_ref, pre_ref, bias_ref, sums_ref = refs
    hidden = pre_ref.shape[1]
    share = slope_0_ref.shape[1]
    bias_ref[...] = jnp.zeros_like(bias_ref)
    sums_ref[...] = jnp.zeros_like(sums_ref)

    def step(i, carry):
        rows = tile_rows(i, tile)
        d_low = low_ref[rows, :]
        d_normed = resid_ref[rows, :]
        for part in range(0, hidden, columns):
            cut = slice(part, part + columns)
            slope_ref = (slope_0_ref, slope_1_ref)[part // share]
            slope = slope_ref[rows, part % share : part % share + columns].astype(F32)
            d_pre = (dot_nt(d_low, w_out_ref[cut, :]) * slope).astype(BF16)
            pre_ref[rows, cut] = d_pre
            bias_ref[0:1, cut] += row_sum(d_pre.astype(F32))
            d_normed += dot_nt(d_pre, w_in_ref[:, cut])
        xhat = xhat_ref[rows, :]
        sums_ref[0:1, :] += row_sum(d_normed * xhat)
        sums_ref[1:2, :] += row_sum(d_normed)
        d_xhat = d_normed * vec_ref[1:2, :]
        d_one = rstd_ref[rows, :] * (
            d_xhat
            - jnp.mean(d_xhat, axis=-1, keepdims=True)
            - xhat * jnp.mean(d_xhat * xhat, axis=-1, keepdims=True)
        )
        one_ref[rows, :] = d_one
        mix_ref[rows, :] = d_one.astype(BF16)
        return carry

    lax.fori_loop(0, low_ref.shape[0] // tile, step, 0)
    if len(refs) == 7:
        grad_in_part(place_ref, low_t_ref, pre_ref, bias_ref, two_ref, sums_ref, send_ref, keep_ref)


def grad_in_part(place_ref, low_ref, pre_ref, bias_ref, two_ref, one_ref, send_ref, keep_ref):
    c = place_ref[2]
    split = pre_ref.shape[1]
    owners, width = 32, low_ref.shape[0]
    size = width // owners

    def gathered(values, first, part):
        total = values.shape[1]
        high = values.astype(BF16)
        rest = values - high.astype(F32)
        middle = rest.astype(BF16)
        lowest = (rest - middle.astype(F32)).astype(BF16)
        matrix = spread_matrix(part, first, total).astype(BF16)
        mask = owner_mask(total // part, total)
        return sum(dot_nt(jnp.where(mask, piece, 0.0).astype(BF16), matrix) for piece in (high, middle, lowest))

    line_0 = gathered(bias_ref[0:1, :], 0, 4 * size)
    line_1 = jnp.zeros((owners, LANES), F32)
    for i, (ref, row) in enumerate(
        ((two_ref, 0), (one_ref, 0), (one_ref, 1), (two_ref, 1), (two_ref, 2))
    ):
        line_1 += gathered(ref[row : row + 1, :], i * size, size)
    send_ref[:, :, :, :, split:] = jnp.zeros(send_ref.shape[:4] + (LANES,), BF16)
    keep_ref[:, :, :, :, split:] = jnp.zeros(keep_ref.shape[:4] + (LANES,), BF16)
    rows = send_ref.shape[3]
    columns = 768
    for cut in (slice(at, at + columns) for at in range(0, split, columns)):
        total = dot(low_ref[...], pre_ref[:, cut])
        for z in range(4):
            for xx in range(2):
                for yy in range(2):
                    at = (8 * z + 4 * xx + yy) * rows
                    first, second = total[at : at + rows], total[at + 2 * rows : at + 3 * rows]
                    away, stay = slot(place_ref, xx, yy, 1 - c), slot(place_ref, xx, yy, c)
                    send_ref[away[0], z, away[1], :, cut] = jnp.where(c == 0, second, first).astype(BF16)
                    keep_ref[stay[0], z, stay[1], :, cut] = jnp.where(c == 0, first, second).astype(BF16)
    for z in range(4):
        for xx in range(2):
            for yy in range(2):
                at = 8 * z + 4 * xx + yy
                away, stay = slot(place_ref, xx, yy, 1 - c), slot(place_ref, xx, yy, c)
                for row, line in enumerate((line_0, line_1)):
                    first, second = line[at : at + 1], line[at + 2 : at + 3]
                    side = jnp.where(c == 0, second, first)
                    send_ref[away[0], z, away[1], row : row + 1, split:] = side.astype(BF16)
                    side = jnp.where(c == 0, first, second)
                    keep_ref[stay[0], z, stay[1], row : row + 1, split:] = side.astype(BF16)


def ffn_back(place, d_low, d_resid, slopes, w_out, w_in, norm, low_t, sums_two, chained, tile=512, columns=768):
    count, width = d_low.shape
    hidden = 2 * slopes[0].shape[1]
    out_shape = [((count, width), BF16), ((count, width), F32)]
    backs = [((count, hidden), BF16), ((8, hidden), F32), ((8, width), F32)]
    scratch_shapes = []
    if chained:
        shape = (2, 4, 2, width // 32, hidden + LANES)
        out_shape += [(shape, BF16), (shape, BF16)]
        scratch_shapes = [pltpu.VMEM(*each) for each in backs]
    else:
        out_shape += backs
    return vmem_call(
        functools.partial(ffn_back_kernel, tile=tile, columns=columns),
        "ffn_back",
        out_shape,
        12,
        cost(6 * count * hidden * width, 6 * count * hidden + 4 * hidden * width),
        scratch_shapes,
        places=1,
    )(place, d_low, d_resid, *slopes, w_out, w_in, *norm, low_t, sums_two)


def mix_back_kernel(place_ref, low_ref, one_ref, hid_ref, seq_ref, send_ref, keep_ref, spec_ref):
    width = low_ref.shape[1]
    length = seq_ref.shape[0]
    block = length // 2
    y = place_ref[3]

    def step(r, carry):
        for part in range(2):
            cut = slice(part * width, (part + 1) * width)
            spec = dot(low_ref[tile_rows(r, length), :], hid_ref[:, cut])
            spec_ref[part * length : (part + 1) * length, :] = spec.astype(BF16)
        for spot, away in ((1 - y, True), (y, False)):
            total = dot(seq_ref[tile_rows(spot, block), :], spec_ref[...])
            total += one_ref[tile_rows(2 * r + spot, block), :]
            if away:
                send_ref[r] = total.astype(BF16)
            else:
                keep_ref[r] = total
        return carry

    lax.fori_loop(0, low_ref.shape[0] // length, step, 0)


def mix_back(place, d_low, d_one, hid_table, seq_table):
    count, width = d_low.shape
    length = seq_table.shape[0]
    half, block = count // length, length // 2
    return vmem_call(
        mix_back_kernel,
        "mix_back",
        [((half, block, width), BF16), ((half, block, width), F32)],
        14,
        cost(4 * count * width * (length + width), 10 * count * width),
        [pltpu.VMEM((2 * length, width), BF16)],
        places=1,
    )(place, d_low, d_one, hid_table, seq_table)


def join_kernel(place_ref, *refs, first, earlier):
    *ins, out_ref, wide_ref, sem = refs
    ins = ins[: len(ins) - earlier]
    y = place_ref[3]
    half = out_ref.shape[0] // 2
    copies = []
    for i, ref in enumerate(ins):
        rows = ref.shape[0]
        source = ref
        if ref.dtype != out_ref.dtype:
            source = wide_ref.at[pl.ds(0, rows)]
            wide_ref[:rows] = ref[...].astype(wide_ref.dtype)
        at = half * y if rows == half and first == 0 and i == 0 else half * (1 - y) + first
        copies.append(pltpu.make_async_copy(source, out_ref.at[pl.ds(at, rows)], sem.at[i]))
        copies[-1].start()
    for copy in copies:
        copy.wait()


def join(place, keep, other, first=0, joined=None):
    half, block, width = keep.shape
    ins = [other] if joined is not None else [keep, other]
    wide = other.shape if other.dtype != keep.dtype else (1, 8, LANES)
    earlier = [] if joined is None else [joined]
    return vmem_call(
        functools.partial(join_kernel, first=first, earlier=len(earlier)),
        "join_rows",
        [((2 * half, block, width), keep.dtype)],
        4,
        cost(0, 16 * half * block * width),
        [pltpu.VMEM(wide, keep.dtype), pltpu.SemaphoreType.DMA((2,))],
        places=1,
        anywhere=len(earlier),
        outside=True,
        aliases={2: 0} if earlier else None,
    )(place, *ins, *earlier)[0]


def finish_kernel(own_ref, *refs, spots):
    parts, (first_ref, near_ref, out_ref, w_ref, *smalls) = refs[:3], refs[3:]
    split = w_ref.shape[1]
    out_ref[...] = first_ref[...] + near_ref[...].astype(F32)
    total = own_ref[...]
    for ref in parts:
        total += ref[...].astype(F32)
    w_ref[...] = total[:, :split]
    for ref, (line, at) in zip(smalls, spots):
        ref[...] = total[line : line + 1, split + at : split + at + ref.shape[1]]


def finish(own, parts, first, near, split, sizes, spots):
    rows, _ = own.shape
    return vmem_call(
        functools.partial(finish_kernel, spots=spots),
        "finish_sums",
        [(first.shape, F32), ((rows, split), F32)] + [((1, size), F32) for size in sizes],
        4,
        cost(3 * rows * split, 14 * rows * split),
    )(own, *parts, first, near)


def add_up(keep, other):
    return keep.astype(F32) + other.astype(F32)


def per_device(grid, tokens, weight_in, bias_in, weight_out, bias_out, gain_mix, shift_mix, gain_ffn, shift_ffn, cotangent):
    rows, block, width = tokens.shape
    part_in, hidden = weight_in.shape
    part_out = weight_out.shape[0]
    half = rows // 2
    length = 2 * block
    devices = grid.dp * grid.seq
    z, x, c, y = grid.place()
    place = jnp.stack([z, x, c, y]).astype(jnp.int32)
    zero = jnp.uint32(0)
    across = ((1 - y) * half).astype(jnp.uint32)
    ahead = [((z + step) % 4).astype(jnp.uint32) for step in range(4)]
    place, across, ahead, weight_in = together(place, across, ahead, weight_in)
    chained = grid.chained and part_in % 8 == 0

    def other_rows(value):
        return lax.dynamic_slice(value, (across, zero, zero), (half,) + value.shape[1:])

    def join_rows(keep, other):
        other = other.astype(keep.dtype)
        return jnp.where(
            y == 0, jnp.concatenate([keep, other], 0), jnp.concatenate([other, keep], 0)
        )

    def core(value):
        return send(value, grid.cores)

    smalls = (bias_in, bias_out, gain_mix, shift_mix, gain_ffn, shift_ffn)
    sizes = [v.shape[0] for v in smalls]
    spots = [(0, 0)] + [(1, i * sizes[1]) for i in range(5)]
    lines = [0, 0]
    for value, (line, at) in zip(smalls, spots):
        lines[line] += jnp.pad(value, (at, LANES - at - value.shape[0]))
    strip = jnp.pad(jnp.stack(lines), ((0, part_in - 2), (0, 0)))
    tok_other = send(other_rows(tokens), grid.blocks)

    cos_seq, sin_seq = dft_tables(length)
    cos_hid, sin_hid = dft_tables(width)
    mix_tables = (
        table(np.concatenate([cos_seq, sin_seq], 0)),
        table(np.concatenate([cos_hid, -sin_hid], 0)),
    )
    if chained:
        packed = jnp.concatenate([weight_in, strip], axis=1)
        packed, shard_out = together(packed, weight_out)
        *pieces, near_out, tok_other = together(
            *(send(packed, grid.shifts[step]) for step in range(1, 4)),
            send(shard_out, grid.across),
            tok_other,
        )
        pair = jnp.stack([shard_out, near_out])
        column = jnp.stack([packed] + pieces)
        column, pair, tok_other = together(column, pair, tok_other)
        near, ring_1, far_pair, twin_column, (xhat, rstd) = together(
            send(column, grid.across_0),
            send(pair, grid.ring),
            send(pair, grid.blocks),
            core(column),
            mix(place, tokens, tok_other, *mix_tables),
        )
        both = jnp.concatenate([column, near], axis=0)
        both, pairs = together(both, jnp.concatenate([far_pair, ring_1], axis=0))
        far, ring_2 = together(send(both, grid.across_1), send(pairs, grid.ring))
        ring_3 = send(ring_2, grid.ring)
        groups = [column, near, far, twin_column, core(after(near, far)), core(far)]
        w_in, bias, vectors, low, low_t = first_weight(place, xhat, groups, hidden)
        cot_part = after(other_rows(cotangent), vectors)
        cot_0 = send(cot_part[:1], grid.blocks)
    else:
        cot_other = send(other_rows(cotangent), grid.blocks)
        xhat, rstd = mix(place, tokens, tok_other, *mix_tables)
        w_in = lax.all_gather(weight_in, AXES, axis=0, tiled=True)
        w_out = lax.all_gather(weight_out, AXES, axis=0, tiled=True)
        extra = lax.all_gather(strip, AXES, axis=0)[:, :2]
        bias, *vectors = [
            extra[:, line, at : at + size].reshape(1, -1).astype(F32)
            for size, (line, at) in zip(sizes, spots)
        ]
        vectors = jnp.concatenate(vectors + [jnp.zeros((3, width), F32)], axis=0)
        low, low_t = ffn_low(xhat, vectors)
    act_0, slope_0 = ffn_in(low, w_in, bias, 0, 2)
    if chained:
        early = [pair, far_pair, ring_1, ring_2]
        act_0, slope_0, low, ring_3, cot_0, twins = together(
            act_0, slope_0, low, ring_3, cot_0, [core(p) for p in early]
        )
        ring_4 = send(ring_3[:2], grid.ring)
        cot_1 = send(after(cot_part[1:], cot_0), grid.blocks)
        pairs = early + [ring_3] + twins + [core(ring_3)]
        act_1, slope_1, w_out, branch = ffn_in_last(place, low, w_in, bias, act_0, pairs)
        ring_4, cot_1, branch = together(ring_4, cot_1, branch)
    else:
        act_1, slope_1 = ffn_in(low, w_in, bias, 1, 2)
    acts, slopes = [act_0, act_1], [slope_0, slope_1]
    if chained:
        w_out, out_send, out_keep, d_resid, d_low, sums_two = ffn_out(
            place, branch, xhat, cotangent, (cot_0, cot_1), vectors, acts, w_out, [ring_4, core(ring_4)]
        )
    else:
        branch = dot(act_0, w_out[: hidden // 2]) + dot(act_1, w_out[hidden // 2 :])
        out_send, out_keep, d_resid, d_low, sums_two = ffn_out(
            place, branch, xhat, cotangent, (cot_other[:1], cot_other[1:]), vectors
        )

    norm = (xhat, rstd, vectors)
    back_tables = (
        table(np.concatenate([cos_hid, -sin_hid], 1)),
        table(np.concatenate([cos_seq, sin_seq], 1)),
    )

    def pack_small(bias_sum, norm_sum):
        grads = (bias_sum, sums_two[0], norm_sum[0], norm_sum[1], sums_two[1], sums_two[2])
        lines = [0, 0]
        for value, (line, at) in zip(grads, spots):
            value = value.reshape(devices, -1)
            lines[line] += jnp.pad(value, ((0, 0), (at, LANES - at - value.shape[1])))
        return jnp.pad(jnp.stack(lines, axis=1), ((0, 0), (0, part_in - 2), (0, 0)))

    def low_send(value, perm):
        return send(value.astype(BF16), perm)

    if chained:
        (away_a, keep_a), start = together(grad_out(place, acts, d_low, w_out, part_out, 0, 1), d_low)
        twin_a, (away_b, keep_b) = together(core(away_a), grad_out(place, acts, start, w_out, part_out, 1, 3))
        quad = add_up(keep_a[0], twin_a[0])
        start, away_b, quad, out_send = together(start, away_b, quad, out_send)
        twin_b, ring, out_other, (d_mix, d_one, away, keep) = together(
            core(away_b),
            low_send(quad, grid.ring),
            send(out_send, grid.blocks),
            ffn_back(place, start, d_resid, slopes, w_out, w_in, norm, low_t, sums_two, True),
        )
        quad = add_up(add_up(keep_b[0], twin_b[0]), ring)
        twin, quad = together(core(away[0]), quad)
        first, ring, output, twin_1, (gt_send, gt_keep) = together(
            low_send(add_up(keep[0], twin), grid.across_1),
            low_send(quad, grid.ring),
            join(place, out_keep, out_other),
            core(away[1]),
            mix_back(place, d_mix, d_one, *back_tables),
        )
        pair = add_up(add_up(keep[1], twin_1), first)
        quad = add_up(add_up(keep_b[1], twin_b[1]), ring)
        second, ring, gt_0 = together(
            low_send(pair[:, 0], grid.across_0),
            low_send(quad, grid.ring),
            send(gt_send[:1], grid.blocks),
        )
        column = add_up(pair[:, 1], second)
        quad = add_up(add_up(keep_b[2], twin_b[2]), ring)
        gt_1 = send(after(gt_send[1:], quad), grid.blocks)
        grad_tokens = join(place, gt_keep, gt_0)
        parts, far, gt_1, grad_tokens, column = together(
            [low_send(pick(column, ahead[step]), grid.shifts[step]) for step in (2, 3)],
            low_send(quad[2:], grid.across),
            gt_1,
            grad_tokens,
            column,
        )
        quad = add_up(quad[:2], far)
        near, last, grad_tokens = together(
            low_send(quad[1], grid.blocks),
            low_send(pick(column, ahead[1]), grid.shifts[1]),
            join(place, gt_keep, gt_1, 1, grad_tokens),
        )
        my_w_out, my_w_in, *my_small = finish(
            pick(column, ahead[0]), parts + [last], quad[0], near, hidden, sizes, spots
        )
        my_small = [v.reshape(-1) for v in my_small]
    else:
        output = join_rows(out_keep, send(out_send, grid.blocks))
        grad_w_out = jnp.concatenate([dot_tn(act, d_low) for act in acts], axis=0)
        my_w_out = lax.psum_scatter(grad_w_out, AXES, scatter_dimension=0, tiled=True)
        d_mix, d_one, pre, bias_sum, norm_sum = ffn_back(
            place, d_low, d_resid, slopes, w_out, w_in, norm, low_t, sums_two, False
        )
        gt_send, gt_keep = mix_back(place, d_mix, d_one, *back_tables)
        grad_tokens = join_rows(gt_keep, send(gt_send, grid.blocks))
        my_w_in = lax.psum_scatter(dot(low_t, pre), AXES, scatter_dimension=0, tiled=True)
        strips = pack_small(bias_sum[0], norm_sum)
        my_strip = lax.psum_scatter(strips, AXES, scatter_dimension=0, tiled=True)[0, :2]
        my_small = [my_strip[line, at : at + size] for size, (line, at) in zip(sizes, spots)]
    return (
        output,
        grad_tokens,
        my_w_in,
        my_small[0],
        my_w_out,
        my_small[1],
        my_small[2],
        my_small[3],
        my_small[4],
        my_small[5],
    )


def solution(mesh):
    grid = Grid(mesh)
    cut, cut2 = P(AXES), P(AXES, None)
    block = P("dp", "seq", None)
    in_specs = (block, cut2, cut, cut2, cut, cut, cut, cut, cut, block)
    out_specs = (block, block, cut2, cut, cut2, cut, cut, cut, cut, cut)

    def program(*arrays):
        return per_device(grid, *arrays)

    return jax.shard_map(
        program, mesh=mesh, in_specs=in_specs, out_specs=out_specs, check_vma=False
    )
```
